256 devices in a mesh: dp: 64 (over z, x, y_hi), tensor: 4 (over y_lo, core).
Axes of the slice: x: 4, y: 4 (y_hi: 2, y_lo: 2; y = y_hi * 2 + y_lo), z: 8, core: 2. Of those that a mesh axis runs over, the one named last changes fastest.
Arguments:
- inputs: float32 [64, 197, 768], P('dp')
- cotangent: float32 [64, 197, 768], P('dp'), may hold values from -6 to 6
- norm_gains: float32 [2, 768], P(None, 'dp'), may hold values from 0.5 to 1.5
- attn_mats: float32 [4, 768, 768], P(None, 'dp', 'tensor')
- router: float32 [768, 3], P('dp'), may hold values from -0.4375 to 0.4375
- expert_in: float32 [3, 768, 1536], P(None, 'dp', 'tensor'), may hold values from -0.21875 to 0.21875
- expert_out: float32 [3, 768, 1536], P(None, 'dp', 'tensor'), may hold values from -0.3125 to 0.3125
- moment_gains: float32 [2, 768], P(None, 'dp'), may hold values from -128 to 128
- moment_attn: float32 [4, 768, 768], P(None, 'dp', 'tensor'), may hold values from -32 to 32
- moment_router: float32 [768, 3], P('dp'), may hold values from -320 to 320
- moment_in: float32 [3, 768, 1536], P(None, 'dp', 'tensor'), may hold values from -32 to 32
- moment_out: float32 [3, 768, 1536], P(None, 'dp', 'tensor'), may hold values from -32 to 32
- routes: int32 [64, 197, 2], P('dp'), may hold values from 0 to 2, all different within a row; in each aligned block of 197 rows (0 to 196, 197 to 393, ..., all dimensions but the last counted through in order) at most 197 rows name the same one
Outputs:
- output: float32 [64, 197, 768], P('dp')
- grad_inputs: float32 [64, 197, 768], P('dp')
- grad_gains: float32 [2, 768], P(None, 'dp')
- grad_attn: float32 [4, 768, 768], P(None, 'dp', 'tensor')
- grad_router: float32 [768, 3], P('dp')
- grad_in: float32 [3, 768, 1536], P(None, 'dp', 'tensor')
- grad_out: float32 [3, 768, 1536], P(None, 'dp', 'tensor')
- gains_new: float32 [2, 768], P(None, 'dp')
- attn_new: float32 [4, 768, 768], P(None, 'dp', 'tensor')
- router_new: float32 [768, 3], P('dp')
- in_new: float32 [3, 768, 1536], P(None, 'dp', 'tensor')
- out_new: float32 [3, 768, 1536], P(None, 'dp', 'tensor')
- moment_gains_new: float32 [2, 768], P(None, 'dp')
- moment_attn_new: float32 [4, 768, 768], P(None, 'dp', 'tensor')
- moment_router_new: float32 [768, 3], P('dp')
- moment_in_new: float32 [3, 768, 1536], P(None, 'dp', 'tensor')
- moment_out_new: float32 [3, 768, 1536], P(None, 'dp', 'tensor')
The draws below stay inside these ranges and needn't reach their ends.
Inputs may be any that keep to these rules, and one draw needn't show every extreme that they name: `routes`: in the rows of one index of dp no expert is named by more than 197 of them, a bound that some block reaches; a row's two experts differ.
All inputs are finite; a program needn't handle non-finite values.
Results may differ from the reference program's by a relative error of at most 0.025.
The reference program's roundings to bfloat16 on the way count: a program that leaves them out, or rounds other values in their place, can miss the bound.
Values may be sent and summed in bfloat16 or wider, within the bound.
A program may use at most 128 MiB of HBM per device.

```python
import math
import jax
import jax.numpy as jnp
import numpy as np
from jax import lax

D = 768
HEADS = 12
HEAD_DIM = 64
FF = 1536
SEQ = 197
EF = 3
NS_ITERS = 3
IMG_DEV = 1
IMAGES = 64
CAP = 197
N_DP = 64
N_TENSOR = 4


def draw_inputs(key, part):
    first_key = jax.random.fold_in(key, 0)
    return jax.random.normal(first_key, (IMAGES, SEQ, D), jnp.float32)


def draw_attn_mats(key, part):
    keys_all = jax.random.split(key, 1)
    full_width = HEADS * HEAD_DIM
    base_draw = jax.random.normal(keys_all[0], (4, D, full_width), jnp.float32) / math.sqrt(D)
    return jnp.concatenate([base_draw[:3], base_draw[3:] * math.sqrt(8.0)], axis=0)


def level_of(rng, shape, cuts, smallest, high):
    loudness, own = 1.0, jax.random.fold_in(rng, 6)
    for axis_at, shards_of in cuts:
        steps = jnp.exp(jax.random.uniform(jax.random.fold_in(own, axis_at), (shards_of,), jnp.float32, smallest / len(cuts), high / len(cuts)))
        loudness = loudness * jnp.repeat(steps, shape[axis_at] // shards_of).reshape([-1 if axis == axis_at else 1 for axis in range(len(shape))])
    return loudness


def assign_block(stream_key, own, number, rows, amount, top, bound, lean):
    sequence = jax.random.permutation(stream_key, amount)
    packed, ordinary = portions_of(amount, rows * top, bound, lean, True), portions_of(amount, rows * top, bound, lean, False)
    places = jnp.arange(amount)

    def named(sizes, turn):
        used = int((sizes > 0).sum())
        fixed = max(1, used // 4)
        shifted = fixed + (places - fixed + turn * (used - fixed)) % max(1, amount - fixed)
        return jnp.zeros((amount,), jnp.int32).at[sequence[jnp.where(places < fixed, places, shifted)]].set(jnp.asarray(sizes, jnp.int32))

    sizes = jnp.where(number % 4 == 0, named(packed, number // 4), named(ordinary, number - number // 4 - 1))
    mixed = jax.random.permutation(jax.random.fold_in(own, 3), amount)
    giver, receiver = mixed[0:amount // 2 * 2:2], mixed[1:amount // 2 * 2:2]
    slack = jnp.minimum(sizes[giver] - 1, bound - sizes[receiver]) // 2
    slack = jnp.where((giver == sequence[0]) | (receiver == sequence[0]) | (sizes[receiver] == 0), 0, jnp.maximum(slack, 0))
    shifted = jax.random.randint(jax.random.fold_in(own, 4), (amount // 2,), 0, 1 << 20) % (slack + 1)
    sizes = sizes.at[giver].add(-shifted).at[receiver].add(shifted)
    members = jnp.searchsorted(jnp.cumsum(sizes), jnp.arange(rows * top), side="right").astype(jnp.int32)
    table = members.reshape(top, rows).T
    table = table[jax.random.permutation(jax.random.fold_in(own, 1), rows)]
    turn = jax.random.randint(jax.random.fold_in(own, 2), (rows, 1), 0, top)
    return jnp.take_along_axis(table, (jnp.arange(top)[None, :] + turn) % top, axis=1)


def portions_of(number_of, total, reach, slope, full):
    weights = [(1 << 20) // math.isqrt(rank ** slope) + 1 for rank in range(1, number_of + 1)]
    largest = reach if full else min(reach, max(-(-total // number_of), total * weights[0] // sum(weights)))
    least = 1 if total - largest >= number_of - 1 else 0
    given, rest = [largest] + [least] * (number_of - 1), total - largest - least * (number_of - 1)
    while rest > 0:
        movable = [i for i in range(1, number_of) if given[i] < largest] or [i for i in range(1, number_of) if given[i] < reach]
        pool, remaining = sum([weights[i] for i in movable]), rest
        for i in movable:
            extra = min(reach - given[i], max(1, remaining * weights[i] // pool), rest)
            given[i] = given[i] + extra
            rest = rest - extra
    return np.array(given)


def gaussian(stream_key, dims, scale, limit, cuts=(), kind=jnp.bfloat16):
    entries = scale * jax.random.normal(stream_key, dims, jnp.float32)
    if cuts:
        entries = entries * level_of(stream_key, dims, cuts, -0.22, 0.18)
    return jnp.clip(entries, -limit, limit).astype(kind)


def setup_inputs(seed: int = 0) -> dict:
    key_of = jax.random.split(jax.random.key(seed), 14)
    inputs = draw_inputs(jax.random.fold_in(key_of[13], 71), 0)
    cotangent = gaussian(key_of[1], (IMAGES, SEQ, D), 1.0, 6.0, ((0, 64),), jnp.float32)
    norm_gains = jnp.clip(1.0 + 0.1 * jax.random.normal(key_of[2], (2, D), jnp.float32), 0.5, 1.5)
    attn_mats = draw_attn_mats(jax.random.fold_in(key_of[13], 71), 0)
    router = gaussian(key_of[4], (D, EF), (D // 4) ** -0.5, 0.4375, ((0, 64),), jnp.float32)
    expert_in = gaussian(key_of[5], (EF, D, FF), D ** -0.5, 0.21875, ((1, 64), (2, 4)), jnp.float32)
    expert_out = gaussian(key_of[6], (EF, D, FF), (FF // 4) ** -0.5, 0.3125, ((1, 64), (2, 4)), jnp.float32)
    moment_gains = gaussian(key_of[7], (2, D), 20.0, 128.0, ((1, 64),), jnp.float32)
    moment_attn = gaussian(key_of[8], (4, D, HEADS * HEAD_DIM), 5.0, 32.0, ((1, 64), (2, 4)), jnp.float32)
    moment_router = gaussian(key_of[9], (D, EF), 50.0, 320.0, ((0, 64),), jnp.float32)
    moment_in = gaussian(key_of[10], (EF, D, FF), 5.0, 32.0, ((1, 64), (2, 4)), jnp.float32)
    moment_out = gaussian(key_of[11], (EF, D, FF), 5.0, 32.0, ((1, 64), (2, 4)), jnp.float32)
    routes_keys = jax.random.split(jax.random.fold_in(key_of[12], 1), IMAGES * SEQ // (IMG_DEV * SEQ))
    routes_turns = jax.random.permutation(jax.random.fold_in(key_of[12], 3), IMAGES * SEQ // (IMG_DEV * SEQ))
    routes = jax.vmap(lambda own, number: assign_block(jax.random.fold_in(key_of[12], 2), own, number, IMG_DEV * SEQ, EF, 2, CAP, 1))(routes_keys, routes_turns).reshape((IMAGES, SEQ, 2))
    return {"inputs": inputs, "cotangent": cotangent, "norm_gains": norm_gains, "attn_mats": attn_mats, "router": router, "expert_in": expert_in, "expert_out": expert_out, "moment_gains": moment_gains, "moment_attn": moment_attn, "moment_router": moment_router, "moment_in": moment_in, "moment_out": moment_out, "routes": routes}


EPSILON = 1e-06
MOMENTUM = 0.9
MUON_RATE = 0.5
SMALL_RATE = 0.5
NEWTON_A = 3.4445
NEWTON_B = -4.775
NEWTON_C = 2.0315
ROOT_HALF = 0.7071067811865476
INV_ROOT_TAU = 0.3989422804014327

def round_half(operand):
    return lax.optimization_barrier(operand.astype(jnp.bfloat16))

def to_single(operand):
    return operand.astype(jnp.float32)

def norm_forward(row_data, gain_row):
    center = row_data - lax.optimization_barrier(jnp.mean(row_data, axis=-1, keepdims=True))
    inv_std = lax.rsqrt(lax.optimization_barrier(jnp.mean(center * center, axis=-1, keepdims=True)) + EPSILON)
    normal = center * inv_std
    return (normal, inv_std, round_half(normal * gain_row))

def norm_backward(grad_result, normal, inv_std, gain_row):
    scaled = grad_result * gain_row
    grad_data = inv_std * (scaled - lax.optimization_barrier(jnp.mean(scaled, axis=-1, keepdims=True)) - normal * lax.optimization_barrier(jnp.mean(scaled * normal, axis=-1, keepdims=True)))
    return (grad_data, lax.optimization_barrier(jnp.sum(grad_result * normal, axis=0)))

def gelu_value(pre_act):
    return 0.5 * pre_act * (1.0 + lax.erf(pre_act * ROOT_HALF))

def gelu_slope(pre_act):
    return 0.5 * (1.0 + lax.erf(pre_act * ROOT_HALF)) + pre_act * INV_ROOT_TAU * jnp.exp(-0.5 * pre_act * pre_act)

def slot_tables(picked, experts, capacity):
    flat_picks = picked.reshape(-1)
    assign_count = flat_picks.shape[0]
    one_hot = (flat_picks[:, None] == jnp.arange(experts, dtype=jnp.int32)[None, :]).astype(jnp.int32)
    before = jnp.cumsum(one_hot, axis=0) - one_hot
    slot_place = lax.optimization_barrier(jnp.sum(before * one_hot, axis=1))
    target = (flat_picks * capacity + slot_place).astype(jnp.int32)
    slot_owner = jnp.full((experts * capacity,), assign_count, jnp.int32).at[target].set(jnp.arange(assign_count, dtype=jnp.int32))
    return (target, slot_owner)

def score_table(queries, key_rows):
    return jnp.einsum('bqhd,bkhd->bhqk', to_single(queries), to_single(key_rows)) * (1.0 / math.sqrt(HEAD_DIM))

def attention_forward(normed, mats_half, image_count):
    head_count = mats_half.shape[2] // HEAD_DIM

    def project(which_mat):
        return round_half(jnp.dot(normed, mats_half[which_mat], preferred_element_type=jnp.float32)).reshape(image_count, SEQ, head_count, HEAD_DIM)
    queries = project(0)
    key_rows = project(1)
    value_rows = project(2)
    scores = score_table(queries, key_rows)
    row_peak = lax.optimization_barrier(jnp.max(scores, axis=-1, keepdims=True))
    log_total = row_peak + jnp.log(lax.optimization_barrier(jnp.sum(jnp.exp(scores - row_peak), axis=-1, keepdims=True)))
    prob_half = round_half(jnp.exp(scores - log_total))
    attn_rows = round_half(jnp.einsum('bhqk,bkhd->bqhd', to_single(prob_half), to_single(value_rows)))
    return (queries, key_rows, value_rows, log_total, attn_rows.reshape(image_count * SEQ, head_count * HEAD_DIM))

def attention_backward(grad_attn_rows, queries, key_rows, value_rows, log_total, image_count):
    head_count = queries.shape[2]
    grad_heads = grad_attn_rows.reshape(image_count, SEQ, head_count, HEAD_DIM)
    prob_full = jnp.exp(score_table(queries, key_rows) - log_total)
    prob_half = round_half(prob_full)
    grad_prob = jnp.einsum('bqhd,bkhd->bhqk', to_single(grad_heads), to_single(value_rows))
    grad_values = round_half(jnp.einsum('bhqk,bqhd->bkhd', to_single(prob_half), to_single(grad_heads)))
    spread = lax.optimization_barrier(jnp.sum(prob_full * grad_prob, axis=-1, keepdims=True))
    grad_scores = round_half(prob_full * (grad_prob - spread) * (1.0 / math.sqrt(HEAD_DIM)))
    grad_queries = round_half(jnp.einsum('bhqk,bkhd->bqhd', to_single(grad_scores), to_single(key_rows)))
    grad_keys = round_half(jnp.einsum('bhqk,bqhd->bkhd', to_single(grad_scores), to_single(queries)))
    full_width = head_count * HEAD_DIM
    return (grad_queries.reshape(image_count * SEQ, full_width), grad_keys.reshape(image_count * SEQ, full_width), grad_values.reshape(image_count * SEQ, full_width))

def orthogonalize(matrix):
    current = round_half(matrix * lax.rsqrt(jnp.sum(matrix * matrix) + EPSILON))
    for iteration in range(NS_ITERS):
        gram_mat = round_half(lax.dot_general(current, current, (((0,), (0,)), ((), ())), preferred_element_type=jnp.float32))
        square = jnp.dot(gram_mat, gram_mat, preferred_element_type=jnp.float32)
        poly_mat = round_half(NEWTON_B * to_single(gram_mat) + NEWTON_C * square)
        current = round_half(NEWTON_A * to_single(current) + jnp.dot(current, poly_mat, preferred_element_type=jnp.float32))
    return current

def muon_blocks(look):
    block_count, rows_all, col_count = look.shape
    piece_width = col_count // N_TENSOR
    split_blocks = jnp.transpose(look.reshape(block_count, rows_all, N_TENSOR, piece_width), (0, 2, 1, 3)).reshape(block_count * N_TENSOR, rows_all, piece_width)
    solved = lax.map(orthogonalize, split_blocks)
    return jnp.transpose(solved.reshape(block_count, N_TENSOR, rows_all, piece_width), (0, 2, 1, 3)).reshape(block_count, rows_all, col_count)

def reference(inputs, cotangent, norm_gains, attn_mats, router, expert_in, expert_out, moment_gains, moment_attn, moment_router, moment_in, moment_out, routes):
    gains_half = round_half(norm_gains)
    gain_one = to_single(gains_half[0])
    gain_two = to_single(gains_half[1])
    attn_half = round_half(attn_mats)
    router_half = round_half(router)
    in_single = to_single(round_half(expert_in))
    out_single = to_single(round_half(expert_out))
    full_width = HEADS * HEAD_DIM

    def block_step(totals, pieces):
        acc_gains, acc_attn, acc_router, acc_in, acc_out = totals
        block_in, block_cot, block_route = pieces
        row_in = block_in.reshape(-1, D)
        row_count = row_in.shape[0]
        normal_one, inv_one, normed_one = norm_forward(row_in, gain_one)
        queries, key_rows, value_rows, log_total, attn_rows = attention_forward(normed_one, attn_half, IMG_DEV)
        middle = row_in + jnp.dot(attn_rows, attn_half[3].T, preferred_element_type=jnp.float32)
        normal_two, inv_two, normed_two = norm_forward(middle, gain_two)
        target, slot_owner = slot_tables(block_route, EF, CAP)
        logits = jnp.dot(normed_two, router_half, preferred_element_type=jnp.float32)
        chosen = jnp.take_along_axis(logits, block_route, axis=1)
        gate_vals = jax.nn.sigmoid(chosen - chosen[:, ::-1])
        padded = jnp.concatenate([normed_two, jnp.zeros((1, D), jnp.bfloat16)], axis=0)
        dispatched = padded[slot_owner // 2].reshape(EF, CAP, D)
        pre_act = jnp.einsum('ecd,edf->ecf', to_single(dispatched), in_single)
        hidden = round_half(gelu_value(pre_act))
        expert_rows = jnp.einsum('ecf,edf->ecd', to_single(hidden), out_single)
        per_choice = expert_rows.reshape(EF * CAP, D)[target].reshape(row_count, 2, D)
        output_rows = middle + lax.optimization_barrier(jnp.sum(gate_vals[:, :, None] * per_choice, axis=1))
        grad_rows = block_cot.reshape(-1, D)
        grad_choice = lax.optimization_barrier(jnp.sum(grad_rows[:, None, :] * per_choice, axis=2))
        gate_flat = jnp.concatenate([gate_vals.reshape(-1), jnp.zeros((1,), jnp.float32)])
        grad_pad = jnp.concatenate([grad_rows, jnp.zeros((1, D), jnp.float32)], axis=0)
        grad_expert = round_half(gate_flat[slot_owner][:, None] * grad_pad[slot_owner // 2]).reshape(EF, CAP, D)
        grad_hidden = jnp.einsum('ecd,edf->ecf', to_single(grad_expert), out_single)
        grad_pre = round_half(grad_hidden * gelu_slope(pre_act))
        grad_dispatch = jnp.einsum('ecf,edf->ecd', to_single(grad_pre), in_single)
        grad_normed_moe = lax.optimization_barrier(jnp.sum(grad_dispatch.reshape(EF * CAP, D)[target].reshape(row_count, 2, D), axis=1))
        step_in = jnp.einsum('ecd,ecf->edf', to_single(dispatched), to_single(grad_pre))
        step_out = jnp.einsum('ecd,ecf->edf', to_single(grad_expert), to_single(hidden))
        gate_prod = gate_vals[:, 0] * gate_vals[:, 1]
        grad_first = (grad_choice[:, 0] - grad_choice[:, 1]) * gate_prod
        grad_picked = jnp.stack([grad_first, -grad_first], axis=1)
        one_hot = (block_route[:, :, None] == jnp.arange(EF, dtype=jnp.int32)[None, None, :]).astype(jnp.float32)
        grad_logits = round_half(lax.optimization_barrier(jnp.sum(grad_picked[:, :, None] * one_hot, axis=1)))
        step_router = jnp.dot(normed_two.T, grad_logits, preferred_element_type=jnp.float32)
        grad_normed_two = grad_normed_moe + jnp.dot(grad_logits, router_half.T, preferred_element_type=jnp.float32)
        grad_mid_norm, step_gain_two = norm_backward(grad_normed_two, normal_two, inv_two, gain_two)
        grad_middle = grad_rows + grad_mid_norm
        grad_mid_half = round_half(grad_middle)
        grad_attn_rows = round_half(jnp.dot(grad_mid_half, attn_half[3], preferred_element_type=jnp.float32))
        step_proj = jnp.dot(grad_mid_half.T, attn_rows, preferred_element_type=jnp.float32)
        grad_queries, grad_keys, grad_values = attention_backward(grad_attn_rows, queries, key_rows, value_rows, log_total, IMG_DEV)
        step_attn = jnp.stack([jnp.dot(normed_one.T, grad_queries, preferred_element_type=jnp.float32), jnp.dot(normed_one.T, grad_keys, preferred_element_type=jnp.float32), jnp.dot(normed_one.T, grad_values, preferred_element_type=jnp.float32), step_proj])
        grad_normed_one = jnp.dot(grad_queries, attn_half[0].T, preferred_element_type=jnp.float32) + jnp.dot(grad_keys, attn_half[1].T, preferred_element_type=jnp.float32) + jnp.dot(grad_values, attn_half[2].T, preferred_element_type=jnp.float32)
        grad_in_norm, step_gain_one = norm_backward(grad_normed_one, normal_one, inv_one, gain_one)
        grad_inputs_rows = grad_middle + grad_in_norm
        new_totals = (acc_gains + jnp.stack([step_gain_one, step_gain_two]), acc_attn + step_attn, acc_router + step_router, acc_in + step_in, acc_out + step_out)
        return (new_totals, (output_rows, grad_inputs_rows))
    start = (jnp.zeros((2, D), jnp.float32), jnp.zeros((4, D, full_width), jnp.float32), jnp.zeros((D, EF), jnp.float32), jnp.zeros((EF, D, FF), jnp.float32), jnp.zeros((EF, D, FF), jnp.float32))
    block_inputs = inputs.reshape(N_DP, IMG_DEV, SEQ, D)
    block_cots = cotangent.reshape(N_DP, IMG_DEV, SEQ, D)
    block_routes = routes.reshape(N_DP, IMG_DEV * SEQ, 2)
    totals, stacked = lax.scan(block_step, start, (block_inputs, block_cots, block_routes))
    grad_gains, grad_attn, grad_router, grad_in, grad_out = totals
    output = stacked[0].reshape(IMAGES, SEQ, D)
    grad_inputs = stacked[1].reshape(IMAGES, SEQ, D)
    small_step = SMALL_RATE / math.sqrt(IMAGES * SEQ)
    moment_gains_new = MOMENTUM * moment_gains + grad_gains
    moment_attn_new = MOMENTUM * moment_attn + grad_attn
    moment_router_new = MOMENTUM * moment_router + grad_router
    moment_in_new = MOMENTUM * moment_in + grad_in
    moment_out_new = MOMENTUM * moment_out + grad_out
    gains_new = norm_gains - small_step * moment_gains_new
    router_new = router - small_step * moment_router_new
    look_attn = grad_attn + MOMENTUM * moment_attn_new
    look_in = grad_in + MOMENTUM * moment_in_new
    look_out = grad_out + MOMENTUM * moment_out_new
    attn_new = attn_mats - MUON_RATE * to_single(muon_blocks(look_attn))
    in_new = expert_in - MUON_RATE * to_single(muon_blocks(look_in))
    out_new = expert_out - MUON_RATE * to_single(muon_blocks(look_out))
    return (output, grad_inputs, grad_gains, grad_attn, grad_router, grad_in, grad_out, gains_new, attn_new, router_new, in_new, out_new, moment_gains_new, moment_attn_new, moment_router_new, moment_in_new, moment_out_new)
```

```python
import math

import jax
import jax.numpy as jnp
import numpy as np
from jax import lax
from jax.sharding import PartitionSpec as P

HEAD_DIM = 64
EF = 3
NS_ITERS = 3
CAP = 197


EPSILON = 1e-06
MOMENTUM = 0.9
MUON_RATE = 0.5
SMALL_RATE = 0.5
NEWTON_A = 3.4445
NEWTON_B = -4.775
NEWTON_C = 2.0315
ROOT_HALF = 0.7071067811865476
INV_ROOT_TAU = 0.3989422804014327


def for_sending(value):
    return jax.tree.map(lambda a: a.astype(jnp.bfloat16) if a.dtype == jnp.float32 else a, value)


def round_half(operand):
    return operand.astype(jnp.bfloat16)


def settle(operand):
    return lax.optimization_barrier(operand.astype(jnp.bfloat16))


def to_single(operand):
    return operand.astype(jnp.float32)


def contract_rows(left_mat, right_mat):
    return lax.dot_general(
        left_mat, right_mat, (((0,), (0,)), ((), ())), preferred_element_type=jnp.float32
    )


def contract_cols(left_mat, right_mat):
    return lax.dot_general(
        left_mat, right_mat, (((1,), (1,)), ((), ())), preferred_element_type=jnp.float32
    )


def fold_sources(received, source_count):
    return jnp.sum(
        received.reshape((source_count, received.shape[0] // source_count) + received.shape[1:]),
        axis=0,
    )


def norm_forward(row_data, gain_row):
    center = row_data - jnp.mean(row_data, axis=-1, keepdims=True)
    inv_std = lax.rsqrt(jnp.mean(center * center, axis=-1, keepdims=True) + EPSILON)
    normal = center * inv_std
    return (normal, inv_std, round_half(normal * gain_row))


def norm_backward(grad_result, normal, inv_std, gain_row):
    scaled = grad_result * gain_row
    grad_data = inv_std * (
        scaled
        - jnp.mean(scaled, axis=-1, keepdims=True)
        - normal * jnp.mean(scaled * normal, axis=-1, keepdims=True)
    )
    return (grad_data, jnp.sum(grad_result * normal, axis=0))


def gelu_value(pre_act):
    return 0.5 * pre_act * (1.0 + lax.erf(pre_act * ROOT_HALF))


def gelu_slope(pre_act):
    return 0.5 * (1.0 + lax.erf(pre_act * ROOT_HALF)) + pre_act * INV_ROOT_TAU * jnp.exp(
        -0.5 * pre_act * pre_act
    )


def score_table(queries, key_rows):
    return jnp.einsum("bqhd,bkhd->bhqk", queries, key_rows, preferred_element_type=jnp.float32) * (
        1.0 / math.sqrt(HEAD_DIM)
    )


def attention_forward(normed, mats_half, image_count, seq_len):
    head_count = mats_half.shape[2] // HEAD_DIM

    def project(which_mat):
        return round_half(
            jnp.dot(normed, mats_half[which_mat], preferred_element_type=jnp.float32)
        ).reshape(image_count, seq_len, head_count, HEAD_DIM)

    queries = project(0)
    key_rows = project(1)
    value_rows = project(2)
    scores = score_table(queries, key_rows)
    row_peak = jnp.max(scores, axis=-1, keepdims=True)
    log_total = row_peak + jnp.log(jnp.sum(jnp.exp(scores - row_peak), axis=-1, keepdims=True))
    prob_half = round_half(jnp.exp(scores - log_total))
    attn_rows = round_half(
        jnp.einsum("bhqk,bkhd->bqhd", prob_half, value_rows, preferred_element_type=jnp.float32)
    )
    return (
        queries,
        key_rows,
        value_rows,
        log_total,
        attn_rows.reshape(image_count * seq_len, head_count * HEAD_DIM),
    )


def attention_backward(grad_attn_rows, queries, key_rows, value_rows, log_total):
    image_count, seq_len, head_count, head_size = queries.shape
    grad_heads = grad_attn_rows.reshape(image_count, seq_len, head_count, head_size)
    prob_full = jnp.exp(score_table(queries, key_rows) - log_total)
    prob_half = round_half(prob_full)
    grad_prob = jnp.einsum(
        "bqhd,bkhd->bhqk", grad_heads, value_rows, preferred_element_type=jnp.float32
    )
    grad_values = round_half(
        jnp.einsum("bhqk,bqhd->bkhd", prob_half, grad_heads, preferred_element_type=jnp.float32)
    )
    spread = jnp.sum(prob_full * grad_prob, axis=-1, keepdims=True)
    grad_scores = round_half(prob_full * (grad_prob - spread) * (1.0 / math.sqrt(HEAD_DIM)))
    grad_queries = round_half(
        jnp.einsum("bhqk,bkhd->bqhd", grad_scores, key_rows, preferred_element_type=jnp.float32)
    )
    grad_keys = round_half(
        jnp.einsum("bhqk,bqhd->bkhd", grad_scores, queries, preferred_element_type=jnp.float32)
    )
    row_total = image_count * seq_len
    full_width = head_count * head_size
    return (
        grad_queries.reshape(row_total, full_width),
        grad_keys.reshape(row_total, full_width),
        grad_values.reshape(row_total, full_width),
    )


def orthogonalize(matrix):
    current = settle(matrix * lax.rsqrt(jnp.sum(matrix * matrix) + EPSILON))
    for iteration in range(NS_ITERS):
        gram_mat = settle(contract_rows(current, current))
        square = jnp.dot(gram_mat, gram_mat, preferred_element_type=jnp.float32)
        poly_mat = round_half(NEWTON_B * to_single(gram_mat) + NEWTON_C * square)
        current = settle(
            NEWTON_A * to_single(current)
            + jnp.dot(current, poly_mat, preferred_element_type=jnp.float32)
        )
    return current


def orthogonalize_attention(block_mat):
    rows_all, slot_width = block_mat.shape
    sub_blocks = jnp.transpose(block_mat.reshape(rows_all, 2, slot_width // 2), (1, 0, 2))
    solved = jnp.stack([orthogonalize(sub_blocks[which_mat]) for which_mat in range(2)])
    return jnp.transpose(solved, (1, 0, 2)).reshape(rows_all, slot_width)


def empty_block(block_mat):
    return jnp.zeros(block_mat.shape, jnp.bfloat16)


def shards(
    inputs,
    cotangent,
    norm_gains,
    attn_mats,
    router,
    expert_in,
    expert_out,
    moment_gains,
    moment_attn,
    moment_router,
    moment_in,
    moment_out,
    routes,
):
    image_count, seq_len, model_width = inputs.shape
    dp_count = lax.axis_size("dp")
    row_count = image_count * seq_len
    small_plane = jnp.zeros((1, norm_gains.shape[1], attn_mats.shape[2]), jnp.bfloat16)
    small_plane = small_plane.at[0, :, :2].set(round_half(norm_gains).T)
    small_plane = small_plane.at[0, :, 2 : 2 + EF].set(round_half(router))
    packed = lax.all_gather(
        jnp.concatenate([round_half(attn_mats), small_plane], axis=0), "dp", axis=1, tiled=True
    )
    attn_half = packed[:4]
    gains_half = packed[4, :, :2].T
    router_half = packed[4, :, 2 : 2 + EF]
    in_half = lax.all_gather(round_half(expert_in), "dp", axis=1, tiled=True)
    out_half = lax.all_gather(round_half(expert_out), "dp", axis=1, tiled=True)
    gain_one = to_single(gains_half[0])
    gain_two = to_single(gains_half[1])
    row_in = inputs.reshape(row_count, model_width)
    normal_one, inv_one, normed_one = norm_forward(row_in, gain_one)
    queries, key_rows, value_rows, log_total, attn_rows = attention_forward(
        normed_one, attn_half, image_count, seq_len
    )
    attn_part = contract_cols(attn_rows, attn_half[3])
    attn_full = lax.psum(attn_part.astype(jnp.bfloat16), "tensor").astype(jnp.float32)
    middle = row_in + attn_full
    normal_two, inv_two, normed_two = norm_forward(middle, gain_two)
    picked = routes.reshape(row_count, 2)
    one_hot = (picked[:, :, None] == jnp.arange(EF, dtype=jnp.int32)[None, None, :]).astype(
        jnp.float32
    )
    logits = jnp.dot(normed_two, router_half, preferred_element_type=jnp.float32)
    chosen = jnp.sum(logits[:, None, :] * one_hot, axis=2)
    gate_vals = jax.nn.sigmoid(chosen - chosen[:, ::-1])
    gate_table = jnp.sum(gate_vals[:, :, None] * one_hot, axis=1)
    grad_rows = cotangent.reshape(row_count, model_width)
    pre_act = jnp.einsum("td,edf->etf", normed_two, in_half, preferred_element_type=jnp.float32)
    hidden = round_half(gelu_value(pre_act))
    expert_rows = jnp.einsum("etf,edf->etd", hidden, out_half, preferred_element_type=jnp.float32)
    moe_part = jnp.sum(gate_table.T[:, :, None] * expert_rows, axis=0)
    moe_full = lax.psum(moe_part.astype(jnp.bfloat16), "tensor").astype(jnp.float32)
    output_rows = middle + moe_full
    grad_each = jnp.sum(grad_rows[None] * expert_rows, axis=2).T
    grad_choice_part = jnp.sum(grad_each[:, None, :] * one_hot, axis=2)
    grad_expert = round_half(gate_table.T[:, :, None] * grad_rows[None])
    grad_hidden = jnp.einsum(
        "etd,edf->etf", grad_expert, out_half, preferred_element_type=jnp.float32
    )
    grad_pre = round_half(grad_hidden * gelu_slope(pre_act))
    grad_normed_part = jnp.einsum(
        "etf,edf->td", grad_pre, in_half, preferred_element_type=jnp.float32
    )
    grad_in = jnp.einsum("td,etf->edf", normed_two, grad_pre, preferred_element_type=jnp.float32)
    grad_out = jnp.einsum("etd,etf->edf", grad_expert, hidden, preferred_element_type=jnp.float32)
    joined = lax.psum(
        jnp.concatenate([grad_normed_part, grad_choice_part], axis=1).astype(jnp.bfloat16), "tensor"
    ).astype(jnp.float32)
    grad_normed_moe, grad_choice = joined[:, :model_width], joined[:, model_width:]
    gate_prod = gate_vals[:, 0] * gate_vals[:, 1]
    grad_first = (grad_choice[:, 0] - grad_choice[:, 1]) * gate_prod
    grad_picked = jnp.stack([grad_first, -grad_first], axis=1)
    grad_logits = round_half(jnp.sum(grad_picked[:, :, None] * one_hot, axis=1))
    grad_router = contract_rows(normed_two, grad_logits)
    grad_normed_two = grad_normed_moe + contract_cols(grad_logits, router_half)
    grad_mid_norm, grad_gain_two = norm_backward(grad_normed_two, normal_two, inv_two, gain_two)
    grad_middle = grad_rows + grad_mid_norm
    grad_mid_half = round_half(grad_middle)
    grad_attn_rows = round_half(
        jnp.dot(grad_mid_half, attn_half[3], preferred_element_type=jnp.float32)
    )
    grad_proj_out = contract_rows(grad_mid_half, attn_rows)
    grad_queries, grad_keys, grad_values = attention_backward(
        grad_attn_rows, queries, key_rows, value_rows, log_total
    )
    grad_attn = jnp.stack(
        [
            contract_rows(normed_one, grad_queries),
            contract_rows(normed_one, grad_keys),
            contract_rows(normed_one, grad_values),
            grad_proj_out,
        ]
    )
    grad_normed_one_part = (
        contract_cols(grad_queries, attn_half[0])
        + contract_cols(grad_keys, attn_half[1])
        + contract_cols(grad_values, attn_half[2])
    )
    grad_normed_one = lax.psum(grad_normed_one_part.astype(jnp.bfloat16), "tensor").astype(
        jnp.float32
    )
    grad_in_norm, grad_gain_one = norm_backward(grad_normed_one, normal_one, inv_one, gain_one)
    grad_inputs_rows = grad_middle + grad_in_norm
    gains_cols = jnp.stack([grad_gain_one, grad_gain_two], axis=1)
    small_cols = jnp.concatenate([gains_cols, grad_router], axis=1)
    got_attn, got_in, got_out, got_small = (
        lax.all_to_all(
            grad_attn.astype(jnp.bfloat16), "dp", split_axis=1, concat_axis=0, tiled=True
        ).astype(grad_attn.dtype),
        lax.all_to_all(
            grad_in.astype(jnp.bfloat16), "dp", split_axis=1, concat_axis=0, tiled=True
        ).astype(grad_in.dtype),
        lax.all_to_all(
            grad_out.astype(jnp.bfloat16), "dp", split_axis=1, concat_axis=0, tiled=True
        ).astype(grad_out.dtype),
        lax.all_to_all(
            small_cols[None].astype(jnp.bfloat16), "dp", split_axis=1, concat_axis=0, tiled=True
        ).astype(jnp.float32),
    )
    sum_attn = fold_sources(got_attn, dp_count)
    sum_in = fold_sources(got_in, dp_count)
    sum_out = fold_sources(got_out, dp_count)
    sum_small = fold_sources(got_small, dp_count)[0]
    sum_gains = sum_small[:, :2].T
    sum_router = sum_small[:, 2:]
    small_step = SMALL_RATE / math.sqrt(image_count * dp_count * seq_len)
    moment_gains_new = MOMENTUM * moment_gains + sum_gains
    moment_attn_new = MOMENTUM * moment_attn + sum_attn
    moment_router_new = MOMENTUM * moment_router + sum_router
    moment_in_new = MOMENTUM * moment_in + sum_in
    moment_out_new = MOMENTUM * moment_out + sum_out
    gains_new = norm_gains - small_step * moment_gains_new
    router_new = router - small_step * moment_router_new
    look_attn = sum_attn + MOMENTUM * moment_attn_new
    look_in = sum_in + MOMENTUM * moment_in_new
    look_out = sum_out + MOMENTUM * moment_out_new
    shard_rows = look_in.shape[1]
    slot_width = look_in.shape[2]
    blocks = 2 * EF + 2
    per_owner = -(-blocks // dp_count)
    slot_count = dp_count * per_owner
    slot_list = list(range(blocks))
    block_list = [
        slot_list.index(slot_number) if slot_number in slot_list else blocks
        for slot_number in range(slot_count)
    ]
    slot_of_block = np.array(slot_list)
    block_of_slot = np.array(block_list)
    kind_of_slot = np.where(block_of_slot < 2, 0, np.where(block_of_slot < blocks, 1, 2))
    attn_slots = jnp.transpose(
        jnp.transpose(look_attn, (1, 0, 2)).reshape(shard_rows, 2, slot_width), (1, 0, 2)
    )
    stacked = jnp.concatenate(
        [attn_slots, look_in, look_out, jnp.zeros((1, shard_rows, slot_width), jnp.float32)], axis=0
    )
    outgoing = jnp.take(stacked, jnp.asarray(block_of_slot, dtype=jnp.int32), axis=0)
    arrived = lax.all_to_all(
        for_sending(outgoing), "dp", split_axis=0, concat_axis=1, tiled=True
    ).astype(outgoing.dtype)
    own_index = lax.axis_index("dp")
    kind_table = jnp.asarray(kind_of_slot, dtype=jnp.int32)
    kind_now = kind_table[own_index * per_owner + 0]
    results = [
        lax.switch(kind_now, [orthogonalize_attention, orthogonalize, empty_block], arrived[0])
    ]
    finished = jnp.stack(results)
    returned = lax.all_to_all(
        for_sending(finished), "dp", split_axis=1, concat_axis=0, tiled=True
    ).astype(finished.dtype)
    updates = to_single(jnp.take(returned, jnp.asarray(slot_of_block, dtype=jnp.int32), axis=0))
    update_attn = jnp.transpose(
        jnp.transpose(updates[0:2], (1, 0, 2)).reshape(shard_rows, 4, slot_width // 2), (1, 0, 2)
    )
    attn_new = attn_mats - MUON_RATE * update_attn
    in_new = expert_in - MUON_RATE * updates[2 : EF + 2]
    out_new = expert_out - MUON_RATE * updates[EF + 2 : 2 * EF + 2]
    output = output_rows.reshape(image_count, seq_len, model_width)
    grad_inputs = grad_inputs_rows.reshape(image_count, seq_len, model_width)
    return (
        output,
        grad_inputs,
        sum_gains,
        sum_attn,
        sum_router,
        sum_in,
        sum_out,
        gains_new,
        attn_new,
        router_new,
        in_new,
        out_new,
        moment_gains_new,
        moment_attn_new,
        moment_router_new,
        moment_in_new,
        moment_out_new,
    )


def solution(mesh):
    return jax.shard_map(
        shards,
        mesh=mesh,
        in_specs=(
            P("dp", None, None),
            P("dp", None, None),
            P(None, "dp"),
            P(None, "dp", "tensor"),
            P("dp", None),
            P(None, "dp", "tensor"),
            P(None, "dp", "tensor"),
            P(None, "dp"),
            P(None, "dp", "tensor"),
            P("dp", None),
            P(None, "dp", "tensor"),
            P(None, "dp", "tensor"),
            P("dp", None, None),
        ),
        out_specs=(
            P("dp", None, None),
            P("dp", None, None),
            P(None, "dp"),
            P(None, "dp", "tensor"),
            P("dp", None),
            P(None, "dp", "tensor"),
            P(None, "dp", "tensor"),
            P(None, "dp"),
            P(None, "dp", "tensor"),
            P("dp", None),
            P(None, "dp", "tensor"),
            P(None, "dp", "tensor"),
            P(None, "dp"),
            P(None, "dp", "tensor"),
            P("dp", None),
            P(None, "dp", "tensor"),
            P(None, "dp", "tensor"),
        ),
        check_vma=False,
    )
```

```python
import math

import jax
import jax.numpy as jnp
import numpy as np
from jax import lax
from jax.experimental import pallas as pl
from jax.experimental.pallas import tpu as pltpu
from jax.sharding import PartitionSpec as P

HEAD_DIM = 64
EF = 3
NS_ITERS = 3
CAP = 197


EPSILON = 1e-06
MOMENTUM = 0.9
MUON_RATE = 0.5
SMALL_RATE = 0.5
NEWTON_A = 3.4445
NEWTON_B = -4.775
NEWTON_C = 2.0315
ROOT_HALF = 0.7071067811865476
INV_ROOT_TAU = 0.3989422804014327


def round_half(operand):
    return operand.astype(jnp.bfloat16)


def settle(operand):
    return lax.optimization_barrier(operand.astype(jnp.bfloat16))


def to_single(operand):
    return operand.astype(jnp.float32)


def contract_rows(left_mat, right_mat):
    return lax.dot_general(
        left_mat, right_mat, (((0,), (0,)), ((), ())), preferred_element_type=jnp.float32
    )


def contract_cols(left_mat, right_mat):
    return lax.dot_general(
        left_mat, right_mat, (((1,), (1,)), ((), ())), preferred_element_type=jnp.float32
    )


NZ, NX, NY = 8, 4, 2
ROW = 12
LANE = 128
PACK = 304
SPLIT = 128
PLANE = NX * NY
BLOCKS = 8
MESH_ID = pl.DeviceIdType.MESH
GROUPS = ((0, 4), (4, 4), (8, 4), (12, 4), (16, 4), (20, 4), (24, 1))


def spread_matrix(block_count, padded):
    table = np.zeros((block_count * PLANE * ROW, PLANE * padded), np.float32)
    for block in range(block_count):
        for member in range(PLANE):
            for row in range(ROW):
                table[
                    block * PLANE * ROW + member * ROW + row, member * padded + block * ROW + row
                ] = 1.0
    return jnp.asarray(table, jnp.bfloat16)


def place_of(me):
    return me // PLANE, lax.rem(me // NY, NX), lax.rem(me, NY)


def dp_index(z, x, y):
    return z * PLANE + x * NY + y


def wrap(value, count):
    return lax.rem(value + 2 * count, count)


def neighbours(me):
    z, x, y = place_of(me)
    return (
        dp_index(wrap(z + 1, NZ), x, y),
        dp_index(wrap(z - 1, NZ), x, y),
        dp_index(z, wrap(x + 1, NX), y),
        dp_index(z, wrap(x - 1, NX), y),
        dp_index(z, x, 1 - y),
    )


def greet(targets, count):
    barrier = pltpu.get_barrier_semaphore()
    for target in targets:
        pl.semaphore_signal(barrier, inc=1, device_id={"dp": target}, device_id_type=MESH_ID)
    pl.semaphore_wait(barrier, count)


def send(source, landing, send_sem, recv_sem, target):
    copy = pltpu.make_async_remote_copy(
        src_ref=source,
        dst_ref=landing,
        send_sem=send_sem,
        recv_sem=recv_sem,
        device_id={"dp": target},
        device_id_type=MESH_ID,
    )
    copy.start()
    return copy


class GatherRing:
    def __init__(self, chunk, position, count, up, down, send_sems, recv_sems, base):
        self.chunk, self.position, self.count = chunk, position, count
        self.up, self.down = up, down
        self.send_sems, self.recv_sems, self.base = send_sems, recv_sems, base
        self.copies = []

    def start(self, step):
        half = step == self.count // 2 - 1
        pair = []
        for side, (sign, target) in enumerate(((-1, self.up), (1, self.down))):
            part = self.chunk(wrap(self.position + sign * step, self.count), side if half else None)
            slot = self.base + 2 * step + side
            pair.append(send(part, part, self.send_sems.at[slot], self.recv_sems.at[slot], target))
        self.copies.append(pair)

    def arrive(self, step):
        for copy in self.copies[step]:
            copy.wait_recv()

    def finish(self):
        for pair in self.copies:
            for copy in pair:
                copy.wait_send()


def gather_kernel(
    shard, four, one, attn_out, small_out, in_out, out_out, slots, local_sem, send_sems, recv_sems
):
    me = lax.axis_index("dp")
    z, x, y = place_of(me)
    up_z, down_z, up_x, down_x, other_y = neighbours(me)
    greet((up_z, down_z, up_x, down_x, other_y), 5)
    own = slots.at[z, NY * x + y]
    keep = pltpu.make_async_copy(shard, own, local_sem)
    keep.start()
    first = send(shard, own, send_sems.at[0], recv_sems.at[0], other_y)
    keep.wait()
    first.wait_recv()

    def part_x_small(index, half):
        if half is None:
            return slots.at[z, pl.ds(NY * index, NY), pl.ds(0, SPLIT)]
        return slots.at[z, NY * index + half, pl.ds(0, SPLIT)]

    def part_z_small(index, half):
        rest = pl.ds(SPLIT, PACK - SPLIT)
        if half is None:
            return slots.at[index, pl.ds(NY * x, NY), rest]
        return slots.at[index, NY * x + half, rest]

    def part_z_large(index, half):
        if half is None:
            return slots.at[index, pl.ds(0, PLANE), pl.ds(0, SPLIT)]
        return slots.at[index, pl.ds(half * (PLANE // 2), PLANE // 2), pl.ds(0, SPLIT)]

    def part_x_large(index, half):
        rest = pl.ds(SPLIT, PACK - SPLIT)
        if half is None:
            return slots.at[pl.ds(0, NZ), pl.ds(NY * index, NY), rest]
        return slots.at[pl.ds(half * (NZ // 2), NZ // 2), pl.ds(NY * index, NY), rest]

    ring_ax = GatherRing(part_x_small, x, NX, up_x, down_x, send_sems, recv_sems, 1)
    ring_bz = GatherRing(part_z_small, z, NZ, up_z, down_z, send_sems, recv_sems, 5)
    ring_az = GatherRing(part_z_large, z, NZ, up_z, down_z, send_sems, recv_sems, 13)
    ring_bx = GatherRing(part_x_large, x, NX, up_x, down_x, send_sems, recv_sems, 21)
    ring_ax.start(0)
    ring_bz.start(0)
    ring_ax.arrive(0)
    ring_ax.start(1)
    ring_bz.arrive(0)
    ring_bz.start(1)
    ring_ax.arrive(1)
    ring_az.start(0)
    ring_bz.arrive(1)
    ring_bz.start(2)
    ring_bz.arrive(2)
    ring_bz.start(3)
    ring_az.arrive(0)
    ring_az.start(1)
    ring_bz.arrive(3)
    ring_bx.start(0)
    ring_az.arrive(1)
    ring_az.start(2)
    ring_az.arrive(2)
    ring_az.start(3)
    ring_bx.arrive(0)
    ring_bx.start(1)
    ring_az.arrive(3)
    ring_bx.arrive(1)

    def compact(plane, carry):
        rows = pl.ds(pl.multiple_of(plane * PLANE * ROW, 32), PLANE * ROW)

        def put(block, value):
            if block < 6:
                attn_out[rows, block * LANE : (block + 1) * LANE] = value
            elif block == 6:
                small_out[rows, :] = value
            else:
                target = in_out if block < 16 else out_out
                index = (block - 7) % 9
                column = (index % 3) * LANE
                target[index // 3, rows, column : column + LANE] = value

        for first_block, block_count in GROUPS:
            padded = 48 if block_count == 4 else 16
            picked = slots[plane, :, pl.ds(first_block * ROW, padded), :]
            moved = jnp.dot(
                (four if block_count == 4 else one)[...],
                picked.reshape(PLANE * padded, LANE),
                preferred_element_type=jnp.float32,
            ).astype(jnp.bfloat16)
            for block in range(block_count):
                put(
                    first_block + block,
                    moved[block * PLANE * ROW : (block + 1) * PLANE * ROW, :],
                )
        return carry

    lax.fori_loop(0, NZ, compact, 0)
    first.wait_send()
    for ring in (ring_ax, ring_bz, ring_az, ring_bx):
        ring.finish()


def vmem_specs(count):
    return [pl.BlockSpec(memory_space=pltpu.VMEM)] * count


def gather_weights(shard):
    shapes = ((768, 768), (768, LANE), (EF, 768, 384), (EF, 768, 384))
    return pl.pallas_call(
        gather_kernel,
        out_shape=[jax.ShapeDtypeStruct(shape, jnp.bfloat16) for shape in shapes],
        in_specs=vmem_specs(3),
        out_specs=vmem_specs(4),
        scratch_shapes=[
            pltpu.VMEM((NZ, PLANE, PACK, LANE), jnp.bfloat16),
            pltpu.SemaphoreType.DMA,
            pltpu.SemaphoreType.DMA((25,)),
            pltpu.SemaphoreType.DMA((25,)),
        ],
        compiler_params=pltpu.CompilerParams(
            collective_id=0, has_side_effects=True, vmem_limit_bytes=60_000_000
        ),
    )(shard, spread_matrix(4, 48), spread_matrix(1, 16))


def pack_rows(attn, small, left, right):
    flat = jnp.concatenate(
        [
            jnp.transpose(attn, (1, 0, 2)).reshape(ROW, 768),
            jnp.pad(small, ((0, 0), (0, LANE - small.shape[1]))),
            jnp.transpose(left, (1, 0, 2)).reshape(ROW, 1152),
            jnp.transpose(right, (1, 0, 2)).reshape(ROW, 1152),
        ],
        axis=1,
    )
    rows = jnp.transpose(flat.reshape(ROW, 25, LANE), (1, 0, 2)).reshape(25 * ROW, LANE)
    return jnp.pad(rows, ((0, PACK - 25 * ROW), (0, 0)))


def unpack_rows(rows):
    flat = jnp.transpose(rows[: 25 * ROW].reshape(25, ROW, LANE), (1, 0, 2)).reshape(ROW, 25 * LANE)
    attn = jnp.transpose(flat[:, :768].reshape(ROW, 4, 192), (1, 0, 2))
    small = flat[:, 768:773]
    left = jnp.transpose(flat[:, 896:2048].reshape(ROW, EF, 384), (1, 0, 2))
    right = jnp.transpose(flat[:, 2048:3200].reshape(ROW, EF, 384), (1, 0, 2))
    return attn, small, left, right


class ReduceRing:
    def __init__(self, chunk, landing, position, count, up, down, send_sems, recv_sems, base):
        self.chunk, self.landing = chunk, landing
        self.position, self.count = position, count
        self.up, self.down = up, down
        self.send_sems, self.recv_sems, self.base = send_sems, recv_sems, base
        self.copies = []

    def start(self, step):
        away = self.count // 2 - step
        pair = []
        for side, (sign, target) in enumerate(((1, self.up), (-1, self.down))):
            half = side if step == 0 else None
            part = self.chunk(wrap(self.position + sign * away, self.count), half)
            slot = self.base + 2 * step + side
            pair.append(
                send(
                    part,
                    self.landing(side, step, half),
                    self.send_sems.at[slot],
                    self.recv_sems.at[slot],
                    target,
                )
            )
        self.copies.append(pair)

    def arrive(self, step):
        for copy in self.copies[step]:
            copy.wait_recv()
        away = self.count // 2 - 1 - step
        if away == 0:
            mine = self.chunk(self.position, None)
            mine[...] = (
                mine[...].astype(jnp.float32)
                + self.landing(0, step, None)[...].astype(jnp.float32)
                + self.landing(1, step, None)[...].astype(jnp.float32)
            ).astype(jnp.bfloat16)
            return
        for side, sign in ((0, 1), (1, -1)):
            half = side if step == 0 else None
            mine = self.chunk(wrap(self.position + sign * away, self.count), half)
            mine[...] = (
                mine[...].astype(jnp.float32)
                + self.landing(side, step, half)[...].astype(jnp.float32)
            ).astype(jnp.bfloat16)

    def finish(self):
        for pair in self.copies:
            for copy in pair:
                copy.wait_send()


def reduce_kernel(
    attn, small, left, right, four, one, total,
    slots, land_az, land_bx, land_ax, land_bz, land_y, send_sems, recv_sems,
):
    me = lax.axis_index("dp")
    z, x, y = place_of(me)
    up_z, down_z, up_x, down_x, other_y = neighbours(me)
    greet((up_z, down_z, up_x, down_x, other_y), 5)

    def expand(plane, carry):
        rows = pl.ds(pl.multiple_of(plane * PLANE * ROW, 32), PLANE * ROW)

        def get(block):
            if block < 6:
                return attn[rows, block * LANE : (block + 1) * LANE]
            if block == 6:
                return small[rows, :]
            source = left if block < 16 else right
            index = (block - 7) % 9
            column = (index % 3) * LANE
            return source[index // 3, rows, column : column + LANE]

        for first_block, block_count in GROUPS:
            padded = 48 if block_count == 4 else 16
            stacked = [get(first_block + block) for block in range(block_count)]
            moved = jnp.dot(
                (four if block_count == 4 else one)[...],
                stacked[0] if block_count == 1 else jnp.concatenate(stacked, axis=0),
                preferred_element_type=jnp.float32,
            ).astype(jnp.bfloat16)
            slots[plane, :, pl.ds(first_block * ROW, padded), :] = moved.reshape(
                PLANE, padded, LANE
            )
        return carry

    lax.fori_loop(0, NZ, expand, 0)
    rest = pl.ds(SPLIT, PACK - SPLIT)
    head = pl.ds(0, SPLIT)

    def part_az(index, half):
        if half is None:
            return slots.at[index, pl.ds(0, PLANE), head]
        return slots.at[index, pl.ds(half * (PLANE // 2), PLANE // 2), head]

    def land_of_az(side, step, half):
        if half is None:
            return land_az.at[side, step]
        return land_az.at[side, step, pl.ds(half * (PLANE // 2), PLANE // 2)]

    def part_bx(index, half):
        if half is None:
            return slots.at[pl.ds(0, NZ), pl.ds(NY * index, NY), rest]
        return slots.at[pl.ds(half * (NZ // 2), NZ // 2), pl.ds(NY * index, NY), rest]

    def land_of_bx(side, step, half):
        if half is None:
            return land_bx.at[side, step]
        return land_bx.at[side, step, pl.ds(half * (NZ // 2), NZ // 2)]

    def part_ax(index, half):
        if half is None:
            return slots.at[z, pl.ds(NY * index, NY), head]
        return slots.at[z, pl.ds(NY * index + half, 1), head]

    def land_of_ax(side, step, half):
        if half is None:
            return land_ax.at[side, step]
        return land_ax.at[side, step, pl.ds(half, 1)]

    def part_bz(index, half):
        if half is None:
            return slots.at[index, pl.ds(NY * x, NY), rest]
        return slots.at[index, pl.ds(NY * x + half, 1), rest]

    def land_of_bz(side, step, half):
        if half is None:
            return land_bz.at[side, step]
        return land_bz.at[side, step, pl.ds(half, 1)]

    ring_az = ReduceRing(part_az, land_of_az, z, NZ, up_z, down_z, send_sems, recv_sems, 1)
    ring_bx = ReduceRing(part_bx, land_of_bx, x, NX, up_x, down_x, send_sems, recv_sems, 9)
    ring_ax = ReduceRing(part_ax, land_of_ax, x, NX, up_x, down_x, send_sems, recv_sems, 13)
    ring_bz = ReduceRing(part_bz, land_of_bz, z, NZ, up_z, down_z, send_sems, recv_sems, 17)
    ring_az.start(0)
    ring_bx.start(0)
    ring_az.arrive(0)
    ring_az.start(1)
    ring_bx.arrive(0)
    ring_bx.start(1)
    ring_az.arrive(1)
    ring_az.start(2)
    ring_az.arrive(2)
    ring_az.start(3)
    ring_bx.arrive(1)
    ring_bz.start(0)
    ring_bz.arrive(0)
    ring_bz.start(1)
    ring_az.arrive(3)
    ring_ax.start(0)
    ring_bz.arrive(1)
    ring_bz.start(2)
    ring_ax.arrive(0)
    ring_ax.start(1)
    ring_bz.arrive(2)
    ring_bz.start(3)
    ring_ax.arrive(1)
    ring_bz.arrive(3)
    last = send(
        slots.at[z, NY * x + 1 - y], land_y, send_sems.at[0], recv_sems.at[0], other_y
    )
    last.wait_recv()
    total[...] = slots[z, NY * x + y].astype(jnp.float32) + land_y[...].astype(jnp.float32)
    last.wait_send()
    for ring in (ring_az, ring_bx, ring_ax, ring_bz):
        ring.finish()


def reduce_grads(attn, small, left, right):
    return pl.pallas_call(
        reduce_kernel,
        out_shape=jax.ShapeDtypeStruct((PACK, LANE), jnp.float32),
        in_specs=vmem_specs(6),
        out_specs=pl.BlockSpec(memory_space=pltpu.VMEM),
        scratch_shapes=[
            pltpu.VMEM((NZ, PLANE, PACK, LANE), jnp.bfloat16),
            pltpu.VMEM((2, 4, PLANE, SPLIT, LANE), jnp.bfloat16),
            pltpu.VMEM((2, 2, NZ, NY, PACK - SPLIT, LANE), jnp.bfloat16),
            pltpu.VMEM((2, 2, NY, SPLIT, LANE), jnp.bfloat16),
            pltpu.VMEM((2, 4, NY, PACK - SPLIT, LANE), jnp.bfloat16),
            pltpu.VMEM((PACK, LANE), jnp.bfloat16),
            pltpu.SemaphoreType.DMA((25,)),
            pltpu.SemaphoreType.DMA((25,)),
        ],
        compiler_params=pltpu.CompilerParams(
            collective_id=1, has_side_effects=True, vmem_limit_bytes=60_000_000
        ),
    )(attn, small, left, right, spread_matrix(4, 48).T, spread_matrix(1, 16).T)


def muon_kernel(
    look, narrow, wide, mask_ref, result,
    arrived, matrix, finished, gram, local_sems, send_sems, recv_sem, back_sem, ret_sems,
):
    me = lax.axis_index("dp")
    shift = lax.rem(lax.axis_index("tensor"), 2) * 4

    def owner_of(block):
        return block * PLANE + shift

    own = lax.rem(me, PLANE) == shift
    my_block = me // PLANE
    barrier = pltpu.get_barrier_semaphore()
    devices = NZ * PLANE

    def hail(target):
        pl.semaphore_signal(barrier, inc=1, device_id={"dp": target}, device_id_type=MESH_ID)

    for block in range(BLOCKS):

        @pl.when(me != owner_of(block))
        def _():
            hail(owner_of(block))

    @pl.when(own)
    def _():
        def hail_one(target, carry):
            @pl.when(target != me)
            def _():
                hail(target)

            return carry

        lax.fori_loop(0, devices, hail_one, 0)
        pl.semaphore_wait(barrier, BLOCKS - 1 + devices - 1)

    @pl.when(jnp.logical_not(own))
    def _():
        pl.semaphore_wait(barrier, BLOCKS)

    def outgoing(block):
        return pltpu.make_async_remote_copy(
            src_ref=look.at[block],
            dst_ref=arrived.at[me],
            send_sem=send_sems.at[block],
            recv_sem=recv_sem,
            device_id={"dp": owner_of(block)},
            device_id_type=MESH_ID,
        )

    for block in range(BLOCKS):

        @pl.when(me != owner_of(block))
        def _():
            outgoing(block).start()

    @pl.when(own)
    def _():
        keep = pltpu.make_async_copy(look.at[my_block], arrived.at[me], local_sems.at[0])
        keep.start()
        keep.wait()
        pltpu.make_async_remote_copy(
            src_ref=arrived.at[pl.ds(0, devices - 1)],
            dst_ref=arrived.at[pl.ds(0, devices - 1)],
            send_sem=back_sem,
            recv_sem=recv_sem,
            device_id={"dp": me},
            device_id_type=MESH_ID,
        ).wait_recv()

        def compact(plane, carry):
            picked = arrived[pl.ds(plane * PLANE, PLANE)].reshape(PLANE * 16, 384)
            rows = pl.ds(pl.multiple_of(plane * PLANE * ROW, 32), PLANE * ROW)
            matrix[rows, :] = jnp.dot(
                narrow[...], picked, preferred_element_type=jnp.float32
            ).astype(jnp.bfloat16)
            return carry

        lax.fori_loop(0, NZ, compact, 0)
        joined = my_block >= 2
        mask = jnp.maximum(mask_ref[...], joined.astype(jnp.float32))
        raw = matrix[...].astype(jnp.float32)
        per_col = jnp.sum(raw * raw, axis=0, keepdims=True)
        square_sum = jnp.dot(
            jnp.broadcast_to(per_col, (8, 384)), mask, preferred_element_type=jnp.float32,
            precision=lax.Precision.HIGHEST,
        )[0:1]
        matrix[...] = (raw * lax.rsqrt(square_sum + EPSILON)).astype(jnp.bfloat16)
        for _ in range(NS_ITERS):
            current = matrix[...]
            gram_mat = (contract_rows(current, current) * mask).astype(jnp.bfloat16)
            square = jnp.dot(gram_mat, gram_mat, preferred_element_type=jnp.float32)
            gram[...] = (
                NEWTON_B * gram_mat.astype(jnp.float32) + NEWTON_C * square
            ).astype(jnp.bfloat16)
            matrix[...] = (
                NEWTON_A * current.astype(jnp.float32)
                + jnp.dot(current, gram[...], preferred_element_type=jnp.float32)
            ).astype(jnp.bfloat16)

        def expand(plane, carry):
            rows = pl.ds(pl.multiple_of(plane * PLANE * ROW, 32), PLANE * ROW)
            finished[pl.ds(plane * PLANE, PLANE)] = (
                jnp.dot(wide[...], matrix[rows, :], preferred_element_type=jnp.float32)
                .astype(jnp.bfloat16)
                .reshape(PLANE, 16, 384)
            )
            return carry

        lax.fori_loop(0, NZ, expand, 0)

        def give(target, carry):
            @pl.when(target != me)
            def _():
                pltpu.make_async_remote_copy(
                    src_ref=finished.at[target],
                    dst_ref=result.at[my_block],
                    send_sem=back_sem,
                    recv_sem=ret_sems.at[my_block],
                    device_id={"dp": target},
                    device_id_type=MESH_ID,
                ).start()

            return carry

        lax.fori_loop(0, devices, give, 0)
        stay = pltpu.make_async_copy(finished.at[me], result.at[my_block], local_sems.at[1])
        stay.start()
        stay.wait()
        pltpu.make_async_remote_copy(
            src_ref=finished.at[pl.ds(0, devices - 1)],
            dst_ref=finished.at[pl.ds(0, devices - 1)],
            send_sem=back_sem,
            recv_sem=recv_sem,
            device_id={"dp": me},
            device_id_type=MESH_ID,
        ).wait_send()

    for block in range(BLOCKS):

        @pl.when(me != owner_of(block))
        def _():
            outgoing(block).wait_send()
            pltpu.make_async_remote_copy(
                src_ref=result.at[block],
                dst_ref=result.at[block],
                send_sem=send_sems.at[block],
                recv_sem=ret_sems.at[block],
                device_id={"dp": owner_of(block)},
                device_id_type=MESH_ID,
            ).wait_recv()


def half_mask():
    side = np.arange(384) // 192
    return jnp.asarray(side[:, None] == side[None, :], jnp.float32)


def muon_step(look):
    return pl.pallas_call(
        muon_kernel,
        out_shape=jax.ShapeDtypeStruct((BLOCKS, 16, 384), jnp.bfloat16),
        in_specs=vmem_specs(4),
        out_specs=pl.BlockSpec(memory_space=pltpu.VMEM),
        scratch_shapes=[
            pltpu.VMEM((NZ * PLANE, 16, 384), jnp.bfloat16),
            pltpu.VMEM((768, 384), jnp.bfloat16),
            pltpu.VMEM((NZ * PLANE, 16, 384), jnp.bfloat16),
            pltpu.VMEM((384, 384), jnp.bfloat16),
            pltpu.SemaphoreType.DMA((2,)),
            pltpu.SemaphoreType.DMA((BLOCKS,)),
            pltpu.SemaphoreType.DMA,
            pltpu.SemaphoreType.DMA,
            pltpu.SemaphoreType.DMA((BLOCKS,)),
        ],
        compiler_params=pltpu.CompilerParams(
            collective_id=2, has_side_effects=True, vmem_limit_bytes=60_000_000
        ),
    )(look, spread_matrix(1, 16), spread_matrix(1, 16).T, half_mask())


def pack_blocks(attn, left, right):
    pairs = jnp.transpose(
        jnp.transpose(attn, (1, 0, 2)).reshape(ROW, 2, 384), (1, 0, 2)
    )
    stacked = jnp.concatenate([pairs, left, right], axis=0)
    return jnp.pad(stacked, ((0, 0), (0, 16 - ROW), (0, 0)))


def norm_forward(row_data, gain_row):
    center = row_data - jnp.mean(row_data, axis=-1, keepdims=True)
    inv_std = lax.rsqrt(jnp.mean(center * center, axis=-1, keepdims=True) + EPSILON)
    normal = center * inv_std
    return (normal, inv_std, round_half(normal * gain_row))


def norm_backward(grad_result, normal, inv_std, gain_row):
    scaled = grad_result * gain_row
    grad_data = inv_std * (
        scaled
        - jnp.mean(scaled, axis=-1, keepdims=True)
        - normal * jnp.mean(scaled * normal, axis=-1, keepdims=True)
    )
    return (grad_data, jnp.sum(grad_result * normal, axis=0))


def gelu_value(pre_act):
    return 0.5 * pre_act * (1.0 + lax.erf(pre_act * ROOT_HALF))


def gelu_slope(pre_act):
    return 0.5 * (1.0 + lax.erf(pre_act * ROOT_HALF)) + pre_act * INV_ROOT_TAU * jnp.exp(
        -0.5 * pre_act * pre_act
    )


def score_table(queries, key_rows):
    return jnp.einsum("bqhd,bkhd->bhqk", queries, key_rows, preferred_element_type=jnp.float32) * (
        1.0 / math.sqrt(HEAD_DIM)
    )


def attention_forward(normed, mats_half, image_count, seq_len):
    head_count = mats_half.shape[2] // HEAD_DIM

    def project(which_mat):
        return round_half(
            jnp.dot(normed, mats_half[which_mat], preferred_element_type=jnp.float32)
        ).reshape(image_count, seq_len, head_count, HEAD_DIM)

    queries = project(0)
    key_rows = project(1)
    value_rows = project(2)
    scores = score_table(queries, key_rows)
    row_peak = jnp.max(scores, axis=-1, keepdims=True)
    log_total = row_peak + jnp.log(jnp.sum(jnp.exp(scores - row_peak), axis=-1, keepdims=True))
    prob_half = round_half(jnp.exp(scores - log_total))
    attn_rows = round_half(
        jnp.einsum("bhqk,bkhd->bqhd", prob_half, value_rows, preferred_element_type=jnp.float32)
    )
    return (
        queries,
        key_rows,
        value_rows,
        log_total,
        attn_rows.reshape(image_count * seq_len, head_count * HEAD_DIM),
    )


def attention_backward(grad_attn_rows, queries, key_rows, value_rows, log_total):
    image_count, seq_len, head_count, head_size = queries.shape
    grad_heads = grad_attn_rows.reshape(image_count, seq_len, head_count, head_size)
    prob_full = jnp.exp(score_table(queries, key_rows) - log_total)
    prob_half = round_half(prob_full)
    grad_prob = jnp.einsum(
        "bqhd,bkhd->bhqk", grad_heads, value_rows, preferred_element_type=jnp.float32
    )
    grad_values = round_half(
        jnp.einsum("bhqk,bqhd->bkhd", prob_half, grad_heads, preferred_element_type=jnp.float32)
    )
    spread = jnp.sum(prob_full * grad_prob, axis=-1, keepdims=True)
    grad_scores = round_half(prob_full * (grad_prob - spread) * (1.0 / math.sqrt(HEAD_DIM)))
    grad_queries = round_half(
        jnp.einsum("bhqk,bkhd->bqhd", grad_scores, key_rows, preferred_element_type=jnp.float32)
    )
    grad_keys = round_half(
        jnp.einsum("bhqk,bqhd->bkhd", grad_scores, queries, preferred_element_type=jnp.float32)
    )
    row_total = image_count * seq_len
    full_width = head_count * head_size
    return (
        grad_queries.reshape(row_total, full_width),
        grad_keys.reshape(row_total, full_width),
        grad_values.reshape(row_total, full_width),
    )


def shards(
    inputs,
    cotangent,
    norm_gains,
    attn_mats,
    router,
    expert_in,
    expert_out,
    moment_gains,
    moment_attn,
    moment_router,
    moment_in,
    moment_out,
    routes,
):
    image_count, seq_len, model_width = inputs.shape
    dp_count = lax.axis_size("dp")
    row_count = image_count * seq_len
    attn_all, small_half, in_half, out_half = gather_weights(
        pack_rows(
            round_half(attn_mats),
            jnp.concatenate([round_half(norm_gains).T, round_half(router)], axis=1),
            round_half(expert_in),
            round_half(expert_out),
        )
    )
    attn_half = jnp.stack([attn_all[:, 192 * which : 192 * which + 192] for which in range(4)])
    gains_half = small_half[:, :2].T
    router_half = small_half[:, 2 : 2 + EF]
    gain_one = to_single(gains_half[0])
    gain_two = to_single(gains_half[1])
    row_in = inputs.reshape(row_count, model_width)
    normal_one, inv_one, normed_one = norm_forward(row_in, gain_one)
    queries, key_rows, value_rows, log_total, attn_rows = attention_forward(
        normed_one, attn_half, image_count, seq_len
    )
    attn_part = contract_cols(attn_rows, attn_half[3])
    attn_full = lax.psum(attn_part.astype(jnp.bfloat16), "tensor").astype(jnp.float32)
    middle = row_in + attn_full
    normal_two, inv_two, normed_two = norm_forward(middle, gain_two)
    picked = routes.reshape(row_count, 2)
    one_hot = (picked[:, :, None] == jnp.arange(EF, dtype=jnp.int32)[None, None, :]).astype(
        jnp.float32
    )
    logits = jnp.dot(normed_two, router_half, preferred_element_type=jnp.float32)
    chosen = jnp.sum(logits[:, None, :] * one_hot, axis=2)
    gate_vals = jax.nn.sigmoid(chosen - chosen[:, ::-1])
    gate_table = jnp.sum(gate_vals[:, :, None] * one_hot, axis=1)
    grad_rows = cotangent.reshape(row_count, model_width)
    pre_act = jnp.einsum("td,edf->etf", normed_two, in_half, preferred_element_type=jnp.float32)
    hidden = round_half(gelu_value(pre_act))
    expert_rows = jnp.einsum("etf,edf->etd", hidden, out_half, preferred_element_type=jnp.float32)
    moe_part = jnp.sum(gate_table.T[:, :, None] * expert_rows, axis=0)
    moe_full = lax.psum(moe_part.astype(jnp.bfloat16), "tensor").astype(jnp.float32)
    output_rows = middle + moe_full
    grad_each = jnp.sum(grad_rows[None] * expert_rows, axis=2).T
    grad_choice_part = jnp.sum(grad_each[:, None, :] * one_hot, axis=2)
    grad_expert = round_half(gate_table.T[:, :, None] * grad_rows[None])
    grad_hidden = jnp.einsum(
        "etd,edf->etf", grad_expert, out_half, preferred_element_type=jnp.float32
    )
    grad_pre = round_half(grad_hidden * gelu_slope(pre_act))
    grad_normed_part = jnp.einsum(
        "etf,edf->td", grad_pre, in_half, preferred_element_type=jnp.float32
    )
    grad_in = jnp.einsum("td,etf->edf", normed_two, grad_pre, preferred_element_type=jnp.float32)
    grad_out = jnp.einsum("etd,etf->edf", grad_expert, hidden, preferred_element_type=jnp.float32)
    joined = lax.psum(
        jnp.concatenate([grad_normed_part, grad_choice_part], axis=1).astype(jnp.bfloat16), "tensor"
    ).astype(jnp.float32)
    grad_normed_moe, grad_choice = joined[:, :model_width], joined[:, model_width:]
    gate_prod = gate_vals[:, 0] * gate_vals[:, 1]
    grad_first = (grad_choice[:, 0] - grad_choice[:, 1]) * gate_prod
    grad_picked = jnp.stack([grad_first, -grad_first], axis=1)
    grad_logits = round_half(jnp.sum(grad_picked[:, :, None] * one_hot, axis=1))
    grad_router = contract_rows(normed_two, grad_logits)
    grad_normed_two = grad_normed_moe + contract_cols(grad_logits, router_half)
    grad_mid_norm, grad_gain_two = norm_backward(grad_normed_two, normal_two, inv_two, gain_two)
    grad_middle = grad_rows + grad_mid_norm
    grad_mid_half = round_half(grad_middle)
    grad_attn_rows = round_half(
        jnp.dot(grad_mid_half, attn_half[3], preferred_element_type=jnp.float32)
    )
    grad_proj_out = contract_rows(grad_mid_half, attn_rows)
    grad_queries, grad_keys, grad_values = attention_backward(
        grad_attn_rows, queries, key_rows, value_rows, log_total
    )
    grad_attn = jnp.concatenate(
        [
            contract_rows(normed_one, grad_queries),
            contract_rows(normed_one, grad_keys),
            contract_rows(normed_one, grad_values),
            grad_proj_out,
        ],
        axis=1,
    )
    grad_normed_one_part = (
        contract_cols(grad_queries, attn_half[0])
        + contract_cols(grad_keys, attn_half[1])
        + contract_cols(grad_values, attn_half[2])
    )
    grad_normed_one = lax.psum(grad_normed_one_part.astype(jnp.bfloat16), "tensor").astype(
        jnp.float32
    )
    grad_in_norm, grad_gain_one = norm_backward(grad_normed_one, normal_one, inv_one, gain_one)
    grad_inputs_rows = grad_middle + grad_in_norm
    gains_cols = jnp.stack([grad_gain_one, grad_gain_two], axis=1)
    small_cols = jnp.concatenate([gains_cols, grad_router], axis=1)
    small_wide = jnp.pad(round_half(small_cols), ((0, 0), (0, LANE - small_cols.shape[1])))
    sum_attn, sum_small, sum_in, sum_out = unpack_rows(
        reduce_grads(round_half(grad_attn), small_wide, round_half(grad_in), round_half(grad_out))
    )
    sum_gains = sum_small[:, :2].T
    sum_router = sum_small[:, 2:]
    small_step = SMALL_RATE / math.sqrt(image_count * dp_count * seq_len)
    moment_gains_new = MOMENTUM * moment_gains + sum_gains
    moment_attn_new = MOMENTUM * moment_attn + sum_attn
    moment_router_new = MOMENTUM * moment_router + sum_router
    moment_in_new = MOMENTUM * moment_in + sum_in
    moment_out_new = MOMENTUM * moment_out + sum_out
    gains_new = norm_gains - small_step * moment_gains_new
    router_new = router - small_step * moment_router_new
    look_attn = sum_attn + MOMENTUM * moment_attn_new
    look_in = sum_in + MOMENTUM * moment_in_new
    look_out = sum_out + MOMENTUM * moment_out_new
    updates = to_single(muon_step(pack_blocks(*map(round_half, (look_attn, look_in, look_out)))))[
        :, :ROW
    ]
    update_attn = jnp.transpose(
        jnp.transpose(updates[0:2], (1, 0, 2)).reshape(ROW, 4, 192), (1, 0, 2)
    )
    attn_new = attn_mats - MUON_RATE * update_attn
    in_new = expert_in - MUON_RATE * updates[2 : EF + 2]
    out_new = expert_out - MUON_RATE * updates[EF + 2 : 2 * EF + 2]
    output = output_rows.reshape(image_count, seq_len, model_width)
    grad_inputs = grad_inputs_rows.reshape(image_count, seq_len, model_width)
    return (
        output,
        grad_inputs,
        sum_gains,
        sum_attn,
        sum_router,
        sum_in,
        sum_out,
        gains_new,
        attn_new,
        router_new,
        in_new,
        out_new,
        moment_gains_new,
        moment_attn_new,
        moment_router_new,
        moment_in_new,
        moment_out_new,
    )


def solution(mesh):
    return jax.shard_map(
        shards,
        mesh=mesh,
        in_specs=(
            P("dp", None, None),
            P("dp", None, None),
            P(None, "dp"),
            P(None, "dp", "tensor"),
            P("dp", None),
            P(None, "dp", "tensor"),
            P(None, "dp", "tensor"),
            P(None, "dp"),
            P(None, "dp", "tensor"),
            P("dp", None),
            P(None, "dp", "tensor"),
            P(None, "dp", "tensor"),
            P("dp", None, None),
        ),
        out_specs=(
            P("dp", None, None),
            P("dp", None, None),
            P(None, "dp"),
            P(None, "dp", "tensor"),
            P("dp", None),
            P(None, "dp", "tensor"),
            P(None, "dp", "tensor"),
            P(None, "dp"),
            P(None, "dp", "tensor"),
            P("dp", None),
            P(None, "dp", "tensor"),
            P(None, "dp", "tensor"),
            P(None, "dp"),
            P(None, "dp", "tensor"),
            P("dp", None),
            P(None, "dp", "tensor"),
            P(None, "dp", "tensor"),
        ),
        check_vma=False,
    )
```

```python
import math

import jax
import jax.numpy as jnp
import numpy as np
from jax import lax
from jax.experimental import pallas as pl
from jax.experimental.pallas import tpu as pltpu
from jax.sharding import PartitionSpec as P

HEAD_DIM = 64
EF = 3
NS_ITERS = 3
CAP = 197


EPSILON = 1e-06
MOMENTUM = 0.9
MUON_RATE = 0.5
SMALL_RATE = 0.5
NEWTON_A = 3.4445
NEWTON_B = -4.775
NEWTON_C = 2.0315
ROOT_HALF = 0.7071067811865476
INV_ROOT_TAU = 0.3989422804014327


def round_half(operand):
    return operand.astype(jnp.bfloat16)


def settle(operand):
    return lax.optimization_barrier(operand.astype(jnp.bfloat16))


def to_single(operand):
    return operand.astype(jnp.float32)


def contract_rows(left_mat, right_mat):
    return lax.dot_general(
        left_mat, right_mat, (((0,), (0,)), ((), ())), preferred_element_type=jnp.float32
    )


def contract_cols(left_mat, right_mat):
    return lax.dot_general(
        left_mat, right_mat, (((1,), (1,)), ((), ())), preferred_element_type=jnp.float32
    )


NZ, NX, NY = 8, 4, 2
ROW = 12
LANE = 128
PACK = 304
SPLIT = 128
PLANE = NX * NY
BLOCKS = 8
MESH_ID = pl.DeviceIdType.MESH
GROUPS = ((0, 4), (4, 4), (8, 4), (12, 4), (16, 4), (20, 4), (24, 1))


def spread_matrix(block_count, padded):
    table = np.zeros((block_count * PLANE * ROW, PLANE * padded), np.float32)
    for block in range(block_count):
        for member in range(PLANE):
            for row in range(ROW):
                table[
                    block * PLANE * ROW + member * ROW + row, member * padded + block * ROW + row
                ] = 1.0
    return jnp.asarray(table, jnp.bfloat16)


def place_of(me):
    return me // PLANE, lax.rem(me // NY, NX), lax.rem(me, NY)


def dp_index(z, x, y):
    return z * PLANE + x * NY + y


def wrap(value, count):
    return lax.rem(value + 2 * count, count)


def neighbours(me):
    z, x, y = place_of(me)
    return (
        dp_index(wrap(z + 1, NZ), x, y),
        dp_index(wrap(z - 1, NZ), x, y),
        dp_index(z, wrap(x + 1, NX), y),
        dp_index(z, wrap(x - 1, NX), y),
        dp_index(z, x, 1 - y),
    )


def greet(targets, count):
    barrier = pltpu.get_barrier_semaphore()
    for target in targets:
        pl.semaphore_signal(barrier, inc=1, device_id={"dp": target}, device_id_type=MESH_ID)
    pl.semaphore_wait(barrier, count)


def send(source, landing, send_sem, recv_sem, target):
    copy = pltpu.make_async_remote_copy(
        src_ref=source,
        dst_ref=landing,
        send_sem=send_sem,
        recv_sem=recv_sem,
        device_id={"dp": target},
        device_id_type=MESH_ID,
    )
    copy.start()
    return copy


class GatherRing:
    def __init__(self, chunk, position, count, up, down, send_sems, recv_sems, base):
        self.chunk, self.position, self.count = chunk, position, count
        self.up, self.down = up, down
        self.send_sems, self.recv_sems, self.base = send_sems, recv_sems, base
        self.copies = []

    def start(self, step):
        half = step == self.count // 2 - 1
        pair = []
        for side, (sign, target) in enumerate(((-1, self.up), (1, self.down))):
            part = self.chunk(wrap(self.position + sign * step, self.count), side if half else None)
            slot = self.base + 2 * step + side
            pair.append(send(part, part, self.send_sems.at[slot], self.recv_sems.at[slot], target))
        self.copies.append(pair)

    def arrive(self, step):
        for copy in self.copies[step]:
            copy.wait_recv()

    def finish(self):
        for pair in self.copies:
            for copy in pair:
                copy.wait_send()


def gather_kernel(
    shard, four, one, attn_out, small_out, in_out, out_out, slots, local_sem, send_sems, recv_sems
):
    me = lax.axis_index("dp")
    z, x, y = place_of(me)
    up_z, down_z, up_x, down_x, other_y = neighbours(me)
    greet((up_z, down_z, up_x, down_x, other_y), 5)
    own = slots.at[z, NY * x + y]
    keep = pltpu.make_async_copy(shard, own, local_sem)
    keep.start()
    first = send(shard, own, send_sems.at[0], recv_sems.at[0], other_y)
    keep.wait()
    first.wait_recv()

    def part_x_small(index, half):
        if half is None:
            return slots.at[z, pl.ds(NY * index, NY), pl.ds(0, SPLIT)]
        return slots.at[z, NY * index + half, pl.ds(0, SPLIT)]

    def part_z_small(index, half):
        rest = pl.ds(SPLIT, PACK - SPLIT)
        if half is None:
            return slots.at[index, pl.ds(NY * x, NY), rest]
        return slots.at[index, NY * x + half, rest]

    def part_z_large(index, half):
        if half is None:
            return slots.at[index, pl.ds(0, PLANE), pl.ds(0, SPLIT)]
        return slots.at[index, pl.ds(half * (PLANE // 2), PLANE // 2), pl.ds(0, SPLIT)]

    def part_x_large(index, half):
        rest = pl.ds(SPLIT, PACK - SPLIT)
        if half is None:
            return slots.at[pl.ds(0, NZ), pl.ds(NY * index, NY), rest]
        return slots.at[pl.ds(half * (NZ // 2), NZ // 2), pl.ds(NY * index, NY), rest]

    ring_ax = GatherRing(part_x_small, x, NX, up_x, down_x, send_sems, recv_sems, 1)
    ring_bz = GatherRing(part_z_small, z, NZ, up_z, down_z, send_sems, recv_sems, 5)
    ring_az = GatherRing(part_z_large, z, NZ, up_z, down_z, send_sems, recv_sems, 13)
    ring_bx = GatherRing(part_x_large, x, NX, up_x, down_x, send_sems, recv_sems, 21)
    ring_ax.start(0)
    ring_bz.start(0)
    ring_ax.arrive(0)
    ring_ax.start(1)
    ring_bz.arrive(0)
    ring_bz.start(1)
    ring_ax.arrive(1)
    ring_az.start(0)
    ring_bz.arrive(1)
    ring_bz.start(2)
    ring_bz.arrive(2)
    ring_bz.start(3)
    ring_az.arrive(0)
    ring_az.start(1)
    ring_bz.arrive(3)
    ring_bx.start(0)
    ring_az.arrive(1)
    ring_az.start(2)
    ring_az.arrive(2)
    ring_az.start(3)
    ring_bx.arrive(0)
    ring_bx.start(1)
    ring_az.arrive(3)
    ring_bx.arrive(1)

    def compact(plane, carry):
        rows = pl.ds(pl.multiple_of(plane * PLANE * ROW, 32), PLANE * ROW)

        def put(block, value):
            if block < 6:
                attn_out[rows, block * LANE : (block + 1) * LANE] = value
            elif block == 6:
                small_out[rows, :] = value
            else:
                target = in_out if block < 16 else out_out
                index = (block - 7) % 9
                column = (index % 3) * LANE
                target[index // 3, rows, column : column + LANE] = value

        for first_block, block_count in GROUPS:
            padded = 48 if block_count == 4 else 16
            picked = slots[plane, :, pl.ds(first_block * ROW, padded), :]
            moved = jnp.dot(
                (four if block_count == 4 else one)[...],
                picked.reshape(PLANE * padded, LANE),
                preferred_element_type=jnp.float32,
            ).astype(jnp.bfloat16)
            for block in range(block_count):
                put(
                    first_block + block,
                    moved[block * PLANE * ROW : (block + 1) * PLANE * ROW, :],
                )
        return carry

    lax.fori_loop(0, NZ, compact, 0)
    first.wait_send()
    for ring in (ring_ax, ring_bz, ring_az, ring_bx):
        ring.finish()


def vmem_specs(count):
    return [pl.BlockSpec(memory_space=pltpu.VMEM)] * count


def gather_weights(shard):
    shapes = ((768, 768), (768, LANE), (EF, 768, 384), (EF, 768, 384))
    return pl.pallas_call(
        gather_kernel,
        out_shape=[jax.ShapeDtypeStruct(shape, jnp.bfloat16) for shape in shapes],
        in_specs=vmem_specs(3),
        out_specs=vmem_specs(4),
        scratch_shapes=[
            pltpu.VMEM((NZ, PLANE, PACK, LANE), jnp.bfloat16),
            pltpu.SemaphoreType.DMA,
            pltpu.SemaphoreType.DMA((25,)),
            pltpu.SemaphoreType.DMA((25,)),
        ],
        compiler_params=pltpu.CompilerParams(
            collective_id=0, has_side_effects=True, vmem_limit_bytes=60_000_000
        ),
    )(shard, spread_matrix(4, 48), spread_matrix(1, 16))


def pack_rows(attn, small, left, right):
    flat = jnp.concatenate(
        [
            jnp.transpose(attn, (1, 0, 2)).reshape(ROW, 768),
            jnp.pad(small, ((0, 0), (0, LANE - small.shape[1]))),
            jnp.transpose(left, (1, 0, 2)).reshape(ROW, 1152),
            jnp.transpose(right, (1, 0, 2)).reshape(ROW, 1152),
        ],
        axis=1,
    )
    rows = jnp.transpose(flat.reshape(ROW, 25, LANE), (1, 0, 2)).reshape(25 * ROW, LANE)
    return jnp.pad(rows, ((0, PACK - 25 * ROW), (0, 0)))


def unpack_rows(rows):
    flat = jnp.transpose(rows[: 25 * ROW].reshape(25, ROW, LANE), (1, 0, 2)).reshape(ROW, 25 * LANE)
    attn = jnp.transpose(flat[:, :768].reshape(ROW, 4, 192), (1, 0, 2))
    small = flat[:, 768:773]
    left = jnp.transpose(flat[:, 896:2048].reshape(ROW, EF, 384), (1, 0, 2))
    right = jnp.transpose(flat[:, 2048:3200].reshape(ROW, EF, 384), (1, 0, 2))
    return attn, small, left, right


class ReduceRing:
    def __init__(self, chunk, landing, position, count, up, down, send_sems, recv_sems, base):
        self.chunk, self.landing = chunk, landing
        self.position, self.count = position, count
        self.up, self.down = up, down
        self.send_sems, self.recv_sems, self.base = send_sems, recv_sems, base
        self.copies = []

    def start(self, step):
        away = self.count // 2 - step
        pair = []
        for side, (sign, target) in enumerate(((1, self.up), (-1, self.down))):
            half = side if step == 0 else None
            part = self.chunk(wrap(self.position + sign * away, self.count), half)
            slot = self.base + 2 * step + side
            pair.append(
                send(
                    part,
                    self.landing(side, step, half),
                    self.send_sems.at[slot],
                    self.recv_sems.at[slot],
                    target,
                )
            )
        self.copies.append(pair)

    def arrive(self, step):
        for copy in self.copies[step]:
            copy.wait_recv()
        away = self.count // 2 - 1 - step
        if away == 0:
            mine = self.chunk(self.position, None)
            mine[...] = (
                mine[...].astype(jnp.float32)
                + self.landing(0, step, None)[...].astype(jnp.float32)
                + self.landing(1, step, None)[...].astype(jnp.float32)
            ).astype(jnp.bfloat16)
            return
        for side, sign in ((0, 1), (1, -1)):
            half = side if step == 0 else None
            mine = self.chunk(wrap(self.position + sign * away, self.count), half)
            mine[...] = (
                mine[...].astype(jnp.float32)
                + self.landing(side, step, half)[...].astype(jnp.float32)
            ).astype(jnp.bfloat16)

    def finish(self):
        for pair in self.copies:
            for copy in pair:
                copy.wait_send()


def reduce_kernel(
    attn, small, left, right, four, one, total,
    slots, land_az, land_bx, land_ax, land_bz, land_y, send_sems, recv_sems,
):
    me = lax.axis_index("dp")
    z, x, y = place_of(me)
    up_z, down_z, up_x, down_x, other_y = neighbours(me)
    greet((up_z, down_z, up_x, down_x, other_y), 5)

    def expand(plane, carry):
        rows = pl.ds(pl.multiple_of(plane * PLANE * ROW, 32), PLANE * ROW)

        def get(block):
            if block < 6:
                return attn[rows, block * LANE : (block + 1) * LANE]
            if block == 6:
                return small[rows, :]
            source = left if block < 16 else right
            index = (block - 7) % 9
            column = (index % 3) * LANE
            return source[index // 3, rows, column : column + LANE]

        for first_block, block_count in GROUPS:
            padded = 48 if block_count == 4 else 16
            stacked = [get(first_block + block) for block in range(block_count)]
            moved = jnp.dot(
                (four if block_count == 4 else one)[...],
                stacked[0] if block_count == 1 else jnp.concatenate(stacked, axis=0),
                preferred_element_type=jnp.float32,
            ).astype(jnp.bfloat16)
            slots[plane, :, pl.ds(first_block * ROW, padded), :] = moved.reshape(
                PLANE, padded, LANE
            )
        return carry

    lax.fori_loop(0, NZ, expand, 0)
    rest = pl.ds(SPLIT, PACK - SPLIT)
    head = pl.ds(0, SPLIT)

    def part_az(index, half):
        if half is None:
            return slots.at[index, pl.ds(0, PLANE), head]
        return slots.at[index, pl.ds(half * (PLANE // 2), PLANE // 2), head]

    def land_of_az(side, step, half):
        if half is None:
            return land_az.at[side, step]
        return land_az.at[side, step, pl.ds(half * (PLANE // 2), PLANE // 2)]

    def part_bx(index, half):
        if half is None:
            return slots.at[pl.ds(0, NZ), pl.ds(NY * index, NY), rest]
        return slots.at[pl.ds(half * (NZ // 2), NZ // 2), pl.ds(NY * index, NY), rest]

    def land_of_bx(side, step, half):
        if half is None:
            return land_bx.at[side, step]
        return land_bx.at[side, step, pl.ds(half * (NZ // 2), NZ // 2)]

    def part_ax(index, half):
        if half is None:
            return slots.at[z, pl.ds(NY * index, NY), head]
        return slots.at[z, pl.ds(NY * index + half, 1), head]

    def land_of_ax(side, step, half):
        if half is None:
            return land_ax.at[side, step]
        return land_ax.at[side, step, pl.ds(half, 1)]

    def part_bz(index, half):
        if half is None:
            return slots.at[index, pl.ds(NY * x, NY), rest]
        return slots.at[index, pl.ds(NY * x + half, 1), rest]

    def land_of_bz(side, step, half):
        if half is None:
            return land_bz.at[side, step]
        return land_bz.at[side, step, pl.ds(half, 1)]

    ring_az = ReduceRing(part_az, land_of_az, z, NZ, up_z, down_z, send_sems, recv_sems, 1)
    ring_bx = ReduceRing(part_bx, land_of_bx, x, NX, up_x, down_x, send_sems, recv_sems, 9)
    ring_ax = ReduceRing(part_ax, land_of_ax, x, NX, up_x, down_x, send_sems, recv_sems, 13)
    ring_bz = ReduceRing(part_bz, land_of_bz, z, NZ, up_z, down_z, send_sems, recv_sems, 17)
    ring_az.start(0)
    ring_bx.start(0)
    ring_az.arrive(0)
    ring_az.start(1)
    ring_bx.arrive(0)
    ring_bx.start(1)
    ring_az.arrive(1)
    ring_az.start(2)
    ring_az.arrive(2)
    ring_az.start(3)
    ring_bx.arrive(1)
    ring_bz.start(0)
    ring_bz.arrive(0)
    ring_bz.start(1)
    ring_az.arrive(3)
    ring_ax.start(0)
    ring_bz.arrive(1)
    ring_bz.start(2)
    ring_ax.arrive(0)
    ring_ax.start(1)
    ring_bz.arrive(2)
    ring_bz.start(3)
    ring_ax.arrive(1)
    ring_bz.arrive(3)
    last = send(
        slots.at[z, NY * x + 1 - y], land_y, send_sems.at[0], recv_sems.at[0], other_y
    )
    last.wait_recv()
    total[...] = slots[z, NY * x + y].astype(jnp.float32) + land_y[...].astype(jnp.float32)
    last.wait_send()
    for ring in (ring_az, ring_bx, ring_ax, ring_bz):
        ring.finish()


def reduce_grads(attn, small, left, right):
    return pl.pallas_call(
        reduce_kernel,
        out_shape=jax.ShapeDtypeStruct((PACK, LANE), jnp.float32),
        in_specs=vmem_specs(6),
        out_specs=pl.BlockSpec(memory_space=pltpu.VMEM),
        scratch_shapes=[
            pltpu.VMEM((NZ, PLANE, PACK, LANE), jnp.bfloat16),
            pltpu.VMEM((2, 4, PLANE, SPLIT, LANE), jnp.bfloat16),
            pltpu.VMEM((2, 2, NZ, NY, PACK - SPLIT, LANE), jnp.bfloat16),
            pltpu.VMEM((2, 2, NY, SPLIT, LANE), jnp.bfloat16),
            pltpu.VMEM((2, 4, NY, PACK - SPLIT, LANE), jnp.bfloat16),
            pltpu.VMEM((PACK, LANE), jnp.bfloat16),
            pltpu.SemaphoreType.DMA((25,)),
            pltpu.SemaphoreType.DMA((25,)),
        ],
        compiler_params=pltpu.CompilerParams(
            collective_id=1, has_side_effects=True, vmem_limit_bytes=60_000_000
        ),
    )(attn, small, left, right, spread_matrix(4, 48).T, spread_matrix(1, 16).T)


def muon_kernel(
    look, narrow, wide, mask_ref, result,
    arrived, matrix, finished, gram, local_sems, send_sems, recv_sem, back_sem, ret_sems,
):
    me = lax.axis_index("dp")
    shift = lax.rem(lax.axis_index("tensor"), 2) * 4

    def owner_of(block):
        return block * PLANE + shift

    own = lax.rem(me, PLANE) == shift
    my_block = me // PLANE
    barrier = pltpu.get_barrier_semaphore()
    devices = NZ * PLANE

    def hail(target):
        pl.semaphore_signal(barrier, inc=1, device_id={"dp": target}, device_id_type=MESH_ID)

    for block in range(BLOCKS):

        @pl.when(me != owner_of(block))
        def _():
            hail(owner_of(block))

    @pl.when(own)
    def _():
        def hail_one(target, carry):
            @pl.when(target != me)
            def _():
                hail(target)

            return carry

        lax.fori_loop(0, devices, hail_one, 0)
        pl.semaphore_wait(barrier, BLOCKS - 1 + devices - 1)

    @pl.when(jnp.logical_not(own))
    def _():
        pl.semaphore_wait(barrier, BLOCKS)

    def outgoing(block):
        return pltpu.make_async_remote_copy(
            src_ref=look.at[block],
            dst_ref=arrived.at[me],
            send_sem=send_sems.at[block],
            recv_sem=recv_sem,
            device_id={"dp": owner_of(block)},
            device_id_type=MESH_ID,
        )

    for block in range(BLOCKS):

        @pl.when(me != owner_of(block))
        def _():
            outgoing(block).start()

    @pl.when(own)
    def _():
        keep = pltpu.make_async_copy(look.at[my_block], arrived.at[me], local_sems.at[0])
        keep.start()
        keep.wait()
        pltpu.make_async_remote_copy(
            src_ref=arrived.at[pl.ds(0, devices - 1)],
            dst_ref=arrived.at[pl.ds(0, devices - 1)],
            send_sem=back_sem,
            recv_sem=recv_sem,
            device_id={"dp": me},
            device_id_type=MESH_ID,
        ).wait_recv()

        def compact(plane, carry):
            picked = arrived[pl.ds(plane * PLANE, PLANE)].reshape(PLANE * 16, 384)
            rows = pl.ds(pl.multiple_of(plane * PLANE * ROW, 32), PLANE * ROW)
            matrix[rows, :] = jnp.dot(
                narrow[...], picked, preferred_element_type=jnp.float32
            ).astype(jnp.bfloat16)
            return carry

        lax.fori_loop(0, NZ, compact, 0)
        joined = my_block >= 2
        mask = jnp.maximum(mask_ref[...], joined.astype(jnp.float32))
        raw = matrix[...].astype(jnp.float32)
        per_col = jnp.sum(raw * raw, axis=0, keepdims=True)
        square_sum = jnp.dot(
            jnp.broadcast_to(per_col, (8, 384)), mask, preferred_element_type=jnp.float32,
            precision=lax.Precision.HIGHEST,
        )[0:1]
        matrix[...] = (raw * lax.rsqrt(square_sum + EPSILON)).astype(jnp.bfloat16)
        for _ in range(NS_ITERS):
            current = matrix[...]
            gram_mat = (contract_rows(current, current) * mask).astype(jnp.bfloat16)
            square = jnp.dot(gram_mat, gram_mat, preferred_element_type=jnp.float32)
            gram[...] = (
                NEWTON_B * gram_mat.astype(jnp.float32) + NEWTON_C * square
            ).astype(jnp.bfloat16)
            matrix[...] = (
                NEWTON_A * current.astype(jnp.float32)
                + jnp.dot(current, gram[...], preferred_element_type=jnp.float32)
            ).astype(jnp.bfloat16)

        def expand(plane, carry):
            rows = pl.ds(pl.multiple_of(plane * PLANE * ROW, 32), PLANE * ROW)
            finished[pl.ds(plane * PLANE, PLANE)] = (
                jnp.dot(wide[...], matrix[rows, :], preferred_element_type=jnp.float32)
                .astype(jnp.bfloat16)
                .reshape(PLANE, 16, 384)
            )
            return carry

        lax.fori_loop(0, NZ, expand, 0)

        def give(target, carry):
            @pl.when(target != me)
            def _():
                pltpu.make_async_remote_copy(
                    src_ref=finished.at[target],
                    dst_ref=result.at[my_block],
                    send_sem=back_sem,
                    recv_sem=ret_sems.at[my_block],
                    device_id={"dp": target},
                    device_id_type=MESH_ID,
                ).start()

            return carry

        lax.fori_loop(0, devices, give, 0)
        stay = pltpu.make_async_copy(finished.at[me], result.at[my_block], local_sems.at[1])
        stay.start()
        stay.wait()
        pltpu.make_async_remote_copy(
            src_ref=finished.at[pl.ds(0, devices - 1)],
            dst_ref=finished.at[pl.ds(0, devices - 1)],
            send_sem=back_sem,
            recv_sem=recv_sem,
            device_id={"dp": me},
            device_id_type=MESH_ID,
        ).wait_send()

    for block in range(BLOCKS):

        @pl.when(me != owner_of(block))
        def _():
            outgoing(block).wait_send()
            pltpu.make_async_remote_copy(
                src_ref=result.at[block],
                dst_ref=result.at[block],
                send_sem=send_sems.at[block],
                recv_sem=ret_sems.at[block],
                device_id={"dp": owner_of(block)},
                device_id_type=MESH_ID,
            ).wait_recv()


def half_mask():
    side = np.arange(384) // 192
    return jnp.asarray(side[:, None] == side[None, :], jnp.float32)


def muon_step(look):
    return pl.pallas_call(
        muon_kernel,
        out_shape=jax.ShapeDtypeStruct((BLOCKS, 16, 384), jnp.bfloat16),
        in_specs=vmem_specs(4),
        out_specs=pl.BlockSpec(memory_space=pltpu.VMEM),
        scratch_shapes=[
            pltpu.VMEM((NZ * PLANE, 16, 384), jnp.bfloat16),
            pltpu.VMEM((768, 384), jnp.bfloat16),
            pltpu.VMEM((NZ * PLANE, 16, 384), jnp.bfloat16),
            pltpu.VMEM((384, 384), jnp.bfloat16),
            pltpu.SemaphoreType.DMA((2,)),
            pltpu.SemaphoreType.DMA((BLOCKS,)),
            pltpu.SemaphoreType.DMA,
            pltpu.SemaphoreType.DMA,
            pltpu.SemaphoreType.DMA((BLOCKS,)),
        ],
        compiler_params=pltpu.CompilerParams(
            collective_id=2, has_side_effects=True, vmem_limit_bytes=60_000_000
        ),
    )(look, spread_matrix(1, 16), spread_matrix(1, 16).T, half_mask())


def pack_blocks(attn, left, right):
    pairs = jnp.transpose(
        jnp.transpose(attn, (1, 0, 2)).reshape(ROW, 2, 384), (1, 0, 2)
    )
    stacked = jnp.concatenate([pairs, left, right], axis=0)
    return jnp.pad(stacked, ((0, 0), (0, 16 - ROW), (0, 0)))


TOKENS = 197
PAD = 208
WIDE = 768
HALF = 384
ERF_TOP = (
    0.00022905065861350646, 0.0034082910107109506, 0.050955695062380861,
    0.18520832239976145, 1.128379143519084,
)
ERF_BOTTOM = (
    -1.1791602954361697e-7, 0.000023547966471313185, 0.0010179625278914885,
    0.014070470171167667, 0.11098505178285362, 0.49746925110067538, 1.0,
)


def rows_dot(left_mat, right_mat):
    return jnp.dot(left_mat, right_mat, preferred_element_type=jnp.float32)


def mean_of(value):
    return jnp.sum(value, axis=-1, keepdims=True) * (1.0 / WIDE)


def norm_parts(row_data):
    center = row_data - mean_of(row_data)
    inv_std = lax.rsqrt(mean_of(center * center) + EPSILON)
    return center * inv_std, inv_std


def norm_pull(grad_result, normal, inv_std, gain_row):
    scaled = grad_result * gain_row
    return inv_std * (scaled - mean_of(scaled) - normal * mean_of(scaled * normal))


class TensorSum:
    def __init__(self, part, land_core, land_chip, final, send_sems, recv_sems, base):
        self.part, self.land_core, self.land_chip, self.final = part, land_core, land_chip, final
        self.send_sems, self.recv_sems, self.base = send_sems, recv_sems, base
        mine = lax.axis_index("tensor")
        self.core = lax.rem(mine, 2)
        self.other_core = mine + 1 - 2 * self.core
        self.other_chip = lax.rem(mine + 2, 4)
        self.copies = []

    def put(self, source, landing, target):
        slot = self.base + len(self.copies)
        copy = pltpu.make_async_remote_copy(
            src_ref=source,
            dst_ref=landing,
            send_sem=self.send_sems.at[slot],
            recv_sem=self.recv_sems.at[slot],
            device_id={"tensor": target},
            device_id_type=MESH_ID,
        )
        copy.start()
        self.copies.append(copy)

    def begin(self):
        self.put(self.part.at[1 - self.core], self.land_core, self.other_core)

    def across(self):
        self.copies[0].wait_recv()
        mine = self.part.at[self.core]
        mine[...] = (
            mine[...].astype(jnp.float32) + self.land_core[...].astype(jnp.float32)
        ).astype(jnp.bfloat16)
        self.put(mine, self.land_chip, self.other_chip)

    def share(self):
        self.copies[1].wait_recv()
        mine = self.final.at[self.core]
        mine[...] = (
            self.part[self.core].astype(jnp.float32) + self.land_chip[...].astype(jnp.float32)
        ).astype(jnp.bfloat16)
        self.put(mine, mine, self.other_core)

    def done(self):
        self.copies[2].wait_recv()

    def value(self):
        return jnp.concatenate(
            [self.final[0][:, :HALF], self.final[1][:, :HALF]], axis=1
        ).astype(jnp.float32)

    def finish(self):
        for copy in self.copies:
            copy.wait_send()


def main_kernel(
    inputs, cotangent, routes, attn_half, small_half, in_half, out_half,
    output, grad_inputs, grad_attn, grad_small, grad_in, grad_out,
    rows_in, rows_cot, prob_all, hidden_all, grad_pre_all,
    part_a, part_b, part_c, part_d, core_a, core_b, core_c, core_d,
    chip_a, chip_b, chip_c, chip_d, final_a, final_b, final_c, final_d,
    send_sems, recv_sems,
):
    mine = lax.axis_index("tensor")
    barrier = pltpu.get_barrier_semaphore()
    for target in (mine + 1 - 2 * lax.rem(mine, 2), lax.rem(mine + 2, 4)):
        pl.semaphore_signal(barrier, inc=1, device_id={"tensor": target}, device_id_type=MESH_ID)
    pl.semaphore_wait(barrier, 2)

    sum_attn = TensorSum(part_a, core_a, chip_a, final_a, send_sems, recv_sems, 0)
    sum_grad = TensorSum(part_b, core_b, chip_b, final_b, send_sems, recv_sems, 3)
    sum_moe = TensorSum(part_c, core_c, chip_c, final_c, send_sems, recv_sems, 6)
    sum_first = TensorSum(part_d, core_d, chip_d, final_d, send_sems, recv_sems, 9)

    def fill(part, value):
        part[0, :, :HALF] = value[:, :HALF].astype(jnp.bfloat16)
        part[1, :, :HALF] = value[:, HALF:].astype(jnp.bfloat16)

    for source, held in ((inputs, rows_in), (cotangent, rows_cot)):
        held[PAD - 16 : PAD, :] = jnp.zeros((16, WIDE), jnp.float32)
        held[0:TOKENS, :] = source[0]
    gain_rows = jnp.transpose(small_half[...].astype(jnp.float32))
    gain_one, gain_two = gain_rows[0:1], gain_rows[1:2]
    row_in = rows_in[...]
    normal_one, inv_one = norm_parts(row_in)
    normed_one = round_half(normal_one * gain_one)
    qkv = round_half(rows_dot(normed_one, attn_half[:, : 3 * 192]))
    row_id = lax.broadcasted_iota(jnp.int32, (PAD, PAD), 0)
    col_id = lax.broadcasted_iota(jnp.int32, (PAD, PAD), 1)
    scale = 1.0 / math.sqrt(HEAD_DIM)

    def head_of(value, which, head):
        start = which * 192 + head * HEAD_DIM
        return value[:, start : start + HEAD_DIM]

    head_rows = []
    for head in range(3):
        scores = contract_cols(head_of(qkv, 0, head), head_of(qkv, 1, head)) * scale
        scores = jnp.where(col_id < TOKENS, scores, -1e30)
        peak = jnp.max(scores, axis=-1, keepdims=True)
        log_total = peak + jnp.log(jnp.sum(jnp.exp(scores - peak), axis=-1, keepdims=True))
        prob = jnp.where(row_id < TOKENS, jnp.exp(scores - log_total), 0.0)
        prob_all[head] = prob
        head_rows.append(round_half(rows_dot(round_half(prob), head_of(qkv, 2, head))))
    blank = jnp.zeros((PAD, HEAD_DIM), jnp.bfloat16)
    attn_rows = jnp.concatenate([blank] + head_rows, axis=1)
    fill(part_a, contract_cols(attn_rows, attn_half[:, 512:768]))
    sum_attn.begin()
    sum_attn.across()
    sum_attn.share()
    sum_attn.done()
    middle = row_in + sum_attn.value()
    normal_two, inv_two = norm_parts(middle)
    normed_two = round_half(normal_two * gain_two)
    logits = rows_dot(normed_two, small_half[...])
    lane_id = lax.broadcasted_iota(jnp.int32, (TOKENS, LANE), 1) - 2
    picks = routes[0]
    gap = jnp.zeros((PAD - TOKENS, LANE), jnp.float32)

    def chosen_mask(which):
        hit = (lane_id == picks[:, which : which + 1]).astype(jnp.float32)
        return jnp.concatenate([hit, gap], axis=0)

    hot_first, hot_second = chosen_mask(0), chosen_mask(1)
    difference = jnp.sum(logits * (hot_first - hot_second), axis=-1, keepdims=True)
    gate_first = jax.nn.sigmoid(difference)
    gate_second = jax.nn.sigmoid(-difference)
    gates = gate_first * hot_first + gate_second * hot_second
    sign = hot_first - hot_second
    cot = rows_cot[...]
    moe_part = jnp.zeros((PAD, WIDE), jnp.float32)
    choice_part = jnp.zeros((PAD, 1), jnp.float32)
    grad_part = jnp.zeros((PAD, WIDE), jnp.float32)
    for expert in range(EF):
        gate = gates[:, 2 + expert : 3 + expert]
        pre_act = rows_dot(normed_two, in_half[expert])
        inner = 1.0 + erf_of(pre_act * ROOT_HALF)
        hidden = round_half(0.5 * pre_act * inner)
        slope = 0.5 * inner + pre_act * INV_ROOT_TAU * jnp.exp(-0.5 * pre_act * pre_act)
        expert_rows = contract_cols(hidden, out_half[expert])
        moe_part = moe_part + gate * expert_rows
        choice_part = choice_part + sign[:, 2 + expert : 3 + expert] * jnp.sum(
            cot * expert_rows, axis=-1, keepdims=True
        )
        grad_expert = round_half(gate * cot)
        grad_pre = round_half(rows_dot(grad_expert, out_half[expert]) * slope)
        grad_part = grad_part + contract_cols(grad_pre, in_half[expert])
        hidden_all[expert] = hidden
        grad_pre_all[expert] = grad_pre
    fill(part_b, grad_part)
    extra = lax.broadcasted_iota(jnp.int32, (PAD, LANE), 1) == 0
    part_b[0, :, HALF:] = jnp.where(extra, choice_part, 0.0).astype(jnp.bfloat16)
    part_b[1, :, HALF:] = jnp.zeros((PAD, LANE), jnp.bfloat16)
    sum_grad.begin()
    fill(part_c, moe_part)
    sum_grad.across()
    for expert in range(EF):
        grad_in[expert] = round_half(contract_rows(normed_two, grad_pre_all[expert]))
    sum_grad.share()
    for expert in range(EF):
        gate = gates[:, 2 + expert : 3 + expert]
        grad_out[expert] = round_half(contract_rows(round_half(gate * cot), hidden_all[expert]))
    sum_moe.begin()
    sum_grad.done()
    choice = final_b[0, :, HALF : HALF + 1].astype(jnp.float32)
    grad_first = choice * gate_first * gate_second
    grad_logits = round_half(grad_first * sign)
    grad_normed_two = sum_grad.value() + contract_cols(grad_logits, small_half[...])
    grad_middle = cot + norm_pull(grad_normed_two, normal_two, inv_two, gain_two)
    grad_gain_two = jnp.sum(grad_normed_two * normal_two, axis=0, keepdims=True)
    router_part = contract_rows(normed_two, grad_logits)
    grad_mid_half = round_half(grad_middle)
    grad_heads = round_half(rows_dot(grad_mid_half, attn_half[:, 512:768]))
    sum_moe.across()
    parts = [[], [], []]
    for head in range(3):
        grad_head = grad_heads[:, HEAD_DIM * (head + 1) : HEAD_DIM * (head + 2)]
        prob = prob_all[head]
        grad_prob = contract_cols(grad_head, head_of(qkv, 2, head))
        parts[2].append(round_half(contract_rows(round_half(prob), grad_head)))
        spread = jnp.sum(prob * grad_prob, axis=-1, keepdims=True)
        grad_scores = round_half(prob * (grad_prob - spread) * scale)
        parts[0].append(round_half(rows_dot(grad_scores, head_of(qkv, 1, head))))
        parts[1].append(round_half(contract_rows(grad_scores, head_of(qkv, 0, head))))
    grad_qkv = jnp.concatenate(parts[0] + parts[1] + parts[2] + [blank] * 3, axis=1)
    fill(part_d, contract_cols(grad_qkv, attn_half[...]))
    sum_first.begin()
    sum_moe.share()
    sum_first.across()
    grad_attn[:, :512] = round_half(contract_rows(normed_one, grad_qkv[:, :512]))
    grad_attn[:, 512:] = round_half(
        contract_rows(normed_one, grad_qkv[:, 512:])
        + contract_rows(grad_mid_half, attn_rows)
    )
    sum_moe.done()
    output[0] = (middle + sum_moe.value())[:TOKENS]
    sum_first.share()
    sum_first.done()
    grad_normed_one = sum_first.value()
    grad_inputs[0] = (grad_middle + norm_pull(grad_normed_one, normal_one, inv_one, gain_one))[
        :TOKENS
    ]
    grad_gain_one = jnp.sum(grad_normed_one * normal_one, axis=0, keepdims=True)
    gain_id = lax.broadcasted_iota(jnp.int32, (LANE, WIDE), 0)
    gain_block = jnp.where(
        gain_id == 0, grad_gain_one, jnp.where(gain_id == 1, grad_gain_two, 0.0)
    )
    grad_small[...] = round_half(jnp.transpose(gain_block) + router_part)
    for summing in (sum_attn, sum_grad, sum_moe, sum_first):
        summing.finish()


def erf_of(value):
    bounded = jnp.clip(value, -3.832506856900711, 3.832506856900711)
    square = bounded * bounded
    top = jnp.full_like(square, ERF_TOP[0])
    for factor in ERF_TOP[1:]:
        top = top * square + factor
    bottom = jnp.full_like(square, ERF_BOTTOM[0])
    for factor in ERF_BOTTOM[1:]:
        bottom = bottom * square + factor
    return bounded * top / bottom


def main_step(inputs, cotangent, routes, attn_half, small_half, in_half, out_half):
    half, single = jnp.bfloat16, jnp.float32
    narrow, wide = (PAD, HALF), (PAD, HALF + LANE)
    shapes = [narrow, wide, narrow, narrow]
    return pl.pallas_call(
        main_kernel,
        out_shape=[
            jax.ShapeDtypeStruct((1, TOKENS, WIDE), single),
            jax.ShapeDtypeStruct((1, TOKENS, WIDE), single),
            jax.ShapeDtypeStruct((WIDE, WIDE), half),
            jax.ShapeDtypeStruct((WIDE, LANE), half),
            jax.ShapeDtypeStruct((EF, WIDE, HALF), half),
            jax.ShapeDtypeStruct((EF, WIDE, HALF), half),
        ],
        in_specs=vmem_specs(7),
        out_specs=vmem_specs(6),
        scratch_shapes=[
            pltpu.VMEM((PAD, WIDE), single),
            pltpu.VMEM((PAD, WIDE), single),
            pltpu.VMEM((3, PAD, PAD), single),
            pltpu.VMEM((EF, PAD, HALF), half),
            pltpu.VMEM((EF, PAD, HALF), half),
        ]
        + [pltpu.VMEM((2,) + shape, half) for shape in shapes]
        + [pltpu.VMEM(shape, half) for shape in shapes]
        + [pltpu.VMEM(shape, half) for shape in shapes]
        + [pltpu.VMEM((2,) + shape, half) for shape in shapes]
        + [pltpu.SemaphoreType.DMA((12,)), pltpu.SemaphoreType.DMA((12,))],
        compiler_params=pltpu.CompilerParams(
            collective_id=3, has_side_effects=True, vmem_limit_bytes=60_000_000
        ),
    )(inputs, cotangent, routes, attn_half, small_half, in_half, out_half)


def shards(
    inputs,
    cotangent,
    norm_gains,
    attn_mats,
    router,
    expert_in,
    expert_out,
    moment_gains,
    moment_attn,
    moment_router,
    moment_in,
    moment_out,
    routes,
):
    attn_all, small_half, in_half, out_half = gather_weights(
        pack_rows(
            round_half(attn_mats),
            jnp.concatenate([round_half(norm_gains).T, round_half(router)], axis=1),
            round_half(expert_in),
            round_half(expert_out),
        )
    )
    output, grad_inputs, grad_attn, grad_small, grad_in, grad_out = main_step(
        inputs, cotangent, routes, attn_all, small_half, in_half, out_half
    )
    sum_attn, sum_small, sum_in, sum_out = unpack_rows(
        reduce_grads(grad_attn, grad_small, grad_in, grad_out)
    )
    sum_gains = sum_small[:, :2].T
    sum_router = sum_small[:, 2:]
    small_step = SMALL_RATE / math.sqrt(lax.axis_size("dp") * TOKENS)
    moment_gains_new = MOMENTUM * moment_gains + sum_gains
    moment_attn_new = MOMENTUM * moment_attn + sum_attn
    moment_router_new = MOMENTUM * moment_router + sum_router
    moment_in_new = MOMENTUM * moment_in + sum_in
    moment_out_new = MOMENTUM * moment_out + sum_out
    gains_new = norm_gains - small_step * moment_gains_new
    router_new = router - small_step * moment_router_new
    look_attn = sum_attn + MOMENTUM * moment_attn_new
    look_in = sum_in + MOMENTUM * moment_in_new
    look_out = sum_out + MOMENTUM * moment_out_new
    updates = to_single(muon_step(pack_blocks(*map(round_half, (look_attn, look_in, look_out)))))[
        :, :ROW
    ]
    update_attn = jnp.transpose(
        jnp.transpose(updates[0:2], (1, 0, 2)).reshape(ROW, 4, 192), (1, 0, 2)
    )
    attn_new = attn_mats - MUON_RATE * update_attn
    in_new = expert_in - MUON_RATE * updates[2 : EF + 2]
    out_new = expert_out - MUON_RATE * updates[EF + 2 : 2 * EF + 2]
    return (
        output,
        grad_inputs,
        sum_gains,
        sum_attn,
        sum_router,
        sum_in,
        sum_out,
        gains_new,
        attn_new,
        router_new,
        in_new,
        out_new,
        moment_gains_new,
        moment_attn_new,
        moment_router_new,
        moment_in_new,
        moment_out_new,
    )


def solution(mesh):
    return jax.shard_map(
        shards,
        mesh=mesh,
        in_specs=(
            P("dp", None, None),
            P("dp", None, None),
            P(None, "dp"),
            P(None, "dp", "tensor"),
            P("dp", None),
            P(None, "dp", "tensor"),
            P(None, "dp", "tensor"),
            P(None, "dp"),
            P(None, "dp", "tensor"),
            P("dp", None),
            P(None, "dp", "tensor"),
            P(None, "dp", "tensor"),
            P("dp", None, None),
        ),
        out_specs=(
            P("dp", None, None),
            P("dp", None, None),
            P(None, "dp"),
            P(None, "dp", "tensor"),
            P("dp", None),
            P(None, "dp", "tensor"),
            P(None, "dp", "tensor"),
            P(None, "dp"),
            P(None, "dp", "tensor"),
            P("dp", None),
            P(None, "dp", "tensor"),
            P(None, "dp", "tensor"),
            P(None, "dp"),
            P(None, "dp", "tensor"),
            P("dp", None),
            P(None, "dp", "tensor"),
            P(None, "dp", "tensor"),
        ),
        check_vma=False,
    )
```

```python
import math

import jax
import jax.numpy as jnp
import numpy as np
from jax import lax
from jax.experimental import pallas as pl
from jax.experimental.pallas import tpu as pltpu
from jax.sharding import PartitionSpec as P

HEAD_DIM = 64
EF = 3
NS_ITERS = 3
CAP = 197


EPSILON = 1e-06
MOMENTUM = 0.9
MUON_RATE = 0.5
SMALL_RATE = 0.5
NEWTON_A = 3.4445
NEWTON_B = -4.775
NEWTON_C = 2.0315
ROOT_HALF = 0.7071067811865476
INV_ROOT_TAU = 0.3989422804014327


def round_half(operand):
    return operand.astype(jnp.bfloat16)


def settle(operand):
    return lax.optimization_barrier(operand.astype(jnp.bfloat16))


def to_single(operand):
    return operand.astype(jnp.float32)


def contract_rows(left_mat, right_mat):
    return lax.dot_general(
        left_mat, right_mat, (((0,), (0,)), ((), ())), preferred_element_type=jnp.float32
    )


def contract_cols(left_mat, right_mat):
    return lax.dot_general(
        left_mat, right_mat, (((1,), (1,)), ((), ())), preferred_element_type=jnp.float32
    )


NZ, NX, NY = 8, 4, 2
ROW = 12
LANE = 128
PACK = 304
SPLIT = 144
PLANE = NX * NY
QUAD = PLANE // 2
BLOCKS = 8
MESH_ID = pl.DeviceIdType.MESH
GROUPS = ((0, 4), (4, 4), (8, 4), (12, 4), (16, 4), (20, 4), (24, 1))


def spread_matrix(block_count, padded):
    table = np.zeros((block_count * QUAD * ROW, QUAD * padded), np.float32)
    for block in range(block_count):
        for member in range(QUAD):
            for row in range(ROW):
                table[
                    block * QUAD * ROW + member * ROW + row, member * padded + block * ROW + row
                ] = 1.0
    return jnp.asarray(table, jnp.bfloat16)


def place_of(me):
    return me // PLANE, lax.rem(me // NY, NX), lax.rem(me, NY)


def dp_index(z, x, y):
    return z * PLANE + x * NY + y


def wrap(value, count):
    return lax.rem(value + 2 * count, count)


def neighbours(me):
    z, x, y = place_of(me)
    return (
        dp_index(wrap(z + 1, NZ), x, y),
        dp_index(wrap(z - 1, NZ), x, y),
        dp_index(z, wrap(x + 1, NX), y),
        dp_index(z, wrap(x - 1, NX), y),
        dp_index(z, x, 1 - y),
    )


def greet(targets, count):
    barrier = pltpu.get_barrier_semaphore()
    for target in targets:
        pl.semaphore_signal(barrier, inc=1, device_id={"dp": target}, device_id_type=MESH_ID)
    pl.semaphore_wait(barrier, count)


def send(source, landing, send_sem, recv_sem, target):
    copy = pltpu.make_async_remote_copy(
        src_ref=source,
        dst_ref=landing,
        send_sem=send_sem,
        recv_sem=recv_sem,
        device_id={"dp": target},
        device_id_type=MESH_ID,
    )
    copy.start()
    return copy


class GatherRing:
    def __init__(self, chunk, position, count, up, down, send_sems, recv_sems, base):
        self.chunk, self.position, self.count = chunk, position, count
        self.up, self.down = up, down
        self.send_sems, self.recv_sems, self.base = send_sems, recv_sems, base
        self.copies = []

    def start(self, step):
        half = step == self.count // 2 - 1
        pair = []
        for side, (sign, target) in enumerate(((-1, self.up), (1, self.down))):
            part = self.chunk(wrap(self.position + sign * step, self.count), side if half else None)
            slot = self.base + 2 * step + side
            pair.append(send(part, part, self.send_sems.at[slot], self.recv_sems.at[slot], target))
        self.copies.append(pair)

    def arrive(self, step):
        for copy in self.copies[step]:
            copy.wait_recv()

    def finish(self):
        for pair in self.copies:
            for copy in pair:
                copy.wait_send()


def run_rounds(queue):
    last = max(begin + ring.count // 2 for ring, begin in queue)
    for turn in range(last + 1):
        for ring, begin in queue:
            step = turn - begin
            if 1 <= step <= ring.count // 2:
                ring.arrive(step - 1)
            if 0 <= step < ring.count // 2:
                ring.start(step)


GATHER_SEMS = 1 + 4 * 20


def gather_kernel(
    shard, four, one, attn_out, small_out, in_out, out_out, slots, local_sem, send_sems, recv_sems
):
    me = lax.axis_index("dp")
    z, x, y = place_of(me)
    up_z, down_z, up_x, down_x, other_y = neighbours(me)
    greet((up_z, down_z, up_x, down_x, other_y), 5)
    own = slots.at[z, NY * x + y]
    keep = pltpu.make_async_copy(shard, own, local_sem)
    keep.start()
    first = send(shard, own, send_sems.at[0], recv_sems.at[0], other_y)
    keep.wait()
    first.wait_recv()

    head, rest = pl.ds(0, SPLIT), pl.ds(SPLIT, PACK - SPLIT)

    def across_x(plane, rows):
        def chunk(index, half):
            if half is None:
                return slots.at[plane, pl.ds(NY * index, NY), rows]
            return slots.at[plane, NY * index + half, rows]

        return chunk

    def across_z(column, rows):
        def chunk(index, half):
            if half is None:
                return slots.at[index, pl.ds(NY * column, NY), rows]
            return slots.at[index, NY * column + half, rows]

        return chunk

    base = iter(range(1, GATHER_SEMS, 4))

    def ring_x(plane, rows):
        return GatherRing(
            across_x(plane, rows), x, NX, up_x, down_x, send_sems, recv_sems, next(base)
        )

    def ring_z(column, rows):
        first_sem = next(base)
        next(base)
        return GatherRing(
            across_z(column, rows), z, NZ, up_z, down_z, send_sems, recv_sems, first_sem
        )

    queue = [(ring_x(z, head), 0), (ring_z(x, rest), 0), (ring_z(x, head), 0), (ring_x(z, rest), 0)]
    for away in (1, NZ - 1):
        queue.append((ring_x(wrap(z + away, NZ), rest), 1))
    for away in (1, NX - 1):
        queue.append((ring_z(wrap(x + away, NX), head), 1))
    queue.append((ring_z(wrap(x + 2, NX), head), 2))
    for away in (2, NZ - 2, 3, NZ - 3, 4):
        queue.append((ring_x(wrap(z + away, NZ), rest), min(away, NZ - away)))
    run_rounds(queue)

    def compact(plane, carry):
        rows = pl.ds(pl.multiple_of(plane * PLANE * ROW, 32), PLANE * ROW)

        def put(block, value):
            if block < 6:
                attn_out[rows, block * LANE : (block + 1) * LANE] = value
            elif block == 6:
                small_out[rows, :] = value
            else:
                target = in_out if block < 16 else out_out
                index = (block - 7) % 9
                column = (index % 3) * LANE
                target[index // 3, rows, column : column + LANE] = value

        for first_block, block_count in GROUPS:
            padded = 48 if block_count == 4 else 16
            picked = slots[plane, :, pl.ds(first_block * ROW, padded), :]
            sides = [
                picked[side * QUAD : (side + 1) * QUAD].reshape(QUAD * padded, LANE)
                for side in range(2)
            ]
            moved = jnp.dot(
                (four if block_count == 4 else one)[...],
                jnp.concatenate(sides, axis=1),
                preferred_element_type=jnp.float32,
            ).astype(jnp.bfloat16)
            for block in range(block_count):
                part = moved[block * QUAD * ROW : (block + 1) * QUAD * ROW]
                put(
                    first_block + block,
                    jnp.concatenate([part[:, :LANE], part[:, LANE:]], axis=0),
                )
        return carry

    lax.fori_loop(0, NZ, compact, 0)
    first.wait_send()
    for ring, _ in queue:
        ring.finish()


def vmem_specs(count):
    return [pl.BlockSpec(memory_space=pltpu.VMEM)] * count


def gather_weights(shard):
    shapes = ((768, 768), (768, LANE), (EF, 768, 384), (EF, 768, 384))
    return pl.pallas_call(
        gather_kernel,
        out_shape=[jax.ShapeDtypeStruct(shape, jnp.bfloat16) for shape in shapes],
        in_specs=vmem_specs(3),
        out_specs=vmem_specs(4),
        scratch_shapes=[
            pltpu.VMEM((NZ, PLANE, PACK, LANE), jnp.bfloat16),
            pltpu.SemaphoreType.DMA,
            pltpu.SemaphoreType.DMA((GATHER_SEMS,)),
            pltpu.SemaphoreType.DMA((GATHER_SEMS,)),
        ],
        compiler_params=pltpu.CompilerParams(
            collective_id=0, has_side_effects=True, vmem_limit_bytes=60_000_000
        ),
    )(shard, spread_matrix(4, 48), spread_matrix(1, 16))


def pack_rows(attn, small, left, right):
    flat = jnp.concatenate(
        [
            jnp.transpose(attn, (1, 0, 2)).reshape(ROW, 768),
            jnp.pad(small, ((0, 0), (0, LANE - small.shape[1]))),
            jnp.transpose(left, (1, 0, 2)).reshape(ROW, 1152),
            jnp.transpose(right, (1, 0, 2)).reshape(ROW, 1152),
        ],
        axis=1,
    )
    rows = jnp.transpose(flat.reshape(ROW, 25, LANE), (1, 0, 2)).reshape(25 * ROW, LANE)
    return jnp.pad(rows, ((0, PACK - 25 * ROW), (0, 0)))


def unpack_rows(rows):
    flat = jnp.transpose(rows[: 25 * ROW].reshape(25, ROW, LANE), (1, 0, 2)).reshape(ROW, 25 * LANE)
    attn = jnp.transpose(flat[:, :768].reshape(ROW, 4, 192), (1, 0, 2))
    small = flat[:, 768:773]
    left = jnp.transpose(flat[:, 896:2048].reshape(ROW, EF, 384), (1, 0, 2))
    right = jnp.transpose(flat[:, 2048:3200].reshape(ROW, EF, 384), (1, 0, 2))
    return attn, small, left, right


class ReduceRing:
    def __init__(self, chunk, landing, position, count, up, down, send_sems, recv_sems, base):
        self.chunk, self.landing = chunk, landing
        self.position, self.count = position, count
        self.up, self.down = up, down
        self.send_sems, self.recv_sems, self.base = send_sems, recv_sems, base
        self.copies = []

    def start(self, step):
        away = self.count // 2 - step
        pair = []
        for side, (sign, target) in enumerate(((1, self.up), (-1, self.down))):
            half = side if step == 0 else None
            part = self.chunk(wrap(self.position + sign * away, self.count), half)
            slot = self.base + 2 * step + side
            pair.append(
                send(
                    part,
                    self.landing(side, step, half),
                    self.send_sems.at[slot],
                    self.recv_sems.at[slot],
                    target,
                )
            )
        self.copies.append(pair)

    def arrive(self, step):
        for copy in self.copies[step]:
            copy.wait_recv()
        away = self.count // 2 - 1 - step
        if away == 0:
            mine = self.chunk(self.position, None)
            mine[...] = (
                mine[...].astype(jnp.float32)
                + self.landing(0, step, None)[...].astype(jnp.float32)
                + self.landing(1, step, None)[...].astype(jnp.float32)
            ).astype(jnp.bfloat16)
            return
        for side, sign in ((0, 1), (1, -1)):
            half = side if step == 0 else None
            mine = self.chunk(wrap(self.position + sign * away, self.count), half)
            mine[...] = (
                mine[...].astype(jnp.float32)
                + self.landing(side, step, half)[...].astype(jnp.float32)
            ).astype(jnp.bfloat16)

    def finish(self):
        for pair in self.copies:
            for copy in pair:
                copy.wait_send()


def reduce_kernel(
    attn, small, left, right, four, one, total,
    slots, land_az, land_bx, land_ax, land_bz, land_y, send_sems, recv_sems,
):
    me = lax.axis_index("dp")
    z, x, y = place_of(me)
    up_z, down_z, up_x, down_x, other_y = neighbours(me)
    greet((up_z, down_z, up_x, down_x, other_y), 5)

    def expand(plane, carry):
        rows = pl.ds(pl.multiple_of(plane * PLANE * ROW, 32), PLANE * ROW)

        def get(block):
            if block < 6:
                return attn[rows, block * LANE : (block + 1) * LANE]
            if block == 6:
                return small[rows, :]
            source = left if block < 16 else right
            index = (block - 7) % 9
            column = (index % 3) * LANE
            return source[index // 3, rows, column : column + LANE]

        for first_block, block_count in GROUPS:
            padded = 48 if block_count == 4 else 16
            stacked = []
            for block in range(block_count):
                part = get(first_block + block)
                stacked.append(
                    jnp.concatenate([part[: QUAD * ROW], part[QUAD * ROW :]], axis=1)
                )
            moved = jnp.dot(
                (four if block_count == 4 else one)[...],
                stacked[0] if block_count == 1 else jnp.concatenate(stacked, axis=0),
                preferred_element_type=jnp.float32,
            ).astype(jnp.bfloat16)
            for side in range(2):
                slots[
                    plane, side * QUAD : (side + 1) * QUAD, pl.ds(first_block * ROW, padded), :
                ] = moved[:, side * LANE : (side + 1) * LANE].reshape(QUAD, padded, LANE)
        return carry

    lax.fori_loop(0, NZ, expand, 0)
    head, rest = pl.ds(0, SPLIT), pl.ds(SPLIT, PACK - SPLIT)

    def across_x(plane, rows):
        def chunk(index, half):
            if half is None:
                return slots.at[plane, pl.ds(NY * index, NY), rows]
            return slots.at[plane, pl.ds(NY * index + half, 1), rows]

        return chunk

    def across_z(column, rows):
        def chunk(index, half):
            if half is None:
                return slots.at[index, pl.ds(NY * column, NY), rows]
            return slots.at[index, pl.ds(NY * column + half, 1), rows]

        return chunk

    def landing_in(held, which):
        def landing(side, step, half):
            if half is None:
                return held.at[which, side, step]
            return held.at[which, side, step, pl.ds(half, 1)]

        return landing

    base = iter(range(1, GATHER_SEMS, 4))

    def ring_x(plane, rows, held, which):
        return ReduceRing(
            across_x(plane, rows), landing_in(held, which), x, NX, up_x, down_x,
            send_sems, recv_sems, next(base),
        )

    def ring_z(column, rows, held, which):
        first_sem = next(base)
        next(base)
        return ReduceRing(
            across_z(column, rows), landing_in(held, which), z, NZ, up_z, down_z,
            send_sems, recv_sems, first_sem,
        )

    queue = []
    for which, away in enumerate((4, 3, NZ - 3, 2, NZ - 2, 1, NZ - 1, 0)):
        queue.append(
            (ring_x(wrap(z + away, NZ), rest, land_bx, which), 4 - min(away, NZ - away))
        )
    for which, (away, begin) in enumerate(((2, 0), (1, 1), (NX - 1, 1), (0, 2))):
        queue.append((ring_z(wrap(x + away, NX), head, land_az, which), begin))
    queue.append((ring_x(z, head, land_ax, 0), 4))
    queue.append((ring_z(x, rest, land_bz, 0), 2))
    run_rounds(queue)
    last = send(
        slots.at[z, NY * x + 1 - y], land_y, send_sems.at[0], recv_sems.at[0], other_y
    )
    last.wait_recv()
    total[...] = slots[z, NY * x + y].astype(jnp.float32) + land_y[...].astype(jnp.float32)
    last.wait_send()
    for ring, _ in queue:
        ring.finish()


def reduce_grads(attn, small, left, right):
    return pl.pallas_call(
        reduce_kernel,
        out_shape=jax.ShapeDtypeStruct((PACK, LANE), jnp.float32),
        in_specs=vmem_specs(6),
        out_specs=pl.BlockSpec(memory_space=pltpu.VMEM),
        scratch_shapes=[
            pltpu.VMEM((NZ, PLANE, PACK, LANE), jnp.bfloat16),
            pltpu.VMEM((NX, 2, 4, NY, SPLIT, LANE), jnp.bfloat16),
            pltpu.VMEM((NZ, 2, 2, NY, PACK - SPLIT, LANE), jnp.bfloat16),
            pltpu.VMEM((1, 2, 2, NY, SPLIT, LANE), jnp.bfloat16),
            pltpu.VMEM((1, 2, 4, NY, PACK - SPLIT, LANE), jnp.bfloat16),
            pltpu.VMEM((PACK, LANE), jnp.bfloat16),
            pltpu.SemaphoreType.DMA((GATHER_SEMS,)),
            pltpu.SemaphoreType.DMA((GATHER_SEMS,)),
        ],
        compiler_params=pltpu.CompilerParams(
            collective_id=1, has_side_effects=True, vmem_limit_bytes=60_000_000
        ),
    )(attn, small, left, right, spread_matrix(4, 48).T, spread_matrix(1, 16).T)


def muon_kernel(
    look, narrow, wide, mask_ref, result,
    arrived, matrix, finished, gram, local_sems, send_sems, recv_sem, back_sem, ret_sems,
):
    me = lax.axis_index("dp")
    shift = lax.rem(lax.axis_index("tensor"), 2) * 4

    def owner_of(block):
        return block * PLANE + shift

    own = lax.rem(me, PLANE) == shift
    my_block = me // PLANE
    barrier = pltpu.get_barrier_semaphore()
    devices = NZ * PLANE

    def hail(target):
        pl.semaphore_signal(barrier, inc=1, device_id={"dp": target}, device_id_type=MESH_ID)

    for block in range(BLOCKS):

        @pl.when(me != owner_of(block))
        def _():
            hail(owner_of(block))

    @pl.when(own)
    def _():
        def hail_one(target, carry):
            @pl.when(target != me)
            def _():
                hail(target)

            return carry

        lax.fori_loop(0, devices, hail_one, 0)
        pl.semaphore_wait(barrier, BLOCKS - 1 + devices - 1)

    @pl.when(jnp.logical_not(own))
    def _():
        pl.semaphore_wait(barrier, BLOCKS)

    def outgoing(block):
        return pltpu.make_async_remote_copy(
            src_ref=look.at[block],
            dst_ref=arrived.at[me],
            send_sem=send_sems.at[block],
            recv_sem=recv_sem,
            device_id={"dp": owner_of(block)},
            device_id_type=MESH_ID,
        )

    for block in range(BLOCKS):

        @pl.when(me != owner_of(block))
        def _():
            outgoing(block).start()

    @pl.when(own)
    def _():
        keep = pltpu.make_async_copy(look.at[my_block], arrived.at[me], local_sems.at[0])
        keep.start()
        keep.wait()
        pltpu.make_async_remote_copy(
            src_ref=arrived.at[pl.ds(0, devices - 1)],
            dst_ref=arrived.at[pl.ds(0, devices - 1)],
            send_sem=back_sem,
            recv_sem=recv_sem,
            device_id={"dp": me},
            device_id_type=MESH_ID,
        ).wait_recv()

        def compact(plane, carry):
            picked = arrived[pl.ds(plane * QUAD, QUAD)].reshape(QUAD * 16, 384)
            rows = pl.ds(pl.multiple_of(plane * QUAD * ROW, 16), QUAD * ROW)
            matrix[rows, :] = jnp.dot(
                narrow[...], picked, preferred_element_type=jnp.float32
            ).astype(jnp.bfloat16)
            return carry

        lax.fori_loop(0, 2 * NZ, compact, 0)
        joined = my_block >= 2
        mask = jnp.maximum(mask_ref[...], joined.astype(jnp.float32))
        raw = matrix[...].astype(jnp.float32)
        per_col = jnp.sum(raw * raw, axis=0, keepdims=True)
        square_sum = jnp.dot(
            jnp.broadcast_to(per_col, (8, 384)), mask, preferred_element_type=jnp.float32,
            precision=lax.Precision.HIGHEST,
        )[0:1]
        matrix[...] = (raw * lax.rsqrt(square_sum + EPSILON)).astype(jnp.bfloat16)
        for _ in range(NS_ITERS):
            current = matrix[...]
            gram_mat = (contract_rows(current, current) * mask).astype(jnp.bfloat16)
            square = jnp.dot(gram_mat, gram_mat, preferred_element_type=jnp.float32)
            gram[...] = (
                NEWTON_B * gram_mat.astype(jnp.float32) + NEWTON_C * square
            ).astype(jnp.bfloat16)
            matrix[...] = (
                NEWTON_A * current.astype(jnp.float32)
                + jnp.dot(current, gram[...], preferred_element_type=jnp.float32)
            ).astype(jnp.bfloat16)

        def expand(plane, carry):
            rows = pl.ds(pl.multiple_of(plane * QUAD * ROW, 16), QUAD * ROW)
            finished[pl.ds(plane * QUAD, QUAD)] = (
                jnp.dot(wide[...], matrix[rows, :], preferred_element_type=jnp.float32)
                .astype(jnp.bfloat16)
                .reshape(QUAD, 16, 384)
            )
            return carry

        lax.fori_loop(0, 2 * NZ, expand, 0)

        def give(target, carry):
            @pl.when(target != me)
            def _():
                pltpu.make_async_remote_copy(
                    src_ref=finished.at[target],
                    dst_ref=result.at[my_block],
                    send_sem=back_sem,
                    recv_sem=ret_sems.at[my_block],
                    device_id={"dp": target},
                    device_id_type=MESH_ID,
                ).start()

            return carry

        lax.fori_loop(0, devices, give, 0)
        stay = pltpu.make_async_copy(finished.at[me], result.at[my_block], local_sems.at[1])
        stay.start()
        stay.wait()
        pltpu.make_async_remote_copy(
            src_ref=finished.at[pl.ds(0, devices - 1)],
            dst_ref=finished.at[pl.ds(0, devices - 1)],
            send_sem=back_sem,
            recv_sem=recv_sem,
            device_id={"dp": me},
            device_id_type=MESH_ID,
        ).wait_send()

    for block in range(BLOCKS):

        @pl.when(me != owner_of(block))
        def _():
            outgoing(block).wait_send()
            pltpu.make_async_remote_copy(
                src_ref=result.at[block],
                dst_ref=result.at[block],
                send_sem=send_sems.at[block],
                recv_sem=ret_sems.at[block],
                device_id={"dp": owner_of(block)},
                device_id_type=MESH_ID,
            ).wait_recv()


def half_mask():
    side = np.arange(384) // 192
    return jnp.asarray(side[:, None] == side[None, :], jnp.float32)


def muon_step(look):
    return pl.pallas_call(
        muon_kernel,
        out_shape=jax.ShapeDtypeStruct((BLOCKS, 16, 384), jnp.bfloat16),
        in_specs=vmem_specs(4),
        out_specs=pl.BlockSpec(memory_space=pltpu.VMEM),
        scratch_shapes=[
            pltpu.VMEM((NZ * PLANE, 16, 384), jnp.bfloat16),
            pltpu.VMEM((768, 384), jnp.bfloat16),
            pltpu.VMEM((NZ * PLANE, 16, 384), jnp.bfloat16),
            pltpu.VMEM((384, 384), jnp.bfloat16),
            pltpu.SemaphoreType.DMA((2,)),
            pltpu.SemaphoreType.DMA((BLOCKS,)),
            pltpu.SemaphoreType.DMA,
            pltpu.SemaphoreType.DMA,
            pltpu.SemaphoreType.DMA((BLOCKS,)),
        ],
        compiler_params=pltpu.CompilerParams(
            collective_id=2, has_side_effects=True, vmem_limit_bytes=60_000_000
        ),
    )(look, spread_matrix(1, 16), spread_matrix(1, 16).T, half_mask())


def pack_blocks(attn, left, right):
    pairs = jnp.transpose(
        jnp.transpose(attn, (1, 0, 2)).reshape(ROW, 2, 384), (1, 0, 2)
    )
    stacked = jnp.concatenate([pairs, left, right], axis=0)
    return jnp.pad(stacked, ((0, 0), (0, 16 - ROW), (0, 0)))


TOKENS = 197
PAD = 208
WIDE = 768
HALF = 384
ERF_TOP = (
    0.00022905065861350646, 0.0034082910107109506, 0.050955695062380861,
    0.18520832239976145, 1.128379143519084,
)
ERF_BOTTOM = (
    -1.1791602954361697e-7, 0.000023547966471313185, 0.0010179625278914885,
    0.014070470171167667, 0.11098505178285362, 0.49746925110067538, 1.0,
)


def rows_dot(left_mat, right_mat):
    return jnp.dot(left_mat, right_mat, preferred_element_type=jnp.float32)


def mean_of(value):
    return jnp.sum(value, axis=-1, keepdims=True) * (1.0 / WIDE)


def norm_parts(row_data):
    center = row_data - mean_of(row_data)
    inv_std = lax.rsqrt(mean_of(center * center) + EPSILON)
    return center * inv_std, inv_std


def norm_pull(grad_result, normal, inv_std, gain_row):
    scaled = grad_result * gain_row
    return inv_std * (scaled - mean_of(scaled) - normal * mean_of(scaled * normal))


class TensorSum:
    def __init__(self, part, land_core, land_chip, final, send_sems, recv_sems, base):
        self.part, self.land_core, self.land_chip, self.final = part, land_core, land_chip, final
        self.send_sems, self.recv_sems, self.base = send_sems, recv_sems, base
        mine = lax.axis_index("tensor")
        self.core = lax.rem(mine, 2)
        self.other_core = mine + 1 - 2 * self.core
        self.other_chip = lax.rem(mine + 2, 4)
        self.copies = []

    def put(self, source, landing, target):
        slot = self.base + len(self.copies)
        copy = pltpu.make_async_remote_copy(
            src_ref=source,
            dst_ref=landing,
            send_sem=self.send_sems.at[slot],
            recv_sem=self.recv_sems.at[slot],
            device_id={"tensor": target},
            device_id_type=MESH_ID,
        )
        copy.start()
        self.copies.append(copy)

    def begin(self):
        self.put(self.part.at[1 - self.core], self.land_core, self.other_core)

    def across(self):
        self.copies[0].wait_recv()
        mine = self.part.at[self.core]
        mine[...] = (
            mine[...].astype(jnp.float32) + self.land_core[...].astype(jnp.float32)
        ).astype(jnp.bfloat16)
        self.put(mine, self.land_chip, self.other_chip)

    def share(self):
        self.copies[1].wait_recv()
        mine = self.final.at[self.core]
        mine[...] = (
            self.part[self.core].astype(jnp.float32) + self.land_chip[...].astype(jnp.float32)
        ).astype(jnp.bfloat16)
        self.put(mine, mine, self.other_core)

    def done(self):
        self.copies[2].wait_recv()

    def value(self):
        return jnp.concatenate(
            [self.final[0][:, :HALF], self.final[1][:, :HALF]], axis=1
        ).astype(jnp.float32)

    def finish(self):
        for copy in self.copies:
            copy.wait_send()


def main_kernel(
    inputs, cotangent, routes, attn_half, small_half, in_half, out_half,
    output, grad_inputs, grad_attn, grad_small, grad_in, grad_out,
    rows_in, rows_cot, prob_all, hidden_all, grad_pre_all,
    part_a, part_b, part_c, part_d, core_a, core_b, core_c, core_d,
    chip_a, chip_b, chip_c, chip_d, final_a, final_b, final_c, final_d,
    send_sems, recv_sems,
):
    mine = lax.axis_index("tensor")
    barrier = pltpu.get_barrier_semaphore()
    for target in (mine + 1 - 2 * lax.rem(mine, 2), lax.rem(mine + 2, 4)):
        pl.semaphore_signal(barrier, inc=1, device_id={"tensor": target}, device_id_type=MESH_ID)
    pl.semaphore_wait(barrier, 2)

    sum_attn = TensorSum(part_a, core_a, chip_a, final_a, send_sems, recv_sems, 0)
    sum_grad = TensorSum(part_b, core_b, chip_b, final_b, send_sems, recv_sems, 3)
    sum_moe = TensorSum(part_c, core_c, chip_c, final_c, send_sems, recv_sems, 6)
    sum_first = TensorSum(part_d, core_d, chip_d, final_d, send_sems, recv_sems, 9)

    def fill(part, value):
        part[0, :, :HALF] = value[:, :HALF].astype(jnp.bfloat16)
        part[1, :, :HALF] = value[:, HALF:].astype(jnp.bfloat16)

    for source, held in ((inputs, rows_in), (cotangent, rows_cot)):
        held[PAD - 16 : PAD, :] = jnp.zeros((16, WIDE), jnp.float32)
        held[0:TOKENS, :] = source[0]
    gain_rows = jnp.transpose(small_half[...].astype(jnp.float32))
    gain_one, gain_two = gain_rows[0:1], gain_rows[1:2]
    row_in = rows_in[...]
    normal_one, inv_one = norm_parts(row_in)
    normed_one = round_half(normal_one * gain_one)
    qkv = round_half(rows_dot(normed_one, attn_half[:, : 3 * 192]))
    row_id = lax.broadcasted_iota(jnp.int32, (PAD, PAD), 0)
    col_id = lax.broadcasted_iota(jnp.int32, (PAD, PAD), 1)
    scale = 1.0 / math.sqrt(HEAD_DIM)

    def head_of(value, which, head):
        start = which * 192 + head * HEAD_DIM
        return value[:, start : start + HEAD_DIM]

    head_rows = []
    for head in range(3):
        scores = contract_cols(head_of(qkv, 0, head), head_of(qkv, 1, head)) * scale
        scores = jnp.where(col_id < TOKENS, scores, -1e30)
        peak = jnp.max(scores, axis=-1, keepdims=True)
        log_total = peak + jnp.log(jnp.sum(jnp.exp(scores - peak), axis=-1, keepdims=True))
        prob = jnp.where(row_id < TOKENS, jnp.exp(scores - log_total), 0.0)
        prob_all[head] = prob
        head_rows.append(round_half(rows_dot(round_half(prob), head_of(qkv, 2, head))))
    blank = jnp.zeros((PAD, HEAD_DIM), jnp.bfloat16)
    attn_rows = jnp.concatenate([blank] + head_rows, axis=1)
    fill(part_a, contract_cols(attn_rows, attn_half[:, 512:768]))
    sum_attn.begin()
    sum_attn.across()
    sum_attn.share()
    sum_attn.done()
    middle = row_in + sum_attn.value()
    normal_two, inv_two = norm_parts(middle)
    normed_two = round_half(normal_two * gain_two)
    logits = rows_dot(normed_two, small_half[...])
    lane_id = lax.broadcasted_iota(jnp.int32, (TOKENS, LANE), 1) - 2
    picks = routes[0]
    gap = jnp.zeros((PAD - TOKENS, LANE), jnp.float32)

    def chosen_mask(which):
        hit = (lane_id == picks[:, which : which + 1]).astype(jnp.float32)
        return jnp.concatenate([hit, gap], axis=0)

    hot_first, hot_second = chosen_mask(0), chosen_mask(1)
    difference = jnp.sum(logits * (hot_first - hot_second), axis=-1, keepdims=True)
    gate_first = jax.nn.sigmoid(difference)
    gate_second = jax.nn.sigmoid(-difference)
    gates = gate_first * hot_first + gate_second * hot_second
    sign = hot_first - hot_second
    cot = rows_cot[...]
    moe_part = jnp.zeros((PAD, WIDE), jnp.float32)
    choice_part = jnp.zeros((PAD, 1), jnp.float32)
    grad_part = jnp.zeros((PAD, WIDE), jnp.float32)
    for expert in range(EF):
        gate = gates[:, 2 + expert : 3 + expert]
        pre_act = rows_dot(normed_two, in_half[expert])
        inner = 1.0 + erf_of(pre_act * ROOT_HALF)
        hidden = round_half(0.5 * pre_act * inner)
        slope = 0.5 * inner + pre_act * INV_ROOT_TAU * jnp.exp(-0.5 * pre_act * pre_act)
        expert_rows = contract_cols(hidden, out_half[expert])
        moe_part = moe_part + gate * expert_rows
        choice_part = choice_part + sign[:, 2 + expert : 3 + expert] * jnp.sum(
            cot * expert_rows, axis=-1, keepdims=True
        )
        grad_expert = round_half(gate * cot)
        grad_pre = round_half(rows_dot(grad_expert, out_half[expert]) * slope)
        grad_part = grad_part + contract_cols(grad_pre, in_half[expert])
        hidden_all[expert] = hidden
        grad_pre_all[expert] = grad_pre
    fill(part_b, grad_part)
    extra = lax.broadcasted_iota(jnp.int32, (PAD, LANE), 1) == 0
    part_b[0, :, HALF:] = jnp.where(extra, choice_part, 0.0).astype(jnp.bfloat16)
    part_b[1, :, HALF:] = jnp.zeros((PAD, LANE), jnp.bfloat16)
    sum_grad.begin()
    fill(part_c, moe_part)
    sum_grad.across()
    for expert in range(EF):
        grad_in[expert] = round_half(contract_rows(normed_two, grad_pre_all[expert]))
    sum_grad.share()
    for expert in range(EF):
        gate = gates[:, 2 + expert : 3 + expert]
        grad_out[expert] = round_half(contract_rows(round_half(gate * cot), hidden_all[expert]))
    sum_moe.begin()
    sum_grad.done()
    choice = final_b[0, :, HALF : HALF + 1].astype(jnp.float32)
    grad_first = choice * gate_first * gate_second
    grad_logits = round_half(grad_first * sign)
    grad_normed_two = sum_grad.value() + contract_cols(grad_logits, small_half[...])
    grad_middle = cot + norm_pull(grad_normed_two, normal_two, inv_two, gain_two)
    grad_gain_two = jnp.sum(grad_normed_two * normal_two, axis=0, keepdims=True)
    router_part = contract_rows(normed_two, grad_logits)
    grad_mid_half = round_half(grad_middle)
    grad_heads = round_half(rows_dot(grad_mid_half, attn_half[:, 512:768]))
    sum_moe.across()
    parts = [[], [], []]
    for head in range(3):
        grad_head = grad_heads[:, HEAD_DIM * (head + 1) : HEAD_DIM * (head + 2)]
        prob = prob_all[head]
        grad_prob = contract_cols(grad_head, head_of(qkv, 2, head))
        parts[2].append(round_half(contract_rows(round_half(prob), grad_head)))
        spread = jnp.sum(prob * grad_prob, axis=-1, keepdims=True)
        grad_scores = round_half(prob * (grad_prob - spread) * scale)
        parts[0].append(round_half(rows_dot(grad_scores, head_of(qkv, 1, head))))
        parts[1].append(round_half(contract_rows(grad_scores, head_of(qkv, 0, head))))
    grad_qkv = jnp.concatenate(parts[0] + parts[1] + parts[2] + [blank] * 3, axis=1)
    fill(part_d, contract_cols(grad_qkv, attn_half[...]))
    sum_first.begin()
    sum_moe.share()
    sum_first.across()
    grad_attn[:, :512] = round_half(contract_rows(normed_one, grad_qkv[:, :512]))
    grad_attn[:, 512:] = round_half(
        contract_rows(normed_one, grad_qkv[:, 512:])
        + contract_rows(grad_mid_half, attn_rows)
    )
    sum_moe.done()
    output[0] = (middle + sum_moe.value())[:TOKENS]
    sum_first.share()
    sum_first.done()
    grad_normed_one = sum_first.value()
    grad_inputs[0] = (grad_middle + norm_pull(grad_normed_one, normal_one, inv_one, gain_one))[
        :TOKENS
    ]
    grad_gain_one = jnp.sum(grad_normed_one * normal_one, axis=0, keepdims=True)
    gain_id = lax.broadcasted_iota(jnp.int32, (LANE, WIDE), 0)
    gain_block = jnp.where(
        gain_id == 0, grad_gain_one, jnp.where(gain_id == 1, grad_gain_two, 0.0)
    )
    grad_small[...] = round_half(jnp.transpose(gain_block) + router_part)
    for summing in (sum_attn, sum_grad, sum_moe, sum_first):
        summing.finish()


def erf_of(value):
    bounded = jnp.clip(value, -3.832506856900711, 3.832506856900711)
    square = bounded * bounded
    top = jnp.full_like(square, ERF_TOP[0])
    for factor in ERF_TOP[1:]:
        top = top * square + factor
    bottom = jnp.full_like(square, ERF_BOTTOM[0])
    for factor in ERF_BOTTOM[1:]:
        bottom = bottom * square + factor
    return bounded * top / bottom


def main_step(inputs, cotangent, routes, attn_half, small_half, in_half, out_half):
    half, single = jnp.bfloat16, jnp.float32
    narrow, wide = (PAD, HALF), (PAD, HALF + LANE)
    shapes = [narrow, wide, narrow, narrow]
    return pl.pallas_call(
        main_kernel,
        out_shape=[
            jax.ShapeDtypeStruct((1, TOKENS, WIDE), single),
            jax.ShapeDtypeStruct((1, TOKENS, WIDE), single),
            jax.ShapeDtypeStruct((WIDE, WIDE), half),
            jax.ShapeDtypeStruct((WIDE, LANE), half),
            jax.ShapeDtypeStruct((EF, WIDE, HALF), half),
            jax.ShapeDtypeStruct((EF, WIDE, HALF), half),
        ],
        in_specs=vmem_specs(7),
        out_specs=vmem_specs(6),
        scratch_shapes=[
            pltpu.VMEM((PAD, WIDE), single),
            pltpu.VMEM((PAD, WIDE), single),
            pltpu.VMEM((3, PAD, PAD), single),
            pltpu.VMEM((EF, PAD, HALF), half),
            pltpu.VMEM((EF, PAD, HALF), half),
        ]
        + [pltpu.VMEM((2,) + shape, half) for shape in shapes]
        + [pltpu.VMEM(shape, half) for shape in shapes]
        + [pltpu.VMEM(shape, half) for shape in shapes]
        + [pltpu.VMEM((2,) + shape, half) for shape in shapes]
        + [pltpu.SemaphoreType.DMA((12,)), pltpu.SemaphoreType.DMA((12,))],
        compiler_params=pltpu.CompilerParams(
            collective_id=3, has_side_effects=True, vmem_limit_bytes=60_000_000
        ),
    )(inputs, cotangent, routes, attn_half, small_half, in_half, out_half)


def shards(
    inputs,
    cotangent,
    norm_gains,
    attn_mats,
    router,
    expert_in,
    expert_out,
    moment_gains,
    moment_attn,
    moment_router,
    moment_in,
    moment_out,
    routes,
):
    attn_all, small_half, in_half, out_half = gather_weights(
        pack_rows(
            round_half(attn_mats),
            jnp.concatenate([round_half(norm_gains).T, round_half(router)], axis=1),
            round_half(expert_in),
            round_half(expert_out),
        )
    )
    output, grad_inputs, grad_attn, grad_small, grad_in, grad_out = main_step(
        inputs, cotangent, routes, attn_all, small_half, in_half, out_half
    )
    sum_attn, sum_small, sum_in, sum_out = unpack_rows(
        reduce_grads(grad_attn, grad_small, grad_in, grad_out)
    )
    sum_gains = sum_small[:, :2].T
    sum_router = sum_small[:, 2:]
    small_step = SMALL_RATE / math.sqrt(lax.axis_size("dp") * TOKENS)
    moment_gains_new = MOMENTUM * moment_gains + sum_gains
    moment_attn_new = MOMENTUM * moment_attn + sum_attn
    moment_router_new = MOMENTUM * moment_router + sum_router
    moment_in_new = MOMENTUM * moment_in + sum_in
    moment_out_new = MOMENTUM * moment_out + sum_out
    gains_new = norm_gains - small_step * moment_gains_new
    router_new = router - small_step * moment_router_new
    look_attn = sum_attn + MOMENTUM * moment_attn_new
    look_in = sum_in + MOMENTUM * moment_in_new
    look_out = sum_out + MOMENTUM * moment_out_new
    updates = to_single(muon_step(pack_blocks(*map(round_half, (look_attn, look_in, look_out)))))[
        :, :ROW
    ]
    update_attn = jnp.transpose(
        jnp.transpose(updates[0:2], (1, 0, 2)).reshape(ROW, 4, 192), (1, 0, 2)
    )
    attn_new = attn_mats - MUON_RATE * update_attn
    in_new = expert_in - MUON_RATE * updates[2 : EF + 2]
    out_new = expert_out - MUON_RATE * updates[EF + 2 : 2 * EF + 2]
    return (
        output,
        grad_inputs,
        sum_gains,
        sum_attn,
        sum_router,
        sum_in,
        sum_out,
        gains_new,
        attn_new,
        router_new,
        in_new,
        out_new,
        moment_gains_new,
        moment_attn_new,
        moment_router_new,
        moment_in_new,
        moment_out_new,
    )


def solution(mesh):
    return jax.shard_map(
        shards,
        mesh=mesh,
        in_specs=(
            P("dp", None, None),
            P("dp", None, None),
            P(None, "dp"),
            P(None, "dp", "tensor"),
            P("dp", None),
            P(None, "dp", "tensor"),
            P(None, "dp", "tensor"),
            P(None, "dp"),
            P(None, "dp", "tensor"),
            P("dp", None),
            P(None, "dp", "tensor"),
            P(None, "dp", "tensor"),
            P("dp", None, None),
        ),
        out_specs=(
            P("dp", None, None),
            P("dp", None, None),
            P(None, "dp"),
            P(None, "dp", "tensor"),
            P("dp", None),
            P(None, "dp", "tensor"),
            P(None, "dp", "tensor"),
            P(None, "dp"),
            P(None, "dp", "tensor"),
            P("dp", None),
            P(None, "dp", "tensor"),
            P(None, "dp", "tensor"),
            P(None, "dp"),
            P(None, "dp", "tensor"),
            P("dp", None),
            P(None, "dp", "tensor"),
            P(None, "dp", "tensor"),
        ),
        check_vma=False,
    )
```

```python
import math

import jax
import jax.numpy as jnp
import numpy as np
from jax import lax
from jax.experimental import pallas as pl
from jax.experimental.pallas import tpu as pltpu
from jax.sharding import PartitionSpec as P

HEAD_DIM = 64
EF = 3
NS_ITERS = 3
CAP = 197


EPSILON = 1e-06
MOMENTUM = 0.9
MUON_RATE = 0.5
SMALL_RATE = 0.5
NEWTON_A = 3.4445
NEWTON_B = -4.775
NEWTON_C = 2.0315
ROOT_HALF = 0.7071067811865476
INV_ROOT_TAU = 0.3989422804014327


def round_half(operand):
    return operand.astype(jnp.bfloat16)


def settle(operand):
    return lax.optimization_barrier(operand.astype(jnp.bfloat16))


def to_single(operand):
    return operand.astype(jnp.float32)


def contract_rows(left_mat, right_mat):
    return lax.dot_general(
        left_mat, right_mat, (((0,), (0,)), ((), ())), preferred_element_type=jnp.float32
    )


def contract_cols(left_mat, right_mat):
    return lax.dot_general(
        left_mat, right_mat, (((1,), (1,)), ((), ())), preferred_element_type=jnp.float32
    )


NZ, NX, NY = 8, 4, 2
ROW = 12
LANE = 128
PACK = 304
PLANE = NX * NY
QUAD = PLANE // 2
BLOCKS = 8
MESH_ID = pl.DeviceIdType.MESH
GROUPS = ((0, 4), (4, 4), (8, 4), (12, 4), (16, 4), (20, 4), (24, 1))


def spread_matrix(block_count, padded):
    table = np.zeros((block_count * QUAD * ROW, QUAD * padded), np.float32)
    for block in range(block_count):
        for member in range(QUAD):
            for row in range(ROW):
                table[
                    block * QUAD * ROW + member * ROW + row, member * padded + block * ROW + row
                ] = 1.0
    return jnp.asarray(table, jnp.bfloat16)


def place_of(me):
    return me // PLANE, lax.rem(me // NY, NX), lax.rem(me, NY)


def dp_index(z, x, y):
    return z * PLANE + x * NY + y


def wrap(value, count):
    return lax.rem(value + 2 * count, count)


def neighbours(me):
    z, x, y = place_of(me)
    return (
        dp_index(wrap(z + 1, NZ), x, y),
        dp_index(wrap(z - 1, NZ), x, y),
        dp_index(z, wrap(x + 1, NX), y),
        dp_index(z, wrap(x - 1, NX), y),
        dp_index(z, x, 1 - y),
    )


def send(source, landing, send_sem, recv_sem, target):
    copy = pltpu.make_async_remote_copy(
        src_ref=source,
        dst_ref=landing,
        send_sem=send_sem,
        recv_sem=recv_sem,
        device_id={"dp": target},
        device_id_type=MESH_ID,
    )
    copy.start()
    return copy


class GatherRing:
    def __init__(self, chunk, position, count, up, down, send_sems, recv_sems, base):
        self.chunk, self.position, self.count = chunk, position, count
        self.up, self.down = up, down
        self.send_sems, self.recv_sems, self.base = send_sems, recv_sems, base
        self.copies = []

    def start(self, step):
        half = step == self.count // 2 - 1
        pair = []
        for side, (sign, target) in enumerate(((-1, self.up), (1, self.down))):
            part = self.chunk(wrap(self.position + sign * step, self.count), side if half else None)
            slot = self.base + 2 * step + side
            pair.append(send(part, part, self.send_sems.at[slot], self.recv_sems.at[slot], target))
        self.copies.append(pair)

    def arrive(self, step):
        for copy in self.copies[step]:
            copy.wait_recv()

    def finish(self):
        for pair in self.copies:
            for copy in pair:
                copy.wait_send()


def vmem_specs(count):
    return [pl.BlockSpec(memory_space=pltpu.VMEM)] * count


def unpack_rows(rows):
    flat = jnp.transpose(rows[: 25 * ROW].reshape(25, ROW, LANE), (1, 0, 2)).reshape(ROW, 25 * LANE)
    attn = jnp.transpose(flat[:, :768].reshape(ROW, 4, 192), (1, 0, 2))
    small = flat[:, 768:773]
    left = jnp.transpose(flat[:, 896:2048].reshape(ROW, EF, 384), (1, 0, 2))
    right = jnp.transpose(flat[:, 2048:3200].reshape(ROW, EF, 384), (1, 0, 2))
    return attn, small, left, right


class ReduceRing:
    def __init__(self, chunk, landing, position, count, up, down, send_sems, recv_sems, base):
        self.chunk, self.landing = chunk, landing
        self.position, self.count = position, count
        self.up, self.down = up, down
        self.send_sems, self.recv_sems, self.base = send_sems, recv_sems, base
        self.copies = []

    def start(self, step):
        away = self.count // 2 - step
        pair = []
        for side, (sign, target) in enumerate(((1, self.up), (-1, self.down))):
            half = side if step == 0 else None
            part = self.chunk(wrap(self.position + sign * away, self.count), half)
            slot = self.base + 2 * step + side
            pair.append(
                send(
                    part,
                    self.landing(side, step, half),
                    self.send_sems.at[slot],
                    self.recv_sems.at[slot],
                    target,
                )
            )
        self.copies.append(pair)

    def arrive(self, step):
        for copy in self.copies[step]:
            copy.wait_recv()
        away = self.count // 2 - 1 - step
        if away == 0:
            mine = self.chunk(self.position, None)
            mine[...] = (
                mine[...].astype(jnp.float32)
                + self.landing(0, step, None)[...].astype(jnp.float32)
                + self.landing(1, step, None)[...].astype(jnp.float32)
            ).astype(jnp.bfloat16)
            return
        for side, sign in ((0, 1), (1, -1)):
            half = side if step == 0 else None
            mine = self.chunk(wrap(self.position + sign * away, self.count), half)
            mine[...] = (
                mine[...].astype(jnp.float32)
                + self.landing(side, step, half)[...].astype(jnp.float32)
            ).astype(jnp.bfloat16)

    def finish(self):
        for pair in self.copies:
            for copy in pair:
                copy.wait_send()


TOKENS = 197
PAD = 208
WIDE = 768
HALF = 384
ERF_TOP = (
    0.00022905065861350646, 0.0034082910107109506, 0.050955695062380861,
    0.18520832239976145, 1.128379143519084,
)
ERF_BOTTOM = (
    -1.1791602954361697e-7, 0.000023547966471313185, 0.0010179625278914885,
    0.014070470171167667, 0.11098505178285362, 0.49746925110067538, 1.0,
)


def rows_dot(left_mat, right_mat):
    return jnp.dot(left_mat, right_mat, preferred_element_type=jnp.float32)


def mean_of(value):
    return jnp.sum(value, axis=-1, keepdims=True) * (1.0 / WIDE)


def norm_parts(row_data):
    center = row_data - mean_of(row_data)
    inv_std = lax.rsqrt(mean_of(center * center) + EPSILON)
    return center * inv_std, inv_std


def norm_pull(grad_result, normal, inv_std, gain_row):
    scaled = grad_result * gain_row
    return inv_std * (scaled - mean_of(scaled) - normal * mean_of(scaled * normal))


class TensorSum:
    def __init__(self, part, land_core, land_chip, final, send_sems, recv_sems, base):
        self.part, self.land_core, self.land_chip, self.final = part, land_core, land_chip, final
        self.send_sems, self.recv_sems, self.base = send_sems, recv_sems, base
        mine = lax.axis_index("tensor")
        self.core = lax.rem(mine, 2)
        self.other_core = mine + 1 - 2 * self.core
        self.other_chip = lax.rem(mine + 2, 4)
        self.copies = []

    def put(self, source, landing, target):
        slot = self.base + len(self.copies)
        copy = pltpu.make_async_remote_copy(
            src_ref=source,
            dst_ref=landing,
            send_sem=self.send_sems.at[slot],
            recv_sem=self.recv_sems.at[slot],
            device_id={"tensor": target},
            device_id_type=MESH_ID,
        )
        copy.start()
        self.copies.append(copy)

    def begin(self):
        self.put(self.part.at[1 - self.core], self.land_core, self.other_core)

    def across(self):
        self.copies[0].wait_recv()
        mine = self.part.at[self.core]
        mine[...] = (
            mine[...].astype(jnp.float32) + self.land_core[...].astype(jnp.float32)
        ).astype(jnp.bfloat16)
        self.put(mine, self.land_chip, self.other_chip)

    def share(self):
        self.copies[1].wait_recv()
        mine = self.final.at[self.core]
        mine[...] = (
            self.part[self.core].astype(jnp.float32) + self.land_chip[...].astype(jnp.float32)
        ).astype(jnp.bfloat16)
        self.put(mine, mine, self.other_core)

    def done(self):
        self.copies[2].wait_recv()

    def value(self):
        return jnp.concatenate(
            [self.final[0][:, :HALF], self.final[1][:, :HALF]], axis=1
        ).astype(jnp.float32)

    def finish(self):
        for copy in self.copies:
            copy.wait_send()


def erf_of(value):
    bounded = jnp.clip(value, -3.832506856900711, 3.832506856900711)
    square = bounded * bounded
    top = jnp.full_like(square, ERF_TOP[0])
    for factor in ERF_TOP[1:]:
        top = top * square + factor
    bottom = jnp.full_like(square, ERF_BOTTOM[0])
    for factor in ERF_BOTTOM[1:]:
        bottom = bottom * square + factor
    return bounded * top / bottom


class Rounds:
    def __init__(self, queue):
        self.queue, self.turn = queue, 0
        self.turns = 1 + max(begin + ring.count // 2 for ring, begin in queue)

    def advance(self):
        for ring, begin in self.queue:
            step = self.turn - begin
            if 1 <= step <= ring.count // 2:
                ring.arrive(step - 1)
            if 0 <= step < ring.count // 2:
                ring.start(step)
        self.turn += 1

    def finish(self):
        for ring, _ in self.queue:
            ring.finish()


SETS = ((0, 48, 48, GROUPS[:2]), (96, 96, 112, GROUPS[2:]))
RING_SEMS = 2 * 77


def mega_kernel(
    inputs, cotangent, routes, gains, router, attn_mats, mats_in, mats_out,
    moment_attn, moment_in, moment_out, four, one, four_back, one_back, mask_ref,
    output, grad_inputs, total, result,
    packed, slots, attn_half, small_half, in_half, out_half,
    rows_in, rows_cot, prob_all, hidden_all, grad_pre_all,
    grad_attn, grad_small, grad_in, grad_out, sums,
    land_az_p, land_bx_p, land_ax_p, land_bz_p, land_y_p,
    land_az_e, land_bx_e, land_ax_e, land_bz_e, land_y_e,
    part_a, part_b, part_c, part_d, core_a, core_b, core_c, core_d,
    chip_a, chip_b, chip_c, chip_d, final_a, final_b, final_c, final_d,
    small_land, look, arrived, matrix, finished, gram,
    gather_send, gather_recv, reduce_send, reduce_recv, send_sems, recv_sems,
    small_send, small_recv, local_sems, muon_send, muon_recv, back_sem, ret_sems,
):
    me = lax.axis_index("dp")
    mine = lax.axis_index("tensor")
    z, x, y = place_of(me)
    up_z, down_z, up_x, down_x, other_y = neighbours(me)
    barrier = pltpu.get_barrier_semaphore()
    for target in (up_z, down_z, up_x, down_x, other_y):
        pl.semaphore_signal(barrier, inc=1, device_id={"dp": target}, device_id_type=MESH_ID)
    for away in (1, 2, 3):
        pl.semaphore_signal(
            barrier, inc=1, device_id={"tensor": lax.rem(mine + away, 4)}, device_id_type=MESH_ID
        )

    diagonal = lax.broadcasted_iota(jnp.int32, (ROW, ROW), 0) == lax.broadcasted_iota(
        jnp.int32, (ROW, ROW), 1
    )
    lanes = lax.broadcasted_iota(jnp.int32, (ROW, LANE), 1)

    def upright(row):
        return jnp.sum(jnp.where(diagonal, row, 0.0), axis=1, keepdims=True)

    def flat_attn(ref):
        return jnp.concatenate([ref[:, which, :] for which in range(4)], axis=1)

    def block_rows(block):
        return slice(block * ROW, (block + 1) * ROW)

    flat = flat_attn(attn_mats)
    for block in range(6):
        packed[block_rows(block), :] = flat[:, block * LANE : (block + 1) * LANE]
    small = jnp.zeros((ROW, LANE), jnp.float32)
    for lane, (source, row) in enumerate(((gains, 0), (gains, 1), (router, 0), (router, 1), (router, 2))):
        small = small + jnp.where(lanes == lane, upright(source[row : row + 1, :]), 0.0)
    packed[block_rows(6), :] = small
    for index in range(9):
        column = (index % 3) * LANE
        packed[block_rows(7 + index), :] = mats_in[index // 3, :, column : column + LANE]
        packed[block_rows(16 + index), :] = mats_out[index // 3, :, column : column + LANE]
    packed[25 * ROW : PACK, :] = jnp.zeros((PACK - 25 * ROW, LANE), jnp.float32)
    slots[z, NY * x + y] = round_half(packed[...])
    pl.semaphore_wait(barrier, 8)

    def across_x(plane, rows, wide):
        def chunk(index, half):
            if half is None:
                return slots.at[plane, pl.ds(NY * index, NY), rows]
            return slots.at[plane, pl.ds(NY * index + half, 1), rows]

        return chunk

    def across_z(column, rows, wide):
        def chunk(index, half):
            if half is None:
                return slots.at[index, pl.ds(NY * column, NY), rows]
            return slots.at[index, pl.ds(NY * column + half, 1), rows]

        return chunk

    def sem_bases(first):
        while True:
            yield first
            first += 4

    def gather_rounds(which):
        low, rows_a, rows_b, _ = SETS[which]
        head, rest = pl.ds(low, rows_a), pl.ds(low + rows_a, rows_b)
        base = sem_bases(77 * which + 1)

        def ring_x(plane, rows):
            return GatherRing(
                across_x(plane, rows, None), x, NX, up_x, down_x, gather_send, gather_recv,
                next(base),
            )

        def ring_z(column, rows):
            first_sem = next(base)
            next(base)
            return GatherRing(
                across_z(column, rows, None), z, NZ, up_z, down_z, gather_send, gather_recv,
                first_sem,
            )

        queue = [
            (ring_x(z, head), 0), (ring_z(x, rest), 0), (ring_z(x, head), 0), (ring_x(z, rest), 0)
        ]
        for away in (1, NZ - 1):
            queue.append((ring_x(wrap(z + away, NZ), rest), 1))
        for away in (1, NX - 1):
            queue.append((ring_z(wrap(x + away, NX), head), 1))
        queue.append((ring_z(wrap(x + 2, NX), head), 2))
        for away in (2, NZ - 2, 3, NZ - 3, 4):
            queue.append((ring_x(wrap(z + away, NZ), rest), min(away, NZ - away)))
        return Rounds(queue)

    def gather_first(which):
        low, rows_a, rows_b, _ = SETS[which]
        own = slots.at[z, NY * x + y, pl.ds(low, rows_a + rows_b)]
        return send(own, own, gather_send.at[77 * which], gather_recv.at[77 * which], other_y)

    lands = (
        (land_az_p, land_bx_p, land_ax_p, land_bz_p, land_y_p),
        (land_az_e, land_bx_e, land_ax_e, land_bz_e, land_y_e),
    )

    def landing_in(held, which):
        def landing(side, step, half):
            if half is None:
                return held.at[which, side, step]
            return held.at[which, side, step, pl.ds(half, 1)]

        return landing

    def reduce_rounds(which):
        low, rows_a, rows_b, _ = SETS[which]
        land_az, land_bx, land_ax, land_bz, _ = lands[which]
        head, rest = pl.ds(low, rows_a), pl.ds(low + rows_a, rows_b)
        base = sem_bases(77 * which + 1)

        def ring_x(plane, rows, held, index):
            return ReduceRing(
                across_x(plane, rows, None), landing_in(held, index), x, NX, up_x, down_x,
                reduce_send, reduce_recv, next(base),
            )

        def ring_z(column, rows, held, index):
            first_sem = next(base)
            next(base)
            return ReduceRing(
                across_z(column, rows, None), landing_in(held, index), z, NZ, up_z, down_z,
                reduce_send, reduce_recv, first_sem,
            )

        queue = []
        for index, away in enumerate((4, 3, NZ - 3, 2, NZ - 2, 1, NZ - 1, 0)):
            queue.append(
                (ring_x(wrap(z + away, NZ), rest, land_bx, index), 4 - min(away, NZ - away))
            )
        for index, (away, begin) in enumerate(((2, 0), (1, 1), (NX - 1, 1), (0, 2))):
            queue.append((ring_z(wrap(x + away, NX), head, land_az, index), begin))
        queue.append((ring_x(z, head, land_ax, 0), 4))
        queue.append((ring_z(x, rest, land_bz, 0), 2))
        return Rounds(queue)

    def reduce_last(which):
        low, rows_a, rows_b, _ = SETS[which]
        return send(
            slots.at[z, NY * x + 1 - y, pl.ds(low, rows_a + rows_b)], lands[which][4],
            reduce_send.at[77 * which], reduce_recv.at[77 * which], other_y,
        )

    def reduce_close(which, copy):
        low, rows_a, rows_b, _ = SETS[which]
        rows = slice(low, low + rows_a + rows_b)
        copy.wait_recv()
        sums[rows, :] = slots[z, NY * x + y, rows].astype(jnp.float32) + lands[which][4][
            ...
        ].astype(jnp.float32)

    def place(refs, block):
        attn_ref, small_ref, in_ref, out_ref = refs
        if block < 6:
            return attn_ref, None, block * LANE
        if block == 6:
            return small_ref, None, 0
        index = (block - 7) % 9
        return (in_ref if block < 16 else out_ref), index // 3, (index % 3) * LANE

    def compact(which):
        refs = (attn_half, small_half, in_half, out_half)

        def body(plane, carry):
            rows = pl.ds(pl.multiple_of(plane * PLANE * ROW, 32), PLANE * ROW)
            for first_block, block_count in SETS[which][3]:
                padded = 48 if block_count == 4 else 16
                picked = slots[plane, :, pl.ds(first_block * ROW, padded), :]
                sides = [
                    picked[side * QUAD : (side + 1) * QUAD].reshape(QUAD * padded, LANE)
                    for side in range(2)
                ]
                moved = rows_dot(
                    (four if block_count == 4 else one)[...], jnp.concatenate(sides, axis=1)
                ).astype(jnp.bfloat16)
                for block in range(block_count):
                    part = moved[block * QUAD * ROW : (block + 1) * QUAD * ROW]
                    value = jnp.concatenate([part[:, :LANE], part[:, LANE:]], axis=0)
                    ref, lead, column = place(refs, first_block + block)
                    if lead is None:
                        ref[rows, column : column + LANE] = value
                    else:
                        ref[lead, rows, column : column + LANE] = value
            return carry

        lax.fori_loop(0, NZ, body, 0)

    def expand(which):
        refs = (grad_attn, grad_small, grad_in, grad_out)

        def body(plane, carry):
            rows = pl.ds(pl.multiple_of(plane * PLANE * ROW, 32), PLANE * ROW)
            for first_block, block_count in SETS[which][3]:
                padded = 48 if block_count == 4 else 16
                stacked = []
                for block in range(block_count):
                    ref, lead, column = place(refs, first_block + block)
                    if lead is None:
                        part = ref[rows, column : column + LANE]
                    else:
                        part = ref[lead, rows, column : column + LANE]
                    stacked.append(
                        jnp.concatenate([part[: QUAD * ROW], part[QUAD * ROW :]], axis=1)
                    )
                moved = rows_dot(
                    (four_back if block_count == 4 else one_back)[...],
                    stacked[0] if block_count == 1 else jnp.concatenate(stacked, axis=0),
                ).astype(jnp.bfloat16)
                for side in range(2):
                    slots[
                        plane, side * QUAD : (side + 1) * QUAD,
                        pl.ds(first_block * ROW, padded), :,
                    ] = moved[:, side * LANE : (side + 1) * LANE].reshape(QUAD, padded, LANE)
            return carry

        lax.fori_loop(0, NZ, body, 0)

    first_p, first_e = gather_first(0), gather_first(1)
    near, far = gather_rounds(0), gather_rounds(1)
    for source, held in ((inputs, rows_in), (cotangent, rows_cot)):
        held[PAD - 16 : PAD, :] = jnp.zeros((16, WIDE), jnp.float32)
        held[0:TOKENS, :] = source[0]
    row_in = rows_in[...]
    normal_one, inv_one = norm_parts(row_in)
    first_p.wait_recv()
    for turn in range(near.turns):
        near.advance()
        if turn == LAG - 1:
            first_e.wait_recv()
        if turn >= LAG:
            far.advance()
    compact(0)

    sum_attn = TensorSum(part_a, core_a, chip_a, final_a, send_sems, recv_sems, 0)
    sum_grad = TensorSum(part_b, core_b, chip_b, final_b, send_sems, recv_sems, 3)
    sum_moe = TensorSum(part_c, core_c, chip_c, final_c, send_sems, recv_sems, 6)
    sum_first = TensorSum(part_d, core_d, chip_d, final_d, send_sems, recv_sems, 9)

    def fill(part, value):
        part[0, :, :HALF] = value[:, :HALF].astype(jnp.bfloat16)
        part[1, :, :HALF] = value[:, HALF:].astype(jnp.bfloat16)

    gain_rows = jnp.transpose(small_half[...].astype(jnp.float32))
    gain_one, gain_two = gain_rows[0:1], gain_rows[1:2]
    normed_one = round_half(normal_one * gain_one)
    qkv = round_half(rows_dot(normed_one, attn_half[:, : 3 * 192]))
    if far.turn < far.turns:
        far.advance()
    row_id = lax.broadcasted_iota(jnp.int32, (PAD, PAD), 0)
    col_id = lax.broadcasted_iota(jnp.int32, (PAD, PAD), 1)
    scale = 1.0 / math.sqrt(HEAD_DIM)

    def head_of(value, which, head):
        start = which * 192 + head * HEAD_DIM
        return value[:, start : start + HEAD_DIM]

    head_rows = []
    for head in range(3):
        scores = contract_cols(head_of(qkv, 0, head), head_of(qkv, 1, head)) * scale
        scores = jnp.where(col_id < TOKENS, scores, -1e30)
        peak = jnp.max(scores, axis=-1, keepdims=True)
        log_total = peak + jnp.log(jnp.sum(jnp.exp(scores - peak), axis=-1, keepdims=True))
        prob = jnp.where(row_id < TOKENS, jnp.exp(scores - log_total), 0.0)
        prob_all[head] = prob
        head_rows.append(round_half(rows_dot(round_half(prob), head_of(qkv, 2, head))))
    blank = jnp.zeros((PAD, HEAD_DIM), jnp.bfloat16)
    attn_rows = jnp.concatenate([blank] + head_rows, axis=1)
    fill(part_a, contract_cols(attn_rows, attn_half[:, 512:768]))
    sum_attn.begin()
    if far.turn < far.turns:
        far.advance()
    sum_attn.across()
    if far.turn < far.turns:
        far.advance()
    sum_attn.share()
    while far.turn < far.turns:
        far.advance()
    sum_attn.done()
    middle = row_in + sum_attn.value()
    normal_two, inv_two = norm_parts(middle)
    normed_two = round_half(normal_two * gain_two)
    compact(1)
    logits = rows_dot(normed_two, small_half[...])
    lane_id = lax.broadcasted_iota(jnp.int32, (TOKENS, LANE), 1) - 2
    picks = routes[0]
    gap = jnp.zeros((PAD - TOKENS, LANE), jnp.float32)

    def chosen_mask(which):
        hit = (lane_id == picks[:, which : which + 1]).astype(jnp.float32)
        return jnp.concatenate([hit, gap], axis=0)

    hot_first, hot_second = chosen_mask(0), chosen_mask(1)
    sign = hot_first - hot_second
    difference = jnp.sum(logits * sign, axis=-1, keepdims=True)
    gate_first = jax.nn.sigmoid(difference)
    gate_second = jax.nn.sigmoid(-difference)
    gates = gate_first * hot_first + gate_second * hot_second
    cot = rows_cot[...]
    moe_part = jnp.zeros((PAD, WIDE), jnp.float32)
    choice_part = jnp.zeros((PAD, 1), jnp.float32)
    grad_part = jnp.zeros((PAD, WIDE), jnp.float32)
    for expert in range(EF):
        gate = gates[:, 2 + expert : 3 + expert]
        pre_act = rows_dot(normed_two, in_half[expert])
        inner = 1.0 + erf_of(pre_act * ROOT_HALF)
        hidden = round_half(0.5 * pre_act * inner)
        slope = 0.5 * inner + pre_act * INV_ROOT_TAU * jnp.exp(-0.5 * pre_act * pre_act)
        expert_rows = contract_cols(hidden, out_half[expert])
        moe_part = moe_part + gate * expert_rows
        choice_part = choice_part + sign[:, 2 + expert : 3 + expert] * jnp.sum(
            cot * expert_rows, axis=-1, keepdims=True
        )
        grad_expert = round_half(gate * cot)
        grad_pre = round_half(rows_dot(grad_expert, out_half[expert]) * slope)
        grad_part = grad_part + contract_cols(grad_pre, in_half[expert])
        hidden_all[expert] = hidden
        grad_pre_all[expert] = grad_pre
    fill(part_b, grad_part)
    extra = lax.broadcasted_iota(jnp.int32, (PAD, LANE), 1) == 0
    part_b[0, :, HALF:] = jnp.where(extra, choice_part, 0.0).astype(jnp.bfloat16)
    part_b[1, :, HALF:] = jnp.zeros((PAD, LANE), jnp.bfloat16)
    sum_grad.begin()
    fill(part_c, moe_part)
    near.finish()
    far.finish()
    first_p.wait_send()
    first_e.wait_send()
    for expert in range(EF):
        grad_in[expert] = round_half(contract_rows(normed_two, grad_pre_all[expert]))
    sum_grad.across()
    for expert in range(EF):
        gate = gates[:, 2 + expert : 3 + expert]
        grad_out[expert] = round_half(contract_rows(round_half(gate * cot), hidden_all[expert]))
    sum_grad.share()
    expand(1)
    far = reduce_rounds(1)
    far.advance()
    sum_moe.begin()
    sum_grad.done()
    choice = final_b[0, :, HALF : HALF + 1].astype(jnp.float32)
    grad_first = choice * gate_first * gate_second
    grad_logits = round_half(grad_first * sign)
    grad_normed_two = sum_grad.value() + contract_cols(grad_logits, small_half[...])
    grad_middle = cot + norm_pull(grad_normed_two, normal_two, inv_two, gain_two)
    far.advance()
    grad_gain_two = jnp.sum(grad_normed_two * normal_two, axis=0, keepdims=True)
    router_part = contract_rows(normed_two, grad_logits)
    grad_mid_half = round_half(grad_middle)
    grad_heads = round_half(rows_dot(grad_mid_half, attn_half[:, 512:768]))
    sum_moe.across()
    parts = [[], [], []]
    for head in range(3):
        grad_head = grad_heads[:, HEAD_DIM * (head + 1) : HEAD_DIM * (head + 2)]
        prob = prob_all[head]
        grad_prob = contract_cols(grad_head, head_of(qkv, 2, head))
        parts[2].append(round_half(contract_rows(round_half(prob), grad_head)))
        spread = jnp.sum(prob * grad_prob, axis=-1, keepdims=True)
        grad_scores = round_half(prob * (grad_prob - spread) * scale)
        parts[0].append(round_half(rows_dot(grad_scores, head_of(qkv, 1, head))))
        parts[1].append(round_half(contract_rows(grad_scores, head_of(qkv, 0, head))))
        if head > 0:
            far.advance()
    grad_qkv = jnp.concatenate(parts[0] + parts[1] + parts[2] + [blank] * 3, axis=1)
    first_part = contract_cols(grad_qkv, attn_half[...])
    fill(part_d, first_part)
    grad_attn[:, :512] = round_half(contract_rows(normed_one, grad_qkv[:, :512]))
    grad_attn[:, 512:] = round_half(
        contract_rows(normed_one, grad_qkv[:, 512:]) + contract_rows(grad_mid_half, attn_rows)
    )
    grad_gain_one = jnp.sum(first_part * normal_one, axis=0, keepdims=True)
    gain_id = lax.broadcasted_iota(jnp.int32, (LANE, WIDE), 0)
    gain_block = jnp.where(
        gain_id == 0, grad_gain_one, jnp.where(gain_id == 1, grad_gain_two, 0.0)
    )
    grad_small[...] = round_half(jnp.transpose(gain_block) + router_part)
    expand(0)
    near = reduce_rounds(0)
    near.advance()
    far.advance()
    sum_first.begin()
    near.advance()
    far.advance()
    sum_moe.share()
    near.advance()
    while far.turn < far.turns:
        far.advance()
    last_e = reduce_last(1)
    sum_first.across()
    sum_moe.done()
    output[0] = (middle + sum_moe.value())[:TOKENS]
    near.advance()
    near.advance()
    reduce_close(1, last_e)
    near.advance()
    while near.turn < near.turns:
        near.advance()
    last_p = reduce_last(0)
    sum_first.share()

    look[...] = jnp.zeros((BLOCKS, 16, HALF), jnp.bfloat16)

    def sum_cols(first_block, block_count):
        return jnp.concatenate(
            [sums[block_rows(first_block + block), :] for block in range(block_count)], axis=1
        )

    def look_of(gradient, moment):
        return round_half(gradient + MOMENTUM * (MOMENTUM * moment + gradient))

    for expert in range(EF):
        look[2 + EF + expert, 0:ROW, :] = look_of(sum_cols(16 + 3 * expert, 3), moment_out[expert])
        if expert > 0:
            look[2 + expert, 0:ROW, :] = look_of(sum_cols(7 + 3 * expert, 3), moment_in[expert])
    reduce_close(0, last_p)
    look[2, 0:ROW, :] = look_of(sum_cols(7, 3), moment_in[0])
    ahead = look_of(sum_cols(0, 6), flat_attn(moment_attn))
    look[0, 0:ROW, :] = ahead[:, :HALF]
    look[1, 0:ROW, :] = ahead[:, HALF:]

    shift = lax.rem(mine, 2) * 4
    own = lax.rem(me, PLANE) == shift
    my_block = me // PLANE
    devices = NZ * PLANE

    def owner_of(block):
        return block * PLANE + shift

    def outgoing(block):
        return pltpu.make_async_remote_copy(
            src_ref=look.at[block], dst_ref=arrived.at[me], send_sem=muon_send.at[block],
            recv_sem=muon_recv, device_id={"dp": owner_of(block)}, device_id_type=MESH_ID,
        )

    for block in range(BLOCKS):

        @pl.when(me != owner_of(block))
        def _():
            outgoing(block).start()

    small_land[mine] = sums[72:88, :]
    small_copies = []
    for away in (1, 2, 3):
        copy = pltpu.make_async_remote_copy(
            src_ref=small_land.at[mine], dst_ref=small_land.at[mine],
            send_sem=small_send.at[away], recv_sem=small_recv.at[away],
            device_id={"tensor": lax.rem(mine + away, 4)}, device_id_type=MESH_ID,
        )
        copy.start()
        small_copies.append(copy)
    sum_first.done()
    grad_normed_one = sum_first.value()
    grad_inputs[0] = (grad_middle + norm_pull(grad_normed_one, normal_one, inv_one, gain_one))[
        :TOKENS
    ]
    for copy in small_copies:
        copy.wait_recv()
    joint = small_land[0] + small_land[1] + small_land[2] + small_land[3]
    small_lane = lax.broadcasted_iota(jnp.int32, (16, LANE), 1)
    small_row = lax.broadcasted_iota(jnp.int32, (16, LANE), 0)
    total[...] = sums[...]
    total[72:88, :] = jnp.where((small_lane == 0) & (small_row < ROW), joint, sums[72:88, :])
    for copy in small_copies:
        copy.wait_send()

    @pl.when(own)
    def _():
        keep = pltpu.make_async_copy(look.at[my_block], arrived.at[me], local_sems.at[0])
        keep.start()
        keep.wait()
        pltpu.make_async_remote_copy(
            src_ref=arrived.at[pl.ds(0, devices - 1)], dst_ref=arrived.at[pl.ds(0, devices - 1)],
            send_sem=back_sem, recv_sem=muon_recv, device_id={"dp": me}, device_id_type=MESH_ID,
        ).wait_recv()

        def gathered(quad, carry):
            picked = arrived[pl.ds(quad * QUAD, QUAD)].reshape(QUAD * 16, HALF)
            rows = pl.ds(pl.multiple_of(quad * QUAD * ROW, 16), QUAD * ROW)
            matrix[rows, :] = round_half(rows_dot(one[...], picked))
            return carry

        lax.fori_loop(0, 2 * NZ, gathered, 0)
        joined = my_block >= 2
        mask = jnp.maximum(mask_ref[...], joined.astype(jnp.float32))
        raw = matrix[...].astype(jnp.float32)
        per_col = jnp.sum(raw * raw, axis=0, keepdims=True)
        square_sum = jnp.dot(
            jnp.broadcast_to(per_col, (8, HALF)), mask, preferred_element_type=jnp.float32,
            precision=lax.Precision.HIGHEST,
        )[0:1]
        matrix[...] = round_half(raw * lax.rsqrt(square_sum + EPSILON))
        for _ in range(NS_ITERS):
            current = matrix[...]
            gram_mat = round_half(contract_rows(current, current) * mask)
            square = rows_dot(gram_mat, gram_mat)
            gram[...] = round_half(NEWTON_B * gram_mat.astype(jnp.float32) + NEWTON_C * square)
            matrix[...] = round_half(
                NEWTON_A * current.astype(jnp.float32) + rows_dot(current, gram[...])
            )

        def scattered(quad, carry):
            rows = pl.ds(pl.multiple_of(quad * QUAD * ROW, 16), QUAD * ROW)
            finished[pl.ds(quad * QUAD, QUAD)] = round_half(
                rows_dot(one_back[...], matrix[rows, :])
            ).reshape(QUAD, 16, HALF)
            return carry

        lax.fori_loop(0, 2 * NZ, scattered, 0)

        def give(target, carry):
            @pl.when(target != me)
            def _():
                pltpu.make_async_remote_copy(
                    src_ref=finished.at[target], dst_ref=result.at[my_block], send_sem=back_sem,
                    recv_sem=ret_sems.at[my_block], device_id={"dp": target},
                    device_id_type=MESH_ID,
                ).start()

            return carry

        lax.fori_loop(0, devices, give, 0)
        stay = pltpu.make_async_copy(finished.at[me], result.at[my_block], local_sems.at[1])
        stay.start()
        stay.wait()
        pltpu.make_async_remote_copy(
            src_ref=finished.at[pl.ds(0, devices - 1)], dst_ref=finished.at[pl.ds(0, devices - 1)],
            send_sem=back_sem, recv_sem=muon_recv, device_id={"dp": me}, device_id_type=MESH_ID,
        ).wait_send()

    for block in range(BLOCKS):

        @pl.when(me != owner_of(block))
        def _():
            outgoing(block).wait_send()
            pltpu.make_async_remote_copy(
                src_ref=result.at[block], dst_ref=result.at[block], send_sem=muon_send.at[block],
                recv_sem=ret_sems.at[block], device_id={"dp": owner_of(block)},
                device_id_type=MESH_ID,
            ).wait_recv()

    near.finish()
    far.finish()
    last_p.wait_send()
    last_e.wait_send()
    for summing in (sum_attn, sum_grad, sum_moe, sum_first):
        summing.finish()


LAG = 3


def half_mask():
    side = np.arange(384) // 192
    return jnp.asarray(side[:, None] == side[None, :], jnp.float32)


def whole_step(inputs, cotangent, routes, gains, router, attn, mats_in, mats_out, moments):
    half, single = jnp.bfloat16, jnp.float32
    shapes = [(PAD, HALF), (PAD, HALF + LANE), (PAD, HALF), (PAD, HALF)]
    lands = []
    for _, rows_a, rows_b, _ in SETS:
        lands += [
            pltpu.VMEM((NX, 2, 4, NY, rows_a, LANE), half),
            pltpu.VMEM((NZ, 2, 2, NY, rows_b, LANE), half),
            pltpu.VMEM((1, 2, 2, NY, rows_a, LANE), half),
            pltpu.VMEM((1, 2, 4, NY, rows_b, LANE), half),
            pltpu.VMEM((rows_a + rows_b, LANE), half),
        ]
    weights = [(WIDE, WIDE), (WIDE, LANE), (EF, WIDE, HALF), (EF, WIDE, HALF)]
    dma = pltpu.SemaphoreType.DMA
    four, one = spread_matrix(4, 48), spread_matrix(1, 16)
    return pl.pallas_call(
        mega_kernel,
        out_shape=[
            jax.ShapeDtypeStruct((1, TOKENS, WIDE), single),
            jax.ShapeDtypeStruct((1, TOKENS, WIDE), single),
            jax.ShapeDtypeStruct((PACK, LANE), single),
            jax.ShapeDtypeStruct((BLOCKS, 16, HALF), half),
        ],
        in_specs=vmem_specs(16),
        out_specs=vmem_specs(4),
        scratch_shapes=[
            pltpu.VMEM((PACK, LANE), single),
            pltpu.VMEM((NZ, PLANE, PACK, LANE), half),
        ]
        + [pltpu.VMEM(shape, half) for shape in weights]
        + [
            pltpu.VMEM((PAD, WIDE), single),
            pltpu.VMEM((PAD, WIDE), single),
            pltpu.VMEM((3, PAD, PAD), single),
            pltpu.VMEM((EF, PAD, HALF), half),
            pltpu.VMEM((EF, PAD, HALF), half),
        ]
        + [pltpu.VMEM(shape, half) for shape in weights]
        + [pltpu.VMEM((PACK, LANE), single)]
        + lands
        + [pltpu.VMEM((2,) + shape, half) for shape in shapes]
        + [pltpu.VMEM(shape, half) for shape in shapes]
        + [pltpu.VMEM(shape, half) for shape in shapes]
        + [pltpu.VMEM((2,) + shape, half) for shape in shapes]
        + [
            pltpu.VMEM((4, 16, LANE), single),
            pltpu.VMEM((BLOCKS, 16, HALF), half),
            pltpu.VMEM((NZ * PLANE, 16, HALF), half),
            pltpu.VMEM((WIDE, HALF), half),
            pltpu.VMEM((NZ * PLANE, 16, HALF), half),
            pltpu.VMEM((HALF, HALF), half),
            dma((RING_SEMS,)), dma((RING_SEMS,)), dma((RING_SEMS,)), dma((RING_SEMS,)),
            dma((12,)), dma((12,)), dma((4,)), dma((4,)),
            dma((2,)), dma((BLOCKS,)), dma, dma, dma((BLOCKS,)),
        ],
        compiler_params=pltpu.CompilerParams(
            collective_id=0, has_side_effects=True, vmem_limit_bytes=64_000_000
        ),
    )(
        inputs, cotangent, routes, gains, router, attn, mats_in, mats_out, *moments,
        four, one, four.T, one.T, half_mask(),
    )


def shards(
    inputs,
    cotangent,
    norm_gains,
    attn_mats,
    router,
    expert_in,
    expert_out,
    moment_gains,
    moment_attn,
    moment_router,
    moment_in,
    moment_out,
    routes,
):
    def by_rows(value):
        return jnp.transpose(value, (1, 0, 2))

    output, grad_inputs, total, finished = whole_step(
        inputs, cotangent, routes, norm_gains, router.T, by_rows(attn_mats), expert_in, expert_out,
        (by_rows(moment_attn), moment_in, moment_out),
    )
    sum_attn, sum_small, sum_in, sum_out = unpack_rows(total)
    sum_gains = sum_small[:, :2].T
    sum_router = sum_small[:, 2:]
    small_step = SMALL_RATE / math.sqrt(lax.axis_size("dp") * TOKENS)
    moment_gains_new = MOMENTUM * moment_gains + sum_gains
    moment_attn_new = MOMENTUM * moment_attn + sum_attn
    moment_router_new = MOMENTUM * moment_router + sum_router
    moment_in_new = MOMENTUM * moment_in + sum_in
    moment_out_new = MOMENTUM * moment_out + sum_out
    gains_new = norm_gains - small_step * moment_gains_new
    router_new = router - small_step * moment_router_new
    updates = to_single(finished)[:, :ROW]
    update_attn = jnp.transpose(
        jnp.transpose(updates[0:2], (1, 0, 2)).reshape(ROW, 4, 192), (1, 0, 2)
    )
    attn_new = attn_mats - MUON_RATE * update_attn
    in_new = expert_in - MUON_RATE * updates[2 : EF + 2]
    out_new = expert_out - MUON_RATE * updates[EF + 2 : 2 * EF + 2]
    return (
        output,
        grad_inputs,
        sum_gains,
        sum_attn,
        sum_router,
        sum_in,
        sum_out,
        gains_new,
        attn_new,
        router_new,
        in_new,
        out_new,
        moment_gains_new,
        moment_attn_new,
        moment_router_new,
        moment_in_new,
        moment_out_new,
    )


def solution(mesh):
    return jax.shard_map(
        shards,
        mesh=mesh,
        in_specs=(
            P("dp", None, None),
            P("dp", None, None),
            P(None, "dp"),
            P(None, "dp", "tensor"),
            P("dp", None),
            P(None, "dp", "tensor"),
            P(None, "dp", "tensor"),
            P(None, "dp"),
            P(None, "dp", "tensor"),
            P("dp", None),
            P(None, "dp", "tensor"),
            P(None, "dp", "tensor"),
            P("dp", None, None),
        ),
        out_specs=(
            P("dp", None, None),
            P("dp", None, None),
            P(None, "dp"),
            P(None, "dp", "tensor"),
            P("dp", None),
            P(None, "dp", "tensor"),
            P(None, "dp", "tensor"),
            P(None, "dp"),
            P(None, "dp", "tensor"),
            P("dp", None),
            P(None, "dp", "tensor"),
            P(None, "dp", "tensor"),
            P(None, "dp"),
            P(None, "dp", "tensor"),
            P("dp", None),
            P(None, "dp", "tensor"),
            P(None, "dp", "tensor"),
        ),
        check_vma=False,
    )
```

```python
import math

import jax
import jax.numpy as jnp
import numpy as np
from jax import lax
from jax.experimental import pallas as pl
from jax.experimental.pallas import tpu as pltpu
from jax.sharding import PartitionSpec as P

HEAD_DIM = 64
EF = 3
NS_ITERS = 3
CAP = 197


EPSILON = 1e-06
MOMENTUM = 0.9
MUON_RATE = 0.5
SMALL_RATE = 0.5
NEWTON_A = 3.4445
NEWTON_B = -4.775
NEWTON_C = 2.0315
ROOT_HALF = 0.7071067811865476
INV_ROOT_TAU = 0.3989422804014327


def round_half(operand):
    return operand.astype(jnp.bfloat16)


def settle(operand):
    return lax.optimization_barrier(operand.astype(jnp.bfloat16))


def to_single(operand):
    return operand.astype(jnp.float32)


def contract_rows(left_mat, right_mat):
    return lax.dot_general(
        left_mat, right_mat, (((0,), (0,)), ((), ())), preferred_element_type=jnp.float32
    )


def contract_cols(left_mat, right_mat):
    return lax.dot_general(
        left_mat, right_mat, (((1,), (1,)), ((), ())), preferred_element_type=jnp.float32
    )


NZ, NX, NY = 8, 4, 2
ROW = 12
LANE = 128
PACK = 304
PLANE = NX * NY
QUAD = PLANE // 2
BLOCKS = 8
MESH_ID = pl.DeviceIdType.MESH
GROUPS = ((0, 4), (4, 4), (8, 4), (12, 4), (16, 4), (20, 4), (24, 1))


def spread_matrix(block_count, padded):
    table = np.zeros((block_count * QUAD * ROW, QUAD * padded), np.float32)
    for block in range(block_count):
        for member in range(QUAD):
            for row in range(ROW):
                table[
                    block * QUAD * ROW + member * ROW + row, member * padded + block * ROW + row
                ] = 1.0
    return jnp.asarray(table, jnp.bfloat16)


def place_of(me):
    return me // PLANE, lax.rem(me // NY, NX), lax.rem(me, NY)


def dp_index(z, x, y):
    return z * PLANE + x * NY + y


def wrap(value, count):
    return lax.rem(value + 2 * count, count)


def neighbours(me):
    z, x, y = place_of(me)
    return (
        dp_index(wrap(z + 1, NZ), x, y),
        dp_index(wrap(z - 1, NZ), x, y),
        dp_index(z, wrap(x + 1, NX), y),
        dp_index(z, wrap(x - 1, NX), y),
        dp_index(z, x, 1 - y),
    )


def send(source, landing, send_sem, recv_sem, target):
    copy = pltpu.make_async_remote_copy(
        src_ref=source,
        dst_ref=landing,
        send_sem=send_sem,
        recv_sem=recv_sem,
        device_id={"dp": target},
        device_id_type=MESH_ID,
    )
    copy.start()
    return copy


class GatherRing:
    def __init__(self, chunk, position, count, up, down, send_sems, recv_sems, base):
        self.chunk, self.position, self.count = chunk, position, count
        self.up, self.down = up, down
        self.send_sems, self.recv_sems, self.base = send_sems, recv_sems, base
        self.copies = []

    def start(self, step):
        half = step == self.count // 2 - 1
        pair = []
        for side, (sign, target) in enumerate(((-1, self.up), (1, self.down))):
            part = self.chunk(wrap(self.position + sign * step, self.count), side if half else None)
            slot = self.base + 2 * step + side
            pair.append(send(part, part, self.send_sems.at[slot], self.recv_sems.at[slot], target))
        self.copies.append(pair)

    def arrive(self, step):
        for copy in self.copies[step]:
            copy.wait_recv()

    def finish(self):
        for pair in self.copies:
            for copy in pair:
                copy.wait_send()


def vmem_specs(count):
    return [pl.BlockSpec(memory_space=pltpu.VMEM)] * count


class ReduceRing:
    def __init__(self, chunk, landing, position, count, up, down, send_sems, recv_sems, base):
        self.chunk, self.landing = chunk, landing
        self.position, self.count = position, count
        self.up, self.down = up, down
        self.send_sems, self.recv_sems, self.base = send_sems, recv_sems, base
        self.copies = []

    def start(self, step):
        away = self.count // 2 - step
        pair = []
        for side, (sign, target) in enumerate(((1, self.up), (-1, self.down))):
            half = side if step == 0 else None
            part = self.chunk(wrap(self.position + sign * away, self.count), half)
            slot = self.base + 2 * step + side
            pair.append(
                send(
                    part,
                    self.landing(side, step, half),
                    self.send_sems.at[slot],
                    self.recv_sems.at[slot],
                    target,
                )
            )
        self.copies.append(pair)

    def arrive(self, step):
        for copy in self.copies[step]:
            copy.wait_recv()
        away = self.count // 2 - 1 - step
        if away == 0:
            mine = self.chunk(self.position, None)
            mine[...] = (
                mine[...].astype(jnp.float32)
                + self.landing(0, step, None)[...].astype(jnp.float32)
                + self.landing(1, step, None)[...].astype(jnp.float32)
            ).astype(jnp.bfloat16)
            return
        for side, sign in ((0, 1), (1, -1)):
            half = side if step == 0 else None
            mine = self.chunk(wrap(self.position + sign * away, self.count), half)
            mine[...] = (
                mine[...].astype(jnp.float32)
                + self.landing(side, step, half)[...].astype(jnp.float32)
            ).astype(jnp.bfloat16)

    def finish(self):
        for pair in self.copies:
            for copy in pair:
                copy.wait_send()


TOKENS = 197
PAD = 208
WIDE = 768
HALF = 384
ERF_TOP = (
    0.00022905065861350646, 0.0034082910107109506, 0.050955695062380861,
    0.18520832239976145, 1.128379143519084,
)
ERF_BOTTOM = (
    -1.1791602954361697e-7, 0.000023547966471313185, 0.0010179625278914885,
    0.014070470171167667, 0.11098505178285362, 0.49746925110067538, 1.0,
)


def rows_dot(left_mat, right_mat):
    return jnp.dot(left_mat, right_mat, preferred_element_type=jnp.float32)


def mean_of(value):
    return jnp.sum(value, axis=-1, keepdims=True) * (1.0 / WIDE)


def norm_parts(row_data):
    center = row_data - mean_of(row_data)
    inv_std = lax.rsqrt(mean_of(center * center) + EPSILON)
    return center * inv_std, inv_std


def norm_pull(grad_result, normal, inv_std, gain_row):
    scaled = grad_result * gain_row
    return inv_std * (scaled - mean_of(scaled) - normal * mean_of(scaled * normal))


class TensorSum:
    def __init__(self, part, land_core, land_chip, final, send_sems, recv_sems, base):
        self.part, self.land_core, self.land_chip, self.final = part, land_core, land_chip, final
        self.send_sems, self.recv_sems, self.base = send_sems, recv_sems, base
        mine = lax.axis_index("tensor")
        self.core = lax.rem(mine, 2)
        self.other_core = mine + 1 - 2 * self.core
        self.other_chip = lax.rem(mine + 2, 4)
        self.copies = []

    def put(self, source, landing, target):
        slot = self.base + len(self.copies)
        copy = pltpu.make_async_remote_copy(
            src_ref=source,
            dst_ref=landing,
            send_sem=self.send_sems.at[slot],
            recv_sem=self.recv_sems.at[slot],
            device_id={"tensor": target},
            device_id_type=MESH_ID,
        )
        copy.start()
        self.copies.append(copy)

    def begin(self):
        self.put(self.part.at[1 - self.core], self.land_core, self.other_core)

    def across(self):
        self.copies[0].wait_recv()
        mine = self.part.at[self.core]
        mine[...] = (
            mine[...].astype(jnp.float32) + self.land_core[...].astype(jnp.float32)
        ).astype(jnp.bfloat16)
        self.put(mine, self.land_chip, self.other_chip)

    def share(self):
        self.copies[1].wait_recv()
        mine = self.final.at[self.core]
        mine[...] = (
            self.part[self.core].astype(jnp.float32) + self.land_chip[...].astype(jnp.float32)
        ).astype(jnp.bfloat16)
        self.put(mine, mine, self.other_core)

    def done(self):
        self.copies[2].wait_recv()

    def value(self):
        return jnp.concatenate(
            [self.final[0][:, :HALF], self.final[1][:, :HALF]], axis=1
        ).astype(jnp.float32)

    def finish(self):
        for copy in self.copies:
            copy.wait_send()


def erf_of(value):
    bounded = jnp.clip(value, -3.832506856900711, 3.832506856900711)
    square = bounded * bounded
    top = jnp.full_like(square, ERF_TOP[0])
    for factor in ERF_TOP[1:]:
        top = top * square + factor
    bottom = jnp.full_like(square, ERF_BOTTOM[0])
    for factor in ERF_BOTTOM[1:]:
        bottom = bottom * square + factor
    return bounded * top / bottom


class Rounds:
    def __init__(self, queue):
        self.queue, self.turn = queue, 0
        self.turns = 1 + max(begin + ring.count // 2 for ring, begin in queue)

    def advance(self):
        for ring, begin in self.queue:
            step = self.turn - begin
            if 1 <= step <= ring.count // 2:
                ring.arrive(step - 1)
            if 0 <= step < ring.count // 2:
                ring.start(step)
        self.turn += 1

    def finish(self):
        for ring, _ in self.queue:
            ring.finish()


SETS = ((0, 48, 48, GROUPS[:2]), (96, 96, 112, GROUPS[2:]))
RING_SEMS = 2 * 77


def mega_kernel(
    inputs, cotangent, routes, gains, router, attn_mats, mats_in, mats_out,
    moment_attn, moment_in, moment_out, four, one, four_back, one_back, mask_ref,
    output, grad_inputs, total, result,
    packed, slots, attn_half, small_half, in_half, out_half,
    raw_in, raw_cot, rows_in, rows_cot, prob_all, hidden_all, grad_pre_all,
    grad_attn, grad_small, grad_in, grad_out, sums,
    land_az_p, land_bx_p, land_ax_p, land_bz_p, land_y_p,
    land_az_e, land_bx_e, land_ax_e, land_bz_e, land_y_e,
    part_a, part_b, part_c, part_d, core_a, core_b, core_c, core_d,
    chip_a, chip_b, chip_c, chip_d, final_a, final_b, final_c, final_d,
    small_land, look, arrived, matrix, finished, gram,
    gather_send, gather_recv, reduce_send, reduce_recv, send_sems, recv_sems,
    small_send, small_recv, local_sems, muon_send, muon_recv, back_sem, ret_sems,
):
    me = lax.axis_index("dp")
    mine = lax.axis_index("tensor")
    z, x, y = place_of(me)
    up_z, down_z, up_x, down_x, other_y = neighbours(me)
    loads = []
    for index, (source, held) in enumerate(((inputs, raw_in), (cotangent, raw_cot))):
        copy = pltpu.make_async_copy(source.at[:, 0, :], held, local_sems.at[2 + index])
        copy.start()
        loads.append(copy)
    barrier = pltpu.get_barrier_semaphore()
    for target in (up_z, down_z, up_x, down_x, other_y):
        pl.semaphore_signal(barrier, inc=1, device_id={"dp": target}, device_id_type=MESH_ID)
    for away in (1, 2, 3):
        pl.semaphore_signal(
            barrier, inc=1, device_id={"tensor": lax.rem(mine + away, 4)}, device_id_type=MESH_ID
        )

    diagonal = lax.broadcasted_iota(jnp.int32, (ROW, ROW), 0) == lax.broadcasted_iota(
        jnp.int32, (ROW, ROW), 1
    )
    lanes = lax.broadcasted_iota(jnp.int32, (ROW, LANE), 1)

    def upright(row):
        return jnp.sum(jnp.where(diagonal, row, 0.0), axis=1, keepdims=True)

    def flat_attn(ref):
        return jnp.concatenate([ref[:, which, :] for which in range(4)], axis=1)

    def block_rows(block):
        return slice(block * ROW, (block + 1) * ROW)

    flat = flat_attn(attn_mats)
    for block in range(6):
        packed[block_rows(block), :] = flat[:, block * LANE : (block + 1) * LANE]
    small = jnp.zeros((ROW, LANE), jnp.float32)
    for lane, (source, row) in enumerate(((gains, 0), (gains, 1), (router, 0), (router, 1), (router, 2))):
        small = small + jnp.where(lanes == lane, upright(source[row : row + 1, :]), 0.0)
    packed[block_rows(6), :] = small
    for index in range(9):
        column = (index % 3) * LANE
        packed[block_rows(7 + index), :] = mats_in[index // 3, :, column : column + LANE]
        packed[block_rows(16 + index), :] = mats_out[index // 3, :, column : column + LANE]
    packed[25 * ROW : PACK, :] = jnp.zeros((PACK - 25 * ROW, LANE), jnp.float32)
    slots[z, NY * x + y] = round_half(packed[...])
    pl.semaphore_wait(barrier, 8)

    def across_x(plane, rows, wide):
        def chunk(index, half):
            if half is None:
                return slots.at[plane, pl.ds(NY * index, NY), rows]
            return slots.at[plane, pl.ds(NY * index + half, 1), rows]

        return chunk

    def across_z(column, rows, wide):
        def chunk(index, half):
            if half is None:
                return slots.at[index, pl.ds(NY * column, NY), rows]
            return slots.at[index, pl.ds(NY * column + half, 1), rows]

        return chunk

    def sem_bases(first):
        while True:
            yield first
            first += 4

    def gather_rounds(which):
        low, rows_a, rows_b, _ = SETS[which]
        head, rest = pl.ds(low, rows_a), pl.ds(low + rows_a, rows_b)
        base = sem_bases(77 * which + 1)

        def ring_x(plane, rows):
            return GatherRing(
                across_x(plane, rows, None), x, NX, up_x, down_x, gather_send, gather_recv,
                next(base),
            )

        def ring_z(column, rows):
            first_sem = next(base)
            next(base)
            return GatherRing(
                across_z(column, rows, None), z, NZ, up_z, down_z, gather_send, gather_recv,
                first_sem,
            )

        queue = [
            (ring_x(z, head), 0), (ring_z(x, rest), 0), (ring_z(x, head), 0), (ring_x(z, rest), 0)
        ]
        for away in (1, NZ - 1):
            queue.append((ring_x(wrap(z + away, NZ), rest), 1))
        for away in (1, NX - 1):
            queue.append((ring_z(wrap(x + away, NX), head), 1))
        queue.append((ring_z(wrap(x + 2, NX), head), 2))
        for away in (2, NZ - 2, 3, NZ - 3, 4):
            queue.append((ring_x(wrap(z + away, NZ), rest), min(away, NZ - away)))
        return Rounds(queue)

    def gather_first(which):
        low, rows_a, rows_b, _ = SETS[which]
        own = slots.at[z, NY * x + y, pl.ds(low, rows_a + rows_b)]
        return send(own, own, gather_send.at[77 * which], gather_recv.at[77 * which], other_y)

    lands = (
        (land_az_p, land_bx_p, land_ax_p, land_bz_p, land_y_p),
        (land_az_e, land_bx_e, land_ax_e, land_bz_e, land_y_e),
    )

    def landing_in(held, which):
        def landing(side, step, half):
            if half is None:
                return held.at[which, side, step]
            return held.at[which, side, step, pl.ds(half, 1)]

        return landing

    def reduce_rounds(which):
        low, rows_a, rows_b, _ = SETS[which]
        land_az, land_bx, land_ax, land_bz, _ = lands[which]
        head, rest = pl.ds(low, rows_a), pl.ds(low + rows_a, rows_b)
        base = sem_bases(77 * which + 1)

        def ring_x(plane, rows, held, index):
            return ReduceRing(
                across_x(plane, rows, None), landing_in(held, index), x, NX, up_x, down_x,
                reduce_send, reduce_recv, next(base),
            )

        def ring_z(column, rows, held, index):
            first_sem = next(base)
            next(base)
            return ReduceRing(
                across_z(column, rows, None), landing_in(held, index), z, NZ, up_z, down_z,
                reduce_send, reduce_recv, first_sem,
            )

        queue = []
        for index, away in enumerate((4, 3, NZ - 3, 2, NZ - 2, 1, NZ - 1, 0)):
            queue.append(
                (ring_x(wrap(z + away, NZ), rest, land_bx, index), 4 - min(away, NZ - away))
            )
        for index, (away, begin) in enumerate(((2, 0), (1, 1), (NX - 1, 1), (0, 2))):
            queue.append((ring_z(wrap(x + away, NX), head, land_az, index), begin))
        queue.append((ring_x(z, head, land_ax, 0), 4))
        queue.append((ring_z(x, rest, land_bz, 0), 2))
        return Rounds(queue)

    def reduce_last(which):
        low, rows_a, rows_b, _ = SETS[which]
        return send(
            slots.at[z, NY * x + 1 - y, pl.ds(low, rows_a + rows_b)], lands[which][4],
            reduce_send.at[77 * which], reduce_recv.at[77 * which], other_y,
        )

    def reduce_close(which, copy):
        low, rows_a, rows_b, _ = SETS[which]
        rows = slice(low, low + rows_a + rows_b)
        copy.wait_recv()
        sums[rows, :] = slots[z, NY * x + y, rows].astype(jnp.float32) + lands[which][4][
            ...
        ].astype(jnp.float32)

    def place(refs, block):
        attn_ref, small_ref, in_ref, out_ref = refs
        if block < 6:
            return attn_ref, None, block * LANE
        if block == 6:
            return small_ref, None, 0
        index = (block - 7) % 9
        return (in_ref if block < 16 else out_ref), index // 3, (index % 3) * LANE

    def compact(which):
        refs = (attn_half, small_half, in_half, out_half)

        def body(plane, carry):
            rows = pl.ds(pl.multiple_of(plane * PLANE * ROW, 32), PLANE * ROW)
            for first_block, block_count in SETS[which][3]:
                padded = 48 if block_count == 4 else 16
                picked = slots[plane, :, pl.ds(first_block * ROW, padded), :]
                sides = [
                    picked[side * QUAD : (side + 1) * QUAD].reshape(QUAD * padded, LANE)
                    for side in range(2)
                ]
                moved = rows_dot(
                    (four if block_count == 4 else one)[...], jnp.concatenate(sides, axis=1)
                ).astype(jnp.bfloat16)
                for block in range(block_count):
                    part = moved[block * QUAD * ROW : (block + 1) * QUAD * ROW]
                    value = jnp.concatenate([part[:, :LANE], part[:, LANE:]], axis=0)
                    ref, lead, column = place(refs, first_block + block)
                    if lead is None:
                        ref[rows, column : column + LANE] = value
                    else:
                        ref[lead, rows, column : column + LANE] = value
            return carry

        lax.fori_loop(0, NZ, body, 0)

    def expand(which):
        refs = (grad_attn, grad_small, grad_in, grad_out)

        def body(plane, carry):
            rows = pl.ds(pl.multiple_of(plane * PLANE * ROW, 32), PLANE * ROW)
            for first_block, block_count in SETS[which][3]:
                padded = 48 if block_count == 4 else 16
                stacked = []
                for block in range(block_count):
                    ref, lead, column = place(refs, first_block + block)
                    if lead is None:
                        part = ref[rows, column : column + LANE]
                    else:
                        part = ref[lead, rows, column : column + LANE]
                    stacked.append(
                        jnp.concatenate([part[: QUAD * ROW], part[QUAD * ROW :]], axis=1)
                    )
                moved = rows_dot(
                    (four_back if block_count == 4 else one_back)[...],
                    stacked[0] if block_count == 1 else jnp.concatenate(stacked, axis=0),
                ).astype(jnp.bfloat16)
                for side in range(2):
                    slots[
                        plane, side * QUAD : (side + 1) * QUAD,
                        pl.ds(first_block * ROW, padded), :,
                    ] = moved[:, side * LANE : (side + 1) * LANE].reshape(QUAD, padded, LANE)
            return carry

        lax.fori_loop(0, NZ, body, 0)

    first_p, first_e = gather_first(0), gather_first(1)
    near, far = gather_rounds(0), gather_rounds(1)
    for copy, raw, held in zip(loads, (raw_in, raw_cot), (rows_in, rows_cot)):
        copy.wait()
        held[PAD - 16 : PAD, :] = jnp.zeros((16, WIDE), jnp.float32)
        held[0:TOKENS, :] = raw[...]
    row_in = rows_in[...]
    normal_one, inv_one = norm_parts(row_in)
    first_p.wait_recv()
    for turn in range(near.turns):
        near.advance()
        if turn == LAG - 1:
            first_e.wait_recv()
        if turn >= LAG:
            far.advance()
    compact(0)

    sum_attn = TensorSum(part_a, core_a, chip_a, final_a, send_sems, recv_sems, 0)
    sum_grad = TensorSum(part_b, core_b, chip_b, final_b, send_sems, recv_sems, 3)
    sum_moe = TensorSum(part_c, core_c, chip_c, final_c, send_sems, recv_sems, 6)
    sum_first = TensorSum(part_d, core_d, chip_d, final_d, send_sems, recv_sems, 9)

    def fill(part, value):
        part[0, :, :HALF] = value[:, :HALF].astype(jnp.bfloat16)
        part[1, :, :HALF] = value[:, HALF:].astype(jnp.bfloat16)

    gain_rows = jnp.transpose(small_half[...].astype(jnp.float32))
    gain_one, gain_two = gain_rows[0:1], gain_rows[1:2]
    normed_one = round_half(normal_one * gain_one)
    qkv = round_half(rows_dot(normed_one, attn_half[:, : 3 * 192]))
    if far.turn < far.turns:
        far.advance()
    row_id = lax.broadcasted_iota(jnp.int32, (PAD, PAD), 0)
    col_id = lax.broadcasted_iota(jnp.int32, (PAD, PAD), 1)
    scale = 1.0 / math.sqrt(HEAD_DIM)

    def head_of(value, which, head):
        start = which * 192 + head * HEAD_DIM
        return value[:, start : start + HEAD_DIM]

    head_rows = []
    for head in range(3):
        scores = contract_cols(head_of(qkv, 0, head), head_of(qkv, 1, head)) * scale
        scores = jnp.where(col_id < TOKENS, scores, -1e30)
        peak = jnp.max(scores, axis=-1, keepdims=True)
        log_total = peak + jnp.log(jnp.sum(jnp.exp(scores - peak), axis=-1, keepdims=True))
        prob = jnp.where(row_id < TOKENS, jnp.exp(scores - log_total), 0.0)
        prob_all[head] = prob
        head_rows.append(round_half(rows_dot(round_half(prob), head_of(qkv, 2, head))))
    blank = jnp.zeros((PAD, HEAD_DIM), jnp.bfloat16)
    attn_rows = jnp.concatenate([blank] + head_rows, axis=1)
    fill(part_a, contract_cols(attn_rows, attn_half[:, 512:768]))
    sum_attn.begin()
    if far.turn < far.turns:
        far.advance()
    sum_attn.across()
    if far.turn < far.turns:
        far.advance()
    sum_attn.share()
    while far.turn < far.turns:
        far.advance()
    sum_attn.done()
    middle = row_in + sum_attn.value()
    normal_two, inv_two = norm_parts(middle)
    normed_two = round_half(normal_two * gain_two)
    compact(1)
    logits = rows_dot(normed_two, small_half[...])
    expert_id = lax.broadcasted_iota(jnp.int32, (16, TOKENS), 0)
    lane_id = lax.broadcasted_iota(jnp.int32, (16, LANE), 1) - 2
    spread = (lane_id == lax.broadcasted_iota(jnp.int32, (16, LANE), 0)).astype(jnp.bfloat16)
    gap = jnp.zeros((16, PAD - TOKENS), jnp.float32)

    def chosen_mask(which):
        hit = (expert_id == routes[which : which + 1, :]).astype(jnp.float32)
        return contract_rows(round_half(jnp.concatenate([hit, gap], axis=1)), spread)

    hot_first, hot_second = chosen_mask(0), chosen_mask(1)
    sign = hot_first - hot_second
    difference = jnp.sum(logits * sign, axis=-1, keepdims=True)
    gate_first = jax.nn.sigmoid(difference)
    gate_second = jax.nn.sigmoid(-difference)
    gates = gate_first * hot_first + gate_second * hot_second
    cot = rows_cot[...]
    moe_part = jnp.zeros((PAD, WIDE), jnp.float32)
    choice_part = jnp.zeros((PAD, 1), jnp.float32)
    grad_part = jnp.zeros((PAD, WIDE), jnp.float32)
    for expert in range(EF):
        gate = gates[:, 2 + expert : 3 + expert]
        pre_act = rows_dot(normed_two, in_half[expert])
        inner = 1.0 + erf_of(pre_act * ROOT_HALF)
        hidden = round_half(0.5 * pre_act * inner)
        slope = 0.5 * inner + pre_act * INV_ROOT_TAU * jnp.exp(-0.5 * pre_act * pre_act)
        expert_rows = contract_cols(hidden, out_half[expert])
        moe_part = moe_part + gate * expert_rows
        choice_part = choice_part + sign[:, 2 + expert : 3 + expert] * jnp.sum(
            cot * expert_rows, axis=-1, keepdims=True
        )
        grad_expert = round_half(gate * cot)
        grad_pre = round_half(rows_dot(grad_expert, out_half[expert]) * slope)
        grad_part = grad_part + contract_cols(grad_pre, in_half[expert])
        hidden_all[expert] = hidden
        grad_pre_all[expert] = grad_pre
    fill(part_b, grad_part)
    extra = lax.broadcasted_iota(jnp.int32, (PAD, LANE), 1) == 0
    part_b[0, :, HALF:] = jnp.where(extra, choice_part, 0.0).astype(jnp.bfloat16)
    part_b[1, :, HALF:] = jnp.zeros((PAD, LANE), jnp.bfloat16)
    sum_grad.begin()
    fill(part_c, moe_part)
    near.finish()
    far.finish()
    first_p.wait_send()
    first_e.wait_send()
    for expert in range(EF):
        grad_in[expert] = round_half(contract_rows(normed_two, grad_pre_all[expert]))
    sum_grad.across()
    for expert in range(EF):
        gate = gates[:, 2 + expert : 3 + expert]
        grad_out[expert] = round_half(contract_rows(round_half(gate * cot), hidden_all[expert]))
    sum_grad.share()
    expand(1)
    far = reduce_rounds(1)
    far.advance()
    sum_moe.begin()
    sum_grad.done()
    choice = final_b[0, :, HALF : HALF + 1].astype(jnp.float32)
    grad_first = choice * gate_first * gate_second
    grad_logits = round_half(grad_first * sign)
    grad_normed_two = sum_grad.value() + contract_cols(grad_logits, small_half[...])
    grad_middle = cot + norm_pull(grad_normed_two, normal_two, inv_two, gain_two)
    far.advance()
    grad_gain_two = jnp.sum(grad_normed_two * normal_two, axis=0, keepdims=True)
    router_part = contract_rows(normed_two, grad_logits)
    grad_mid_half = round_half(grad_middle)
    grad_heads = round_half(rows_dot(grad_mid_half, attn_half[:, 512:768]))
    sum_moe.across()
    parts = [[], [], []]
    for head in range(3):
        grad_head = grad_heads[:, HEAD_DIM * (head + 1) : HEAD_DIM * (head + 2)]
        prob = prob_all[head]
        grad_prob = contract_cols(grad_head, head_of(qkv, 2, head))
        parts[2].append(round_half(contract_rows(round_half(prob), grad_head)))
        spread = jnp.sum(prob * grad_prob, axis=-1, keepdims=True)
        grad_scores = round_half(prob * (grad_prob - spread) * scale)
        parts[0].append(round_half(rows_dot(grad_scores, head_of(qkv, 1, head))))
        parts[1].append(round_half(contract_rows(grad_scores, head_of(qkv, 0, head))))
        if head > 0:
            far.advance()
    grad_qkv = jnp.concatenate(parts[0] + parts[1] + parts[2] + [blank] * 3, axis=1)
    first_part = contract_cols(grad_qkv, attn_half[...])
    fill(part_d, first_part)
    grad_attn[:, :512] = round_half(contract_rows(normed_one, grad_qkv[:, :512]))
    grad_attn[:, 512:] = round_half(
        contract_rows(normed_one, grad_qkv[:, 512:]) + contract_rows(grad_mid_half, attn_rows)
    )
    grad_gain_one = jnp.sum(first_part * normal_one, axis=0, keepdims=True)
    gain_id = lax.broadcasted_iota(jnp.int32, (LANE, WIDE), 0)
    gain_block = jnp.where(
        gain_id == 0, grad_gain_one, jnp.where(gain_id == 1, grad_gain_two, 0.0)
    )
    grad_small[...] = round_half(jnp.transpose(gain_block) + router_part)
    expand(0)
    near = reduce_rounds(0)
    near.advance()
    far.advance()
    sum_first.begin()
    near.advance()
    far.advance()
    sum_moe.share()
    near.advance()
    while far.turn < far.turns:
        far.advance()
    last_e = reduce_last(1)
    sum_first.across()
    sum_moe.done()
    output[0] = (middle + sum_moe.value())[:TOKENS]
    near.advance()
    near.advance()
    reduce_close(1, last_e)
    near.advance()
    while near.turn < near.turns:
        near.advance()
    last_p = reduce_last(0)
    sum_first.share()

    look[...] = jnp.zeros((BLOCKS, 16, HALF), jnp.bfloat16)

    def sum_cols(first_block, block_count):
        return jnp.concatenate(
            [sums[block_rows(first_block + block), :] for block in range(block_count)], axis=1
        )

    def look_of(gradient, moment):
        return round_half(gradient + MOMENTUM * (MOMENTUM * moment + gradient))

    for expert in range(EF):
        look[2 + EF + expert, 0:ROW, :] = look_of(sum_cols(16 + 3 * expert, 3), moment_out[expert])
        if expert > 0:
            look[2 + expert, 0:ROW, :] = look_of(sum_cols(7 + 3 * expert, 3), moment_in[expert])
    reduce_close(0, last_p)
    look[2, 0:ROW, :] = look_of(sum_cols(7, 3), moment_in[0])
    ahead = look_of(sum_cols(0, 6), flat_attn(moment_attn))
    look[0, 0:ROW, :] = ahead[:, :HALF]
    look[1, 0:ROW, :] = ahead[:, HALF:]

    shift = lax.rem(mine, 2) * 4
    own = lax.rem(me, PLANE) == shift
    my_block = me // PLANE
    devices = NZ * PLANE

    def owner_of(block):
        return block * PLANE + shift

    def outgoing(block):
        return pltpu.make_async_remote_copy(
            src_ref=look.at[block], dst_ref=arrived.at[me], send_sem=muon_send.at[block],
            recv_sem=muon_recv, device_id={"dp": owner_of(block)}, device_id_type=MESH_ID,
        )

    for block in range(BLOCKS):

        @pl.when(me != owner_of(block))
        def _():
            outgoing(block).start()

    small_land[mine] = sums[72:88, :]
    small_copies = []
    for away in (1, 2, 3):
        copy = pltpu.make_async_remote_copy(
            src_ref=small_land.at[mine], dst_ref=small_land.at[mine],
            send_sem=small_send.at[away], recv_sem=small_recv.at[away],
            device_id={"tensor": lax.rem(mine + away, 4)}, device_id_type=MESH_ID,
        )
        copy.start()
        small_copies.append(copy)
    sum_first.done()
    grad_normed_one = sum_first.value()
    grad_inputs[0] = (grad_middle + norm_pull(grad_normed_one, normal_one, inv_one, gain_one))[
        :TOKENS
    ]
    for copy in small_copies:
        copy.wait_recv()
    joint = small_land[0] + small_land[1] + small_land[2] + small_land[3]
    small_lane = lax.broadcasted_iota(jnp.int32, (16, LANE), 1)
    small_row = lax.broadcasted_iota(jnp.int32, (16, LANE), 0)
    total[...] = sums[...]
    total[72:88, :] = jnp.where((small_lane == 0) & (small_row < ROW), joint, sums[72:88, :])
    for copy in small_copies:
        copy.wait_send()

    @pl.when(own)
    def _():
        keep = pltpu.make_async_copy(look.at[my_block], arrived.at[me], local_sems.at[0])
        keep.start()
        keep.wait()
        pltpu.make_async_remote_copy(
            src_ref=arrived.at[pl.ds(0, devices - 1)], dst_ref=arrived.at[pl.ds(0, devices - 1)],
            send_sem=back_sem, recv_sem=muon_recv, device_id={"dp": me}, device_id_type=MESH_ID,
        ).wait_recv()

        def gathered(quad, carry):
            picked = arrived[pl.ds(quad * QUAD, QUAD)].reshape(QUAD * 16, HALF)
            rows = pl.ds(pl.multiple_of(quad * QUAD * ROW, 16), QUAD * ROW)
            matrix[rows, :] = round_half(rows_dot(one[...], picked))
            return carry

        lax.fori_loop(0, 2 * NZ, gathered, 0)
        joined = my_block >= 2
        mask = jnp.maximum(mask_ref[...], joined.astype(jnp.float32))
        raw = matrix[...].astype(jnp.float32)
        per_col = jnp.sum(raw * raw, axis=0, keepdims=True)
        square_sum = jnp.dot(
            jnp.broadcast_to(per_col, (8, HALF)), mask, preferred_element_type=jnp.float32,
            precision=lax.Precision.HIGHEST,
        )[0:1]
        matrix[...] = round_half(raw * lax.rsqrt(square_sum + EPSILON))
        for _ in range(NS_ITERS):
            current = matrix[...]
            gram_mat = round_half(contract_rows(current, current) * mask)
            square = rows_dot(gram_mat, gram_mat)
            gram[...] = round_half(NEWTON_B * gram_mat.astype(jnp.float32) + NEWTON_C * square)
            matrix[...] = round_half(
                NEWTON_A * current.astype(jnp.float32) + rows_dot(current, gram[...])
            )

        def scattered(quad, carry):
            rows = pl.ds(pl.multiple_of(quad * QUAD * ROW, 16), QUAD * ROW)
            finished[pl.ds(quad * QUAD, QUAD)] = round_half(
                rows_dot(one_back[...], matrix[rows, :])
            ).reshape(QUAD, 16, HALF)
            return carry

        lax.fori_loop(0, 2 * NZ, scattered, 0)

        def give(target, carry):
            @pl.when(target != me)
            def _():
                pltpu.make_async_remote_copy(
                    src_ref=finished.at[target], dst_ref=result.at[my_block], send_sem=back_sem,
                    recv_sem=ret_sems.at[my_block], device_id={"dp": target},
                    device_id_type=MESH_ID,
                ).start()

            return carry

        lax.fori_loop(0, devices, give, 0)
        stay = pltpu.make_async_copy(finished.at[me], result.at[my_block], local_sems.at[1])
        stay.start()
        stay.wait()
        pltpu.make_async_remote_copy(
            src_ref=finished.at[pl.ds(0, devices - 1)], dst_ref=finished.at[pl.ds(0, devices - 1)],
            send_sem=back_sem, recv_sem=muon_recv, device_id={"dp": me}, device_id_type=MESH_ID,
        ).wait_send()

    for block in range(BLOCKS):

        @pl.when(me != owner_of(block))
        def _():
            outgoing(block).wait_send()
            pltpu.make_async_remote_copy(
                src_ref=result.at[block], dst_ref=result.at[block], send_sem=muon_send.at[block],
                recv_sem=ret_sems.at[block], device_id={"dp": owner_of(block)},
                device_id_type=MESH_ID,
            ).wait_recv()

    near.finish()
    far.finish()
    last_p.wait_send()
    last_e.wait_send()
    for summing in (sum_attn, sum_grad, sum_moe, sum_first):
        summing.finish()


LAG = 3


def half_mask():
    side = np.arange(384) // 192
    return jnp.asarray(side[:, None] == side[None, :], jnp.float32)


def whole_step(inputs, cotangent, routes, gains, router, attn, mats_in, mats_out, moments):
    half, single = jnp.bfloat16, jnp.float32
    shapes = [(PAD, HALF), (PAD, HALF + LANE), (PAD, HALF), (PAD, HALF)]
    lands = []
    for _, rows_a, rows_b, _ in SETS:
        lands += [
            pltpu.VMEM((NX, 2, 4, NY, rows_a, LANE), half),
            pltpu.VMEM((NZ, 2, 2, NY, rows_b, LANE), half),
            pltpu.VMEM((1, 2, 2, NY, rows_a, LANE), half),
            pltpu.VMEM((1, 2, 4, NY, rows_b, LANE), half),
            pltpu.VMEM((rows_a + rows_b, LANE), half),
        ]
    weights = [(WIDE, WIDE), (WIDE, LANE), (EF, WIDE, HALF), (EF, WIDE, HALF)]
    dma = pltpu.SemaphoreType.DMA
    four, one = spread_matrix(4, 48), spread_matrix(1, 16)
    return pl.pallas_call(
        mega_kernel,
        out_shape=[
            jax.ShapeDtypeStruct((1, TOKENS, WIDE), single),
            jax.ShapeDtypeStruct((1, TOKENS, WIDE), single),
            jax.ShapeDtypeStruct((PACK, LANE), single),
            jax.ShapeDtypeStruct((BLOCKS, 16, HALF), half),
        ],
        in_specs=[pl.BlockSpec(memory_space=pl.ANY)] * 2 + vmem_specs(14),
        out_specs=vmem_specs(4),
        scratch_shapes=[
            pltpu.VMEM((PACK, LANE), single),
            pltpu.VMEM((NZ, PLANE, PACK, LANE), half),
        ]
        + [pltpu.VMEM(shape, half) for shape in weights]
        + [
            pltpu.VMEM((TOKENS, WIDE), single),
            pltpu.VMEM((TOKENS, WIDE), single),
            pltpu.VMEM((PAD, WIDE), single),
            pltpu.VMEM((PAD, WIDE), single),
            pltpu.VMEM((3, PAD, PAD), single),
            pltpu.VMEM((EF, PAD, HALF), half),
            pltpu.VMEM((EF, PAD, HALF), half),
        ]
        + [pltpu.VMEM(shape, half) for shape in weights]
        + [pltpu.VMEM((PACK, LANE), single)]
        + lands
        + [pltpu.VMEM((2,) + shape, half) for shape in shapes]
        + [pltpu.VMEM(shape, half) for shape in shapes]
        + [pltpu.VMEM(shape, half) for shape in shapes]
        + [pltpu.VMEM((2,) + shape, half) for shape in shapes]
        + [
            pltpu.VMEM((4, 16, LANE), single),
            pltpu.VMEM((BLOCKS, 16, HALF), half),
            pltpu.VMEM((NZ * PLANE, 16, HALF), half),
            pltpu.VMEM((WIDE, HALF), half),
            pltpu.VMEM((NZ * PLANE, 16, HALF), half),
            pltpu.VMEM((HALF, HALF), half),
            dma((RING_SEMS,)), dma((RING_SEMS,)), dma((RING_SEMS,)), dma((RING_SEMS,)),
            dma((12,)), dma((12,)), dma((4,)), dma((4,)),
            dma((4,)), dma((BLOCKS,)), dma, dma, dma((BLOCKS,)),
        ],
        compiler_params=pltpu.CompilerParams(
            collective_id=0, has_side_effects=True, vmem_limit_bytes=64_000_000
        ),
    )(
        inputs, cotangent, routes, gains, router, attn, mats_in, mats_out, *moments,
        four, one, four.T, one.T, half_mask(),
    )


def finish_kernel(
    total, result, rows_out, rows_grad, gains, router, attn, mats_in, mats_out,
    moment_gains, moment_router, moment_attn, moment_in, moment_out,
    output, grad_inputs, sum_gains, sum_attn, sum_router, sum_in, sum_out,
    gains_new, attn_new, router_new, in_new, out_new,
    gains_moved, attn_moved, router_moved, in_moved, out_moved, sems,
):
    copies = [
        pltpu.make_async_copy(source.at[0], landing.at[:, 0, :], sems.at[index])
        for index, (source, landing) in enumerate(((rows_out, output), (rows_grad, grad_inputs)))
    ]
    for copy in copies:
        copy.start()
    small_step = SMALL_RATE / math.sqrt(NZ * PLANE * TOKENS)

    def columns(first_block, block_count):
        return jnp.concatenate(
            [
                total[(first_block + block) * ROW : (first_block + block + 1) * ROW, :]
                for block in range(block_count)
            ],
            axis=1,
        )

    diagonal = lax.broadcasted_iota(jnp.int32, (ROW, ROW), 0) == lax.broadcasted_iota(
        jnp.int32, (ROW, ROW), 1
    )
    small = columns(6, 1)
    small_sets = (
        (0, 2, gains, moment_gains, sum_gains, gains_new, gains_moved),
        (2, EF, router, moment_router, sum_router, router_new, router_moved),
    )
    for first_lane, count, param, moment, gradient, new, moved in small_sets:
        for index in range(count):
            lane = first_lane + index
            row = slice(index, index + 1)
            value = jnp.sum(
                jnp.where(diagonal, small[:, lane : lane + 1], 0.0), axis=0, keepdims=True
            )
            gradient[row, :] = value
            fresh = MOMENTUM * moment[row, :] + value
            moved[row, :] = fresh
            new[row, :] = param[row, :] - small_step * fresh
    flat = columns(0, 6)
    step = jnp.concatenate([result[0, 0:ROW, :], result[1, 0:ROW, :]], axis=1).astype(jnp.float32)
    for which in range(4):
        wide = slice(which * 192, (which + 1) * 192)
        sum_attn[:, which, :] = flat[:, wide]
        attn_moved[:, which, :] = MOMENTUM * moment_attn[:, which, :] + flat[:, wide]
        attn_new[:, which, :] = attn[:, which, :] - MUON_RATE * step[:, wide]
    for first_block, first_slot, param, moment, gradient, new, moved in (
        (7, 2, mats_in, moment_in, sum_in, in_new, in_moved),
        (16, 2 + EF, mats_out, moment_out, sum_out, out_new, out_moved),
    ):
        for expert in range(EF):
            value = columns(first_block + 3 * expert, 3)
            gradient[expert] = value
            moved[expert] = MOMENTUM * moment[expert] + value
            new[expert] = param[expert] - MUON_RATE * result[
                first_slot + expert, 0:ROW, :
            ].astype(jnp.float32)
    for copy in copies:
        copy.wait()


def finish_step(total, result, rows_out, rows_grad, params, moments):
    single = jnp.float32
    rows = jax.ShapeDtypeStruct((TOKENS, 1, WIDE), single)
    group = [
        jax.ShapeDtypeStruct(shape, single)
        for shape in ((2, ROW), (ROW, 4, 192), (EF, ROW), (EF, ROW, HALF), (EF, ROW, HALF))
    ]
    anywhere = pl.BlockSpec(memory_space=pl.ANY)
    return pl.pallas_call(
        finish_kernel,
        out_shape=[rows, rows] + group * 3,
        in_specs=vmem_specs(14),
        out_specs=[anywhere, anywhere] + vmem_specs(15),
        scratch_shapes=[pltpu.SemaphoreType.DMA((2,))],
    )(total, result, rows_out, rows_grad, *params, *moments)


def shards(
    inputs,
    cotangent,
    norm_gains,
    attn_mats,
    router,
    expert_in,
    expert_out,
    moment_gains,
    moment_attn,
    moment_router,
    moment_in,
    moment_out,
    routes,
):
    def by_rows(value):
        return jnp.transpose(value, (1, 0, 2))

    params = (norm_gains, router.T, by_rows(attn_mats), expert_in, expert_out)
    moments = (moment_gains, moment_router.T, by_rows(moment_attn), moment_in, moment_out)
    rows_out, rows_grad, total, finished = whole_step(
        by_rows(inputs), by_rows(cotangent), routes[0].T, *params, moments[2:]
    )
    rows = finish_step(total, finished, rows_out, rows_grad, params, moments)
    output, grad_inputs = (by_rows(value) for value in rows[:2])
    groups = []
    for first in (2, 7, 12):
        gains, attn, router_rows, left, right = rows[first : first + 5]
        groups += [gains, by_rows(attn), router_rows.T, left, right]
    return (output, grad_inputs, *groups)


def solution(mesh):
    return jax.shard_map(
        shards,
        mesh=mesh,
        in_specs=(
            P("dp", None, None),
            P("dp", None, None),
            P(None, "dp"),
            P(None, "dp", "tensor"),
            P("dp", None),
            P(None, "dp", "tensor"),
            P(None, "dp", "tensor"),
            P(None, "dp"),
            P(None, "dp", "tensor"),
            P("dp", None),
            P(None, "dp", "tensor"),
            P(None, "dp", "tensor"),
            P("dp", None, None),
        ),
        out_specs=(
            P("dp", None, None),
            P("dp", None, None),
            P(None, "dp"),
            P(None, "dp", "tensor"),
            P("dp", None),
            P(None, "dp", "tensor"),
            P(None, "dp", "tensor"),
            P(None, "dp"),
            P(None, "dp", "tensor"),
            P("dp", None),
            P(None, "dp", "tensor"),
            P(None, "dp", "tensor"),
            P(None, "dp"),
            P(None, "dp", "tensor"),
            P("dp", None),
            P(None, "dp", "tensor"),
            P(None, "dp", "tensor"),
        ),
        check_vma=False,
    )
```

```python
import math

import jax
import jax.numpy as jnp
import numpy as np
from jax import lax
from jax.experimental import pallas as pl
from jax.experimental.pallas import tpu as pltpu
from jax.sharding import PartitionSpec as P

HEAD_DIM = 64
EF = 3
NS_ITERS = 3
CAP = 197


EPSILON = 1e-06
MOMENTUM = 0.9
MUON_RATE = 0.5
SMALL_RATE = 0.5
NEWTON_A = 3.4445
NEWTON_B = -4.775
NEWTON_C = 2.0315
ROOT_HALF = 0.7071067811865476
INV_ROOT_TAU = 0.3989422804014327


def round_half(operand):
    return operand.astype(jnp.bfloat16)


def settle(operand):
    return lax.optimization_barrier(operand.astype(jnp.bfloat16))


def to_single(operand):
    return operand.astype(jnp.float32)


def contract_rows(left_mat, right_mat):
    return lax.dot_general(
        left_mat, right_mat, (((0,), (0,)), ((), ())), preferred_element_type=jnp.float32
    )


def contract_cols(left_mat, right_mat):
    return lax.dot_general(
        left_mat, right_mat, (((1,), (1,)), ((), ())), preferred_element_type=jnp.float32
    )


NZ, NX, NY = 8, 4, 2
ROW = 12
LANE = 128
PACK = 304
PLANE = NX * NY
QUAD = PLANE // 2
BLOCKS = 8
MESH_ID = pl.DeviceIdType.MESH
GROUPS = ((0, 4), (4, 4), (8, 4), (12, 4), (16, 4), (20, 4), (24, 1))


def spread_matrix(block_count, padded):
    table = np.zeros((block_count * QUAD * ROW, QUAD * padded), np.float32)
    for block in range(block_count):
        for member in range(QUAD):
            for row in range(ROW):
                table[
                    block * QUAD * ROW + member * ROW + row, member * padded + block * ROW + row
                ] = 1.0
    return jnp.asarray(table, jnp.bfloat16)


def place_of(me):
    return me // PLANE, lax.rem(me // NY, NX), lax.rem(me, NY)


def dp_index(z, x, y):
    return z * PLANE + x * NY + y


def wrap(value, count):
    return lax.rem(value + 2 * count, count)


def neighbours(me):
    z, x, y = place_of(me)
    return (
        dp_index(wrap(z + 1, NZ), x, y),
        dp_index(wrap(z - 1, NZ), x, y),
        dp_index(z, wrap(x + 1, NX), y),
        dp_index(z, wrap(x - 1, NX), y),
        dp_index(z, x, 1 - y),
    )


def send(source, landing, send_sem, recv_sem, target):
    copy = pltpu.make_async_remote_copy(
        src_ref=source,
        dst_ref=landing,
        send_sem=send_sem,
        recv_sem=recv_sem,
        device_id={"dp": target},
        device_id_type=MESH_ID,
    )
    copy.start()
    return copy


class GatherRing:
    def __init__(self, chunk, position, count, up, down, send_sems, recv_sems, base):
        self.chunk, self.position, self.count = chunk, position, count
        self.up, self.down = up, down
        self.send_sems, self.recv_sems, self.base = send_sems, recv_sems, base
        self.copies = []

    def start(self, step):
        half = step == self.count // 2 - 1
        pair = []
        for side, (sign, target) in enumerate(((-1, self.up), (1, self.down))):
            part = self.chunk(wrap(self.position + sign * step, self.count), side if half else None)
            slot = self.base + 2 * step + side
            pair.append(send(part, part, self.send_sems.at[slot], self.recv_sems.at[slot], target))
        self.copies.append(pair)

    def arrive(self, step):
        for copy in self.copies[step]:
            copy.wait_recv()

    def finish(self):
        for pair in self.copies:
            for copy in pair:
                copy.wait_send()


def vmem_specs(count):
    return [pl.BlockSpec(memory_space=pltpu.VMEM)] * count


class ReduceRing:
    def __init__(self, chunk, landing, position, count, up, down, send_sems, recv_sems, base):
        self.chunk, self.landing = chunk, landing
        self.position, self.count = position, count
        self.up, self.down = up, down
        self.send_sems, self.recv_sems, self.base = send_sems, recv_sems, base
        self.copies = []

    def start(self, step):
        away = self.count // 2 - step
        pair = []
        for side, (sign, target) in enumerate(((1, self.up), (-1, self.down))):
            half = side if step == 0 else None
            part = self.chunk(wrap(self.position + sign * away, self.count), half)
            slot = self.base + 2 * step + side
            pair.append(
                send(
                    part,
                    self.landing(side, step, half),
                    self.send_sems.at[slot],
                    self.recv_sems.at[slot],
                    target,
                )
            )
        self.copies.append(pair)

    def arrive(self, step):
        for copy in self.copies[step]:
            copy.wait_recv()
        away = self.count // 2 - 1 - step
        if away == 0:
            mine = self.chunk(self.position, None)
            mine[...] = (
                mine[...].astype(jnp.float32)
                + self.landing(0, step, None)[...].astype(jnp.float32)
                + self.landing(1, step, None)[...].astype(jnp.float32)
            ).astype(jnp.bfloat16)
            return
        for side, sign in ((0, 1), (1, -1)):
            half = side if step == 0 else None
            mine = self.chunk(wrap(self.position + sign * away, self.count), half)
            mine[...] = (
                mine[...].astype(jnp.float32)
                + self.landing(side, step, half)[...].astype(jnp.float32)
            ).astype(jnp.bfloat16)

    def finish(self):
        for pair in self.copies:
            for copy in pair:
                copy.wait_send()


TOKENS = 197
PAD = 208
WIDE = 768
HALF = 384
ERF_TOP = (
    0.00022905065861350646, 0.0034082910107109506, 0.050955695062380861,
    0.18520832239976145, 1.128379143519084,
)
ERF_BOTTOM = (
    -1.1791602954361697e-7, 0.000023547966471313185, 0.0010179625278914885,
    0.014070470171167667, 0.11098505178285362, 0.49746925110067538, 1.0,
)


def rows_dot(left_mat, right_mat):
    return jnp.dot(left_mat, right_mat, preferred_element_type=jnp.float32)


def mean_of(value):
    return jnp.sum(value, axis=-1, keepdims=True) * (1.0 / WIDE)


def norm_parts(row_data):
    center = row_data - mean_of(row_data)
    inv_std = lax.rsqrt(mean_of(center * center) + EPSILON)
    return center * inv_std, inv_std


def norm_pull(grad_result, normal, inv_std, gain_row):
    scaled = grad_result * gain_row
    return inv_std * (scaled - mean_of(scaled) - normal * mean_of(scaled * normal))


class TensorSum:
    def __init__(self, part, land_core, land_chip, final, send_sems, recv_sems, base):
        self.part, self.land_core, self.land_chip, self.final = part, land_core, land_chip, final
        self.send_sems, self.recv_sems, self.base = send_sems, recv_sems, base
        mine = lax.axis_index("tensor")
        self.core = lax.rem(mine, 2)
        self.other_core = mine + 1 - 2 * self.core
        self.other_chip = lax.rem(mine + 2, 4)
        self.copies = []

    def put(self, source, landing, target):
        slot = self.base + len(self.copies)
        copy = pltpu.make_async_remote_copy(
            src_ref=source,
            dst_ref=landing,
            send_sem=self.send_sems.at[slot],
            recv_sem=self.recv_sems.at[slot],
            device_id={"tensor": target},
            device_id_type=MESH_ID,
        )
        copy.start()
        self.copies.append(copy)

    def begin(self):
        self.put(self.part.at[1 - self.core], self.land_core, self.other_core)

    def across(self):
        self.copies[0].wait_recv()
        mine = self.part.at[self.core]
        mine[...] = (
            mine[...].astype(jnp.float32) + self.land_core[...].astype(jnp.float32)
        ).astype(jnp.bfloat16)
        self.put(mine, self.land_chip, self.other_chip)

    def share(self):
        self.copies[1].wait_recv()
        mine = self.final.at[self.core]
        mine[...] = (
            self.part[self.core].astype(jnp.float32) + self.land_chip[...].astype(jnp.float32)
        ).astype(jnp.bfloat16)
        self.put(mine, mine, self.other_core)

    def done(self):
        self.copies[2].wait_recv()

    def value(self):
        return jnp.concatenate(
            [self.final[0][:, :HALF], self.final[1][:, :HALF]], axis=1
        ).astype(jnp.float32)

    def finish(self):
        for copy in self.copies:
            copy.wait_send()


def erf_of(value):
    bounded = jnp.clip(value, -3.832506856900711, 3.832506856900711)
    square = bounded * bounded
    top = jnp.full_like(square, ERF_TOP[0])
    for factor in ERF_TOP[1:]:
        top = top * square + factor
    bottom = jnp.full_like(square, ERF_BOTTOM[0])
    for factor in ERF_BOTTOM[1:]:
        bottom = bottom * square + factor
    return bounded * top / bottom


class Rounds:
    def __init__(self, queue):
        self.queue, self.turn = queue, 0
        self.turns = 1 + max(begin + ring.count // 2 for ring, begin in queue)

    def advance(self):
        for ring, begin in self.queue:
            step = self.turn - begin
            if 1 <= step <= ring.count // 2:
                ring.arrive(step - 1)
            if 0 <= step < ring.count // 2:
                ring.start(step)
        self.turn += 1

    def finish(self):
        for ring, _ in self.queue:
            ring.finish()


SETS = ((0, 48, 48, GROUPS[:2]), (96, 96, 112, GROUPS[2:]))
RING_SEMS = 2 * 77


def mega_kernel(
    inputs, cotangent, routes, gains, router, attn_mats, mats_in, mats_out,
    moment_attn, moment_in, moment_out, four, one, four_back, one_back, mask_ref,
    output, grad_inputs, total, result,
    packed, slots, attn_half, small_half, in_half, out_half,
    raw_in, raw_cot, rows_in, rows_cot, prob_all, hidden_all, grad_pre_all,
    grad_attn, grad_small, grad_in, grad_out, sums,
    land_az_p, land_bx_p, land_ax_p, land_bz_p, land_y_p,
    land_az_e, land_bx_e, land_ax_e, land_bz_e, land_y_e,
    part_a, part_b, part_c, part_d, core_a, core_b, core_c, core_d,
    chip_a, chip_b, chip_c, chip_d, final_a, final_b, final_c, final_d,
    small_land, look, arrived, matrix, finished, gram,
    gather_send, gather_recv, reduce_send, reduce_recv, send_sems, recv_sems,
    small_send, small_recv, local_sems, muon_send, muon_recv, back_sem, ret_sems,
):
    me = lax.axis_index("dp")
    mine = lax.axis_index("tensor")
    z, x, y = place_of(me)
    up_z, down_z, up_x, down_x, other_y = neighbours(me)
    loads = []
    for index, (source, held) in enumerate(((inputs, raw_in), (cotangent, raw_cot))):
        copy = pltpu.make_async_copy(source.at[:, 0, :], held, local_sems.at[2 + index])
        copy.start()
        loads.append(copy)
    barrier = pltpu.get_barrier_semaphore()
    for target in (up_z, down_z, up_x, down_x, other_y):
        pl.semaphore_signal(barrier, inc=1, device_id={"dp": target}, device_id_type=MESH_ID)
    for away in (1, 2, 3):
        pl.semaphore_signal(
            barrier, inc=1, device_id={"tensor": lax.rem(mine + away, 4)}, device_id_type=MESH_ID
        )

    diagonal = lax.broadcasted_iota(jnp.int32, (ROW, ROW), 0) == lax.broadcasted_iota(
        jnp.int32, (ROW, ROW), 1
    )
    lanes = lax.broadcasted_iota(jnp.int32, (ROW, LANE), 1)

    def upright(row):
        return jnp.sum(jnp.where(diagonal, row, 0.0), axis=1, keepdims=True)

    def flat_attn(ref):
        return jnp.concatenate([ref[:, which, :] for which in range(4)], axis=1)

    def block_rows(block):
        return slice(block * ROW, (block + 1) * ROW)

    flat = flat_attn(attn_mats)
    for block in range(6):
        packed[block_rows(block), :] = flat[:, block * LANE : (block + 1) * LANE]
    small = jnp.zeros((ROW, LANE), jnp.float32)
    for lane, (source, row) in enumerate(((gains, 0), (gains, 1), (router, 0), (router, 1), (router, 2))):
        small = small + jnp.where(lanes == lane, upright(source[row : row + 1, :]), 0.0)
    packed[block_rows(6), :] = small
    for index in range(9):
        column = (index % 3) * LANE
        packed[block_rows(7 + index), :] = mats_in[index // 3, :, column : column + LANE]
        packed[block_rows(16 + index), :] = mats_out[index // 3, :, column : column + LANE]
    packed[25 * ROW : PACK, :] = jnp.zeros((PACK - 25 * ROW, LANE), jnp.float32)
    slots[z, NY * x + y] = round_half(packed[...])
    pl.semaphore_wait(barrier, 8)

    def across_x(plane, rows, wide):
        def chunk(index, half):
            if half is None:
                return slots.at[plane, pl.ds(NY * index, NY), rows]
            return slots.at[plane, pl.ds(NY * index + half, 1), rows]

        return chunk

    def across_z(column, rows, wide):
        def chunk(index, half):
            if half is None:
                return slots.at[index, pl.ds(NY * column, NY), rows]
            return slots.at[index, pl.ds(NY * column + half, 1), rows]

        return chunk

    def sem_bases(first):
        while True:
            yield first
            first += 4

    def gather_rounds(which):
        low, rows_a, rows_b, _ = SETS[which]
        head, rest = pl.ds(low, rows_a), pl.ds(low + rows_a, rows_b)
        base = sem_bases(77 * which + 1)

        def ring_x(plane, rows):
            return GatherRing(
                across_x(plane, rows, None), x, NX, up_x, down_x, gather_send, gather_recv,
                next(base),
            )

        def ring_z(column, rows):
            first_sem = next(base)
            next(base)
            return GatherRing(
                across_z(column, rows, None), z, NZ, up_z, down_z, gather_send, gather_recv,
                first_sem,
            )

        queue = [
            (ring_x(z, head), 0), (ring_z(x, rest), 0), (ring_z(x, head), 0), (ring_x(z, rest), 0)
        ]
        for away in (1, NZ - 1):
            queue.append((ring_x(wrap(z + away, NZ), rest), 1))
        for away in (1, NX - 1):
            queue.append((ring_z(wrap(x + away, NX), head), 1))
        queue.append((ring_z(wrap(x + 2, NX), head), 2))
        for away in (2, NZ - 2, 3, NZ - 3, 4):
            queue.append((ring_x(wrap(z + away, NZ), rest), min(away, NZ - away)))
        return Rounds(queue)

    def gather_first(which):
        low, rows_a, rows_b, _ = SETS[which]
        own = slots.at[z, NY * x + y, pl.ds(low, rows_a + rows_b)]
        return send(own, own, gather_send.at[77 * which], gather_recv.at[77 * which], other_y)

    lands = (
        (land_az_p, land_bx_p, land_ax_p, land_bz_p, land_y_p),
        (land_az_e, land_bx_e, land_ax_e, land_bz_e, land_y_e),
    )

    def landing_in(held, which):
        def landing(side, step, half):
            if half is None:
                return held.at[which, side, step]
            return held.at[which, side, step, pl.ds(half, 1)]

        return landing

    def reduce_rounds(which):
        low, rows_a, rows_b, _ = SETS[which]
        land_az, land_bx, land_ax, land_bz, _ = lands[which]
        head, rest = pl.ds(low, rows_a), pl.ds(low + rows_a, rows_b)
        base = sem_bases(77 * which + 1)

        def ring_x(plane, rows, held, index):
            return ReduceRing(
                across_x(plane, rows, None), landing_in(held, index), x, NX, up_x, down_x,
                reduce_send, reduce_recv, next(base),
            )

        def ring_z(column, rows, held, index):
            first_sem = next(base)
            next(base)
            return ReduceRing(
                across_z(column, rows, None), landing_in(held, index), z, NZ, up_z, down_z,
                reduce_send, reduce_recv, first_sem,
            )

        queue = []
        for index, away in enumerate((4, 3, NZ - 3, 2, NZ - 2, 1, NZ - 1, 0)):
            queue.append(
                (ring_x(wrap(z + away, NZ), rest, land_bx, index), 4 - min(away, NZ - away))
            )
        for index, (away, begin) in enumerate(((2, 0), (1, 1), (NX - 1, 1), (0, 2))):
            queue.append((ring_z(wrap(x + away, NX), head, land_az, index), begin))
        queue.append((ring_x(z, head, land_ax, 0), 4))
        queue.append((ring_z(x, rest, land_bz, 0), 2))
        return Rounds(queue)

    def reduce_last(which):
        low, rows_a, rows_b, _ = SETS[which]
        return send(
            slots.at[z, NY * x + 1 - y, pl.ds(low, rows_a + rows_b)], lands[which][4],
            reduce_send.at[77 * which], reduce_recv.at[77 * which], other_y,
        )

    def reduce_close(which, copy):
        low, rows_a, rows_b, _ = SETS[which]
        rows = slice(low, low + rows_a + rows_b)
        copy.wait_recv()
        sums[rows, :] = slots[z, NY * x + y, rows].astype(jnp.float32) + lands[which][4][
            ...
        ].astype(jnp.float32)

    def place(refs, block):
        attn_ref, small_ref, in_ref, out_ref = refs
        if block < 6:
            return attn_ref, None, block * LANE
        if block == 6:
            return small_ref, None, 0
        index = (block - 7) % 9
        return (in_ref if block < 16 else out_ref), index // 3, (index % 3) * LANE

    def compact(which):
        refs = (attn_half, small_half, in_half, out_half)

        def body(plane, carry):
            rows = pl.ds(pl.multiple_of(plane * PLANE * ROW, 32), PLANE * ROW)
            for first_block, block_count in SETS[which][3]:
                padded = 48 if block_count == 4 else 16
                picked = slots[plane, :, pl.ds(first_block * ROW, padded), :]
                sides = [
                    picked[side * QUAD : (side + 1) * QUAD].reshape(QUAD * padded, LANE)
                    for side in range(2)
                ]
                moved = rows_dot(
                    (four if block_count == 4 else one)[...], jnp.concatenate(sides, axis=1)
                ).astype(jnp.bfloat16)
                for block in range(block_count):
                    part = moved[block * QUAD * ROW : (block + 1) * QUAD * ROW]
                    value = jnp.concatenate([part[:, :LANE], part[:, LANE:]], axis=0)
                    ref, lead, column = place(refs, first_block + block)
                    if lead is None:
                        ref[rows, column : column + LANE] = value
                    else:
                        ref[lead, rows, column : column + LANE] = value
            return carry

        lax.fori_loop(0, NZ, body, 0)

    def expand(which):
        refs = (grad_attn, grad_small, grad_in, grad_out)

        def body(plane, carry):
            rows = pl.ds(pl.multiple_of(plane * PLANE * ROW, 32), PLANE * ROW)
            for first_block, block_count in SETS[which][3]:
                padded = 48 if block_count == 4 else 16
                stacked = []
                for block in range(block_count):
                    ref, lead, column = place(refs, first_block + block)
                    if lead is None:
                        part = ref[rows, column : column + LANE]
                    else:
                        part = ref[lead, rows, column : column + LANE]
                    stacked.append(
                        jnp.concatenate([part[: QUAD * ROW], part[QUAD * ROW :]], axis=1)
                    )
                moved = rows_dot(
                    (four_back if block_count == 4 else one_back)[...],
                    stacked[0] if block_count == 1 else jnp.concatenate(stacked, axis=0),
                ).astype(jnp.bfloat16)
                for side in range(2):
                    slots[
                        plane, side * QUAD : (side + 1) * QUAD,
                        pl.ds(first_block * ROW, padded), :,
                    ] = moved[:, side * LANE : (side + 1) * LANE].reshape(QUAD, padded, LANE)
            return carry

        lax.fori_loop(0, NZ, body, 0)

    first_p, first_e = gather_first(0), gather_first(1)
    near, far = gather_rounds(0), gather_rounds(1)
    for copy, raw, held in zip(loads, (raw_in, raw_cot), (rows_in, rows_cot)):
        copy.wait()
        held[PAD - 16 : PAD, :] = jnp.zeros((16, WIDE), jnp.float32)
        held[0:TOKENS, :] = raw[...]
    row_in = rows_in[...]
    normal_one, inv_one = norm_parts(row_in)
    first_p.wait_recv()
    for turn in range(near.turns):
        near.advance()
        if turn == LAG - 1:
            first_e.wait_recv()
        if turn >= LAG:
            far.advance()
    compact(0)

    sum_attn = TensorSum(part_a, core_a, chip_a, final_a, send_sems, recv_sems, 0)
    sum_grad = TensorSum(part_b, core_b, chip_b, final_b, send_sems, recv_sems, 3)
    sum_moe = TensorSum(part_c, core_c, chip_c, final_c, send_sems, recv_sems, 6)
    sum_first = TensorSum(part_d, core_d, chip_d, final_d, send_sems, recv_sems, 9)

    def fill(part, value):
        part[0, :, :HALF] = value[:, :HALF].astype(jnp.bfloat16)
        part[1, :, :HALF] = value[:, HALF:].astype(jnp.bfloat16)

    gain_rows = jnp.transpose(small_half[...].astype(jnp.float32))
    gain_one, gain_two = gain_rows[0:1], gain_rows[1:2]
    normed_one = round_half(normal_one * gain_one)
    qkv = round_half(rows_dot(normed_one, attn_half[:, : 3 * 192]))
    if far.turn < far.turns:
        far.advance()
    row_id = lax.broadcasted_iota(jnp.int32, (PAD, PAD), 0)
    col_id = lax.broadcasted_iota(jnp.int32, (PAD, PAD), 1)
    scale = 1.0 / math.sqrt(HEAD_DIM)

    def head_of(value, which, head):
        start = which * 192 + head * HEAD_DIM
        return value[:, start : start + HEAD_DIM]

    head_rows = []
    for head in range(3):
        scores = contract_cols(head_of(qkv, 0, head), head_of(qkv, 1, head)) * scale
        scores = jnp.where(col_id < TOKENS, scores, -1e30)
        peak = jnp.max(scores, axis=-1, keepdims=True)
        log_total = peak + jnp.log(jnp.sum(jnp.exp(scores - peak), axis=-1, keepdims=True))
        prob = jnp.where(row_id < TOKENS, jnp.exp(scores - log_total), 0.0)
        prob_all[head] = prob
        head_rows.append(round_half(rows_dot(round_half(prob), head_of(qkv, 2, head))))
    blank = jnp.zeros((PAD, HEAD_DIM), jnp.bfloat16)
    attn_rows = jnp.concatenate([blank] + head_rows, axis=1)
    fill(part_a, contract_cols(attn_rows, attn_half[:, 512:768]))
    sum_attn.begin()
    if far.turn < far.turns:
        far.advance()
    sum_attn.across()
    if far.turn < far.turns:
        far.advance()
    sum_attn.share()
    while far.turn < far.turns:
        far.advance()
    sum_attn.done()
    middle = row_in + sum_attn.value()
    normal_two, inv_two = norm_parts(middle)
    normed_two = round_half(normal_two * gain_two)
    compact(1)
    logits = rows_dot(normed_two, small_half[...])
    expert_id = lax.broadcasted_iota(jnp.int32, (16, TOKENS), 0)
    lane_id = lax.broadcasted_iota(jnp.int32, (16, LANE), 1) - 2
    spread = (lane_id == lax.broadcasted_iota(jnp.int32, (16, LANE), 0)).astype(jnp.bfloat16)
    gap = jnp.zeros((16, PAD - TOKENS), jnp.float32)

    def chosen_mask(which):
        hit = (expert_id == routes[which : which + 1, :]).astype(jnp.float32)
        return contract_rows(round_half(jnp.concatenate([hit, gap], axis=1)), spread)

    hot_first, hot_second = chosen_mask(0), chosen_mask(1)
    sign = hot_first - hot_second
    difference = jnp.sum(logits * sign, axis=-1, keepdims=True)
    gate_first = jax.nn.sigmoid(difference)
    gate_second = jax.nn.sigmoid(-difference)
    gates = gate_first * hot_first + gate_second * hot_second
    cot = rows_cot[...]
    moe_part = jnp.zeros((PAD, WIDE), jnp.float32)
    choice_part = jnp.zeros((PAD, 1), jnp.float32)
    grad_part = jnp.zeros((PAD, WIDE), jnp.float32)
    for expert in range(EF):
        gate = gates[:, 2 + expert : 3 + expert]
        pre_act = rows_dot(normed_two, in_half[expert])
        inner = 1.0 + erf_of(pre_act * ROOT_HALF)
        hidden = round_half(0.5 * pre_act * inner)
        slope = 0.5 * inner + pre_act * INV_ROOT_TAU * jnp.exp(-0.5 * pre_act * pre_act)
        expert_rows = contract_cols(hidden, out_half[expert])
        moe_part = moe_part + gate * expert_rows
        choice_part = choice_part + sign[:, 2 + expert : 3 + expert] * jnp.sum(
            cot * expert_rows, axis=-1, keepdims=True
        )
        grad_expert = round_half(gate * cot)
        grad_pre = round_half(rows_dot(grad_expert, out_half[expert]) * slope)
        grad_part = grad_part + contract_cols(grad_pre, in_half[expert])
        hidden_all[expert] = hidden
        grad_pre_all[expert] = grad_pre
    fill(part_b, grad_part)
    extra = lax.broadcasted_iota(jnp.int32, (PAD, LANE), 1) == 0
    part_b[0, :, HALF:] = jnp.where(extra, choice_part, 0.0).astype(jnp.bfloat16)
    part_b[1, :, HALF:] = jnp.zeros((PAD, LANE), jnp.bfloat16)
    sum_grad.begin()
    fill(part_c, moe_part)
    near.finish()
    far.finish()
    first_p.wait_send()
    first_e.wait_send()
    for expert in range(EF):
        grad_in[expert] = round_half(contract_rows(normed_two, grad_pre_all[expert]))
    sum_grad.across()
    for expert in range(EF):
        gate = gates[:, 2 + expert : 3 + expert]
        grad_out[expert] = round_half(contract_rows(round_half(gate * cot), hidden_all[expert]))
    sum_grad.share()
    expand(1)
    far = reduce_rounds(1)
    far.advance()
    sum_moe.begin()
    sum_grad.done()
    choice = final_b[0, :, HALF : HALF + 1].astype(jnp.float32)
    grad_first = choice * gate_first * gate_second
    grad_logits = round_half(grad_first * sign)
    grad_normed_two = sum_grad.value() + contract_cols(grad_logits, small_half[...])
    grad_middle = cot + norm_pull(grad_normed_two, normal_two, inv_two, gain_two)
    far.advance()
    grad_gain_two = jnp.sum(grad_normed_two * normal_two, axis=0, keepdims=True)
    router_part = contract_rows(normed_two, grad_logits)
    grad_mid_half = round_half(grad_middle)
    grad_heads = round_half(rows_dot(grad_mid_half, attn_half[:, 512:768]))
    sum_moe.across()
    parts = [[], [], []]
    for head in range(3):
        grad_head = grad_heads[:, HEAD_DIM * (head + 1) : HEAD_DIM * (head + 2)]
        prob = prob_all[head]
        grad_prob = contract_cols(grad_head, head_of(qkv, 2, head))
        parts[2].append(round_half(contract_rows(round_half(prob), grad_head)))
        spread = jnp.sum(prob * grad_prob, axis=-1, keepdims=True)
        grad_scores = round_half(prob * (grad_prob - spread) * scale)
        parts[0].append(round_half(rows_dot(grad_scores, head_of(qkv, 1, head))))
        parts[1].append(round_half(contract_rows(grad_scores, head_of(qkv, 0, head))))
        if head == 2:
            far.advance()
    grad_qkv = jnp.concatenate(parts[0] + parts[1] + parts[2] + [blank] * 3, axis=1)
    first_part = contract_cols(grad_qkv, attn_half[...])
    fill(part_d, first_part)
    grad_attn[:, :512] = round_half(contract_rows(normed_one, grad_qkv[:, :512]))
    grad_attn[:, 512:] = round_half(
        contract_rows(normed_one, grad_qkv[:, 512:]) + contract_rows(grad_mid_half, attn_rows)
    )
    grad_gain_one = jnp.sum(first_part * normal_one, axis=0, keepdims=True)
    gain_id = lax.broadcasted_iota(jnp.int32, (LANE, WIDE), 0)
    gain_block = jnp.where(
        gain_id == 0, grad_gain_one, jnp.where(gain_id == 1, grad_gain_two, 0.0)
    )
    grad_small[...] = round_half(jnp.transpose(gain_block) + router_part)
    expand(0)
    near = reduce_rounds(0)
    near.advance()
    sum_first.begin()
    sum_moe.share()
    while near.turn < near.turns:
        near.advance()
        if far.turn < far.turns:
            far.advance()
        if near.turn == 3:
            sum_first.across()
    while far.turn < far.turns:
        far.advance()
    last_p = reduce_last(0)
    last_e = reduce_last(1)
    sum_first.share()
    sum_moe.done()
    output[0] = (middle + sum_moe.value())[:TOKENS]
    reduce_close(1, last_e)

    look[...] = jnp.zeros((BLOCKS, 16, HALF), jnp.bfloat16)

    def sum_cols(first_block, block_count):
        return jnp.concatenate(
            [sums[block_rows(first_block + block), :] for block in range(block_count)], axis=1
        )

    def look_of(gradient, moment):
        return round_half(gradient + MOMENTUM * (MOMENTUM * moment + gradient))

    for expert in range(EF):
        look[2 + EF + expert, 0:ROW, :] = look_of(sum_cols(16 + 3 * expert, 3), moment_out[expert])
        if expert > 0:
            look[2 + expert, 0:ROW, :] = look_of(sum_cols(7 + 3 * expert, 3), moment_in[expert])
    shift = lax.rem(mine, 2) * 4
    own = lax.rem(me, PLANE) == shift
    my_block = me // PLANE
    devices = NZ * PLANE

    def owner_of(block):
        return block * PLANE + shift

    def outgoing(block):
        return pltpu.make_async_remote_copy(
            src_ref=look.at[block], dst_ref=arrived.at[me], send_sem=muon_send.at[block],
            recv_sem=muon_recv, device_id={"dp": owner_of(block)}, device_id_type=MESH_ID,
        )

    for block in range(3, BLOCKS):

        @pl.when(me != owner_of(block))
        def _():
            outgoing(block).start()

    reduce_close(0, last_p)
    look[2, 0:ROW, :] = look_of(sum_cols(7, 3), moment_in[0])
    ahead = look_of(sum_cols(0, 6), flat_attn(moment_attn))
    look[0, 0:ROW, :] = ahead[:, :HALF]
    look[1, 0:ROW, :] = ahead[:, HALF:]

    for block in range(3):

        @pl.when(me != owner_of(block))
        def _():
            outgoing(block).start()

    small_land[mine] = sums[72:88, :]
    small_copies = []
    for away in (1, 2, 3):
        copy = pltpu.make_async_remote_copy(
            src_ref=small_land.at[mine], dst_ref=small_land.at[mine],
            send_sem=small_send.at[away], recv_sem=small_recv.at[away],
            device_id={"tensor": lax.rem(mine + away, 4)}, device_id_type=MESH_ID,
        )
        copy.start()
        small_copies.append(copy)
    sum_first.done()
    grad_normed_one = sum_first.value()
    grad_inputs[0] = (grad_middle + norm_pull(grad_normed_one, normal_one, inv_one, gain_one))[
        :TOKENS
    ]
    for copy in small_copies:
        copy.wait_recv()
    joint = small_land[0] + small_land[1] + small_land[2] + small_land[3]
    small_lane = lax.broadcasted_iota(jnp.int32, (16, LANE), 1)
    small_row = lax.broadcasted_iota(jnp.int32, (16, LANE), 0)
    total[...] = sums[...]
    total[72:88, :] = jnp.where((small_lane == 0) & (small_row < ROW), joint, sums[72:88, :])
    for copy in small_copies:
        copy.wait_send()

    @pl.when(own)
    def _():
        keep = pltpu.make_async_copy(look.at[my_block], arrived.at[me], local_sems.at[0])
        keep.start()
        keep.wait()
        pltpu.make_async_remote_copy(
            src_ref=arrived.at[pl.ds(0, devices - 1)], dst_ref=arrived.at[pl.ds(0, devices - 1)],
            send_sem=back_sem, recv_sem=muon_recv, device_id={"dp": me}, device_id_type=MESH_ID,
        ).wait_recv()

        def gathered(quad, carry):
            picked = arrived[pl.ds(quad * QUAD, QUAD)].reshape(QUAD * 16, HALF)
            rows = pl.ds(pl.multiple_of(quad * QUAD * ROW, 16), QUAD * ROW)
            matrix[rows, :] = round_half(rows_dot(one[...], picked))
            return carry

        lax.fori_loop(0, 2 * NZ, gathered, 0)
        joined = my_block >= 2
        mask = jnp.maximum(mask_ref[...], joined.astype(jnp.float32))
        raw = matrix[...].astype(jnp.float32)
        per_col = jnp.sum(raw * raw, axis=0, keepdims=True)
        square_sum = jnp.dot(
            jnp.broadcast_to(per_col, (8, HALF)), mask, preferred_element_type=jnp.float32,
            precision=lax.Precision.HIGHEST,
        )[0:1]
        matrix[...] = round_half(raw * lax.rsqrt(square_sum + EPSILON))
        for _ in range(NS_ITERS):
            current = matrix[...]
            gram_mat = round_half(contract_rows(current, current) * mask)
            square = rows_dot(gram_mat, gram_mat)
            gram[...] = round_half(NEWTON_B * gram_mat.astype(jnp.float32) + NEWTON_C * square)
            matrix[...] = round_half(
                NEWTON_A * current.astype(jnp.float32) + rows_dot(current, gram[...])
            )

        def scattered(quad, carry):
            rows = pl.ds(pl.multiple_of(quad * QUAD * ROW, 16), QUAD * ROW)
            finished[pl.ds(quad * QUAD, QUAD)] = round_half(
                rows_dot(one_back[...], matrix[rows, :])
            ).reshape(QUAD, 16, HALF)
            return carry

        lax.fori_loop(0, 2 * NZ, scattered, 0)

        def give(target, carry):
            @pl.when(target != me)
            def _():
                pltpu.make_async_remote_copy(
                    src_ref=finished.at[target], dst_ref=result.at[my_block], send_sem=back_sem,
                    recv_sem=ret_sems.at[my_block], device_id={"dp": target},
                    device_id_type=MESH_ID,
                ).start()

            return carry

        lax.fori_loop(0, devices, give, 0)
        stay = pltpu.make_async_copy(finished.at[me], result.at[my_block], local_sems.at[1])
        stay.start()
        stay.wait()
        pltpu.make_async_remote_copy(
            src_ref=finished.at[pl.ds(0, devices - 1)], dst_ref=finished.at[pl.ds(0, devices - 1)],
            send_sem=back_sem, recv_sem=muon_recv, device_id={"dp": me}, device_id_type=MESH_ID,
        ).wait_send()

    for block in range(BLOCKS):

        @pl.when(me != owner_of(block))
        def _():
            outgoing(block).wait_send()
            pltpu.make_async_remote_copy(
                src_ref=result.at[block], dst_ref=result.at[block], send_sem=muon_send.at[block],
                recv_sem=ret_sems.at[block], device_id={"dp": owner_of(block)},
                device_id_type=MESH_ID,
            ).wait_recv()

    near.finish()
    far.finish()
    last_p.wait_send()
    last_e.wait_send()
    for summing in (sum_attn, sum_grad, sum_moe, sum_first):
        summing.finish()


LAG = 3


def half_mask():
    side = np.arange(384) // 192
    return jnp.asarray(side[:, None] == side[None, :], jnp.float32)


def whole_step(inputs, cotangent, routes, gains, router, attn, mats_in, mats_out, moments):
    half, single = jnp.bfloat16, jnp.float32
    shapes = [(PAD, HALF), (PAD, HALF + LANE), (PAD, HALF), (PAD, HALF)]
    lands = []
    for _, rows_a, rows_b, _ in SETS:
        lands += [
            pltpu.VMEM((NX, 2, 4, NY, rows_a, LANE), half),
            pltpu.VMEM((NZ, 2, 2, NY, rows_b, LANE), half),
            pltpu.VMEM((1, 2, 2, NY, rows_a, LANE), half),
            pltpu.VMEM((1, 2, 4, NY, rows_b, LANE), half),
            pltpu.VMEM((rows_a + rows_b, LANE), half),
        ]
    weights = [(WIDE, WIDE), (WIDE, LANE), (EF, WIDE, HALF), (EF, WIDE, HALF)]
    dma = pltpu.SemaphoreType.DMA
    four, one = spread_matrix(4, 48), spread_matrix(1, 16)
    return pl.pallas_call(
        mega_kernel,
        out_shape=[
            jax.ShapeDtypeStruct((1, TOKENS, WIDE), single),
            jax.ShapeDtypeStruct((1, TOKENS, WIDE), single),
            jax.ShapeDtypeStruct((PACK, LANE), single),
            jax.ShapeDtypeStruct((BLOCKS, 16, HALF), half),
        ],
        in_specs=[pl.BlockSpec(memory_space=pl.ANY)] * 2 + vmem_specs(14),
        out_specs=vmem_specs(4),
        scratch_shapes=[
            pltpu.VMEM((PACK, LANE), single),
            pltpu.VMEM((NZ, PLANE, PACK, LANE), half),
        ]
        + [pltpu.VMEM(shape, half) for shape in weights]
        + [
            pltpu.VMEM((TOKENS, WIDE), single),
            pltpu.VMEM((TOKENS, WIDE), single),
            pltpu.VMEM((PAD, WIDE), single),
            pltpu.VMEM((PAD, WIDE), single),
            pltpu.VMEM((3, PAD, PAD), single),
            pltpu.VMEM((EF, PAD, HALF), half),
            pltpu.VMEM((EF, PAD, HALF), half),
        ]
        + [pltpu.VMEM(shape, half) for shape in weights]
        + [pltpu.VMEM((PACK, LANE), single)]
        + lands
        + [pltpu.VMEM((2,) + shape, half) for shape in shapes]
        + [pltpu.VMEM(shape, half) for shape in shapes]
        + [pltpu.VMEM(shape, half) for shape in shapes]
        + [pltpu.VMEM((2,) + shape, half) for shape in shapes]
        + [
            pltpu.VMEM((4, 16, LANE), single),
            pltpu.VMEM((BLOCKS, 16, HALF), half),
            pltpu.VMEM((NZ * PLANE, 16, HALF), half),
            pltpu.VMEM((WIDE, HALF), half),
            pltpu.VMEM((NZ * PLANE, 16, HALF), half),
            pltpu.VMEM((HALF, HALF), half),
            dma((RING_SEMS,)), dma((RING_SEMS,)), dma((RING_SEMS,)), dma((RING_SEMS,)),
            dma((12,)), dma((12,)), dma((4,)), dma((4,)),
            dma((4,)), dma((BLOCKS,)), dma, dma, dma((BLOCKS,)),
        ],
        compiler_params=pltpu.CompilerParams(
            collective_id=0, has_side_effects=True, vmem_limit_bytes=64_000_000
        ),
    )(
        inputs, cotangent, routes, gains, router, attn, mats_in, mats_out, *moments,
        four, one, four.T, one.T, half_mask(),
    )


def finish_kernel(
    total, result, rows_out, rows_grad, gains, router, attn, mats_in, mats_out,
    moment_gains, moment_router, moment_attn, moment_in, moment_out,
    output, grad_inputs, sum_gains, sum_attn, sum_router, sum_in, sum_out,
    gains_new, attn_new, router_new, in_new, out_new,
    gains_moved, attn_moved, router_moved, in_moved, out_moved, sems,
):
    copies = [
        pltpu.make_async_copy(source.at[0], landing.at[:, 0, :], sems.at[index])
        for index, (source, landing) in enumerate(((rows_out, output), (rows_grad, grad_inputs)))
    ]
    for copy in copies:
        copy.start()
    small_step = SMALL_RATE / math.sqrt(NZ * PLANE * TOKENS)

    def columns(first_block, block_count):
        return jnp.concatenate(
            [
                total[(first_block + block) * ROW : (first_block + block + 1) * ROW, :]
                for block in range(block_count)
            ],
            axis=1,
        )

    diagonal = lax.broadcasted_iota(jnp.int32, (ROW, ROW), 0) == lax.broadcasted_iota(
        jnp.int32, (ROW, ROW), 1
    )
    small = columns(6, 1)
    small_sets = (
        (0, 2, gains, moment_gains, sum_gains, gains_new, gains_moved),
        (2, EF, router, moment_router, sum_router, router_new, router_moved),
    )
    for first_lane, count, param, moment, gradient, new, moved in small_sets:
        for index in range(count):
            lane = first_lane + index
            row = slice(index, index + 1)
            value = jnp.sum(
                jnp.where(diagonal, small[:, lane : lane + 1], 0.0), axis=0, keepdims=True
            )
            gradient[row, :] = value
            fresh = MOMENTUM * moment[row, :] + value
            moved[row, :] = fresh
            new[row, :] = param[row, :] - small_step * fresh
    flat = columns(0, 6)
    step = jnp.concatenate([result[0, 0:ROW, :], result[1, 0:ROW, :]], axis=1).astype(jnp.float32)
    for which in range(4):
        wide = slice(which * 192, (which + 1) * 192)
        sum_attn[:, which, :] = flat[:, wide]
        attn_moved[:, which, :] = MOMENTUM * moment_attn[:, which, :] + flat[:, wide]
        attn_new[:, which, :] = attn[:, which, :] - MUON_RATE * step[:, wide]
    for first_block, first_slot, param, moment, gradient, new, moved in (
        (7, 2, mats_in, moment_in, sum_in, in_new, in_moved),
        (16, 2 + EF, mats_out, moment_out, sum_out, out_new, out_moved),
    ):
        for expert in range(EF):
            value = columns(first_block + 3 * expert, 3)
            gradient[expert] = value
            moved[expert] = MOMENTUM * moment[expert] + value
            new[expert] = param[expert] - MUON_RATE * result[
                first_slot + expert, 0:ROW, :
            ].astype(jnp.float32)
    for copy in copies:
        copy.wait()


def finish_step(total, result, rows_out, rows_grad, params, moments):
    single = jnp.float32
    rows = jax.ShapeDtypeStruct((TOKENS, 1, WIDE), single)
    group = [
        jax.ShapeDtypeStruct(shape, single)
        for shape in ((2, ROW), (ROW, 4, 192), (EF, ROW), (EF, ROW, HALF), (EF, ROW, HALF))
    ]
    anywhere = pl.BlockSpec(memory_space=pl.ANY)
    return pl.pallas_call(
        finish_kernel,
        out_shape=[rows, rows] + group * 3,
        in_specs=vmem_specs(14),
        out_specs=[anywhere, anywhere] + vmem_specs(15),
        scratch_shapes=[pltpu.SemaphoreType.DMA((2,))],
    )(total, result, rows_out, rows_grad, *params, *moments)


def shards(
    inputs,
    cotangent,
    norm_gains,
    attn_mats,
    router,
    expert_in,
    expert_out,
    moment_gains,
    moment_attn,
    moment_router,
    moment_in,
    moment_out,
    routes,
):
    def by_rows(value):
        return jnp.transpose(value, (1, 0, 2))

    params = (norm_gains, router.T, by_rows(attn_mats), expert_in, expert_out)
    moments = (moment_gains, moment_router.T, by_rows(moment_attn), moment_in, moment_out)
    rows_out, rows_grad, total, finished = whole_step(
        by_rows(inputs), by_rows(cotangent), routes[0].T, *params, moments[2:]
    )
    rows = finish_step(total, finished, rows_out, rows_grad, params, moments)
    output, grad_inputs = (by_rows(value) for value in rows[:2])
    groups = []
    for first in (2, 7, 12):
        gains, attn, router_rows, left, right = rows[first : first + 5]
        groups += [gains, by_rows(attn), router_rows.T, left, right]
    return (output, grad_inputs, *groups)


def solution(mesh):
    return jax.shard_map(
        shards,
        mesh=mesh,
        in_specs=(
            P("dp", None, None),
            P("dp", None, None),
            P(None, "dp"),
            P(None, "dp", "tensor"),
            P("dp", None),
            P(None, "dp", "tensor"),
            P(None, "dp", "tensor"),
            P(None, "dp"),
            P(None, "dp", "tensor"),
            P("dp", None),
            P(None, "dp", "tensor"),
            P(None, "dp", "tensor"),
            P("dp", None, None),
        ),
        out_specs=(
            P("dp", None, None),
            P("dp", None, None),
            P(None, "dp"),
            P(None, "dp", "tensor"),
            P("dp", None),
            P(None, "dp", "tensor"),
            P(None, "dp", "tensor"),
            P(None, "dp"),
            P(None, "dp", "tensor"),
            P("dp", None),
            P(None, "dp", "tensor"),
            P(None, "dp", "tensor"),
            P(None, "dp"),
            P(None, "dp", "tensor"),
            P("dp", None),
            P(None, "dp", "tensor"),
            P(None, "dp", "tensor"),
        ),
        check_vma=False,
    )
```
